32 devices in a mesh: fsdp: 8 (over y, x, core), tp: 4 (over z).
Axes of the slice: x: 2, y: 2, z: 4, core: 2. Of those that a mesh axis runs over, the one named last changes fastest.
Arguments:
- residual: bfloat16 [8192, 2048], P(('fsdp', 'tp')), may hold values from -6 to 6
- query_weight: bfloat16 [2048, 2048], P('fsdp', 'tp'), may hold values from -0.125 to 0.125
- key_weight: bfloat16 [2048, 2048], P('fsdp', 'tp'), may hold values from -0.125 to 0.125
- value_weight: bfloat16 [2048, 2048], P('fsdp', 'tp'), may hold values from -0.125 to 0.125
- out_weight: bfloat16 [2048, 2048], P('tp', 'fsdp'), may hold values from -2 to 2
- query_gain: bfloat16 [16, 128], P('tp', 'fsdp'), may hold values from 0.5 to 1.5
- key_gain: bfloat16 [16, 128], P('tp', 'fsdp'), may hold values from 0.5 to 1.5
- attn_gain: bfloat16 [2048], P('fsdp'), may hold values from 0.5 to 1.5
- mlp_gain: bfloat16 [2048], P('fsdp'), may hold values from 0.5 to 1.5
- router_weight: bfloat16 [2048, 16], P('fsdp'), may hold values from -0.09375 to 0.09375
- gate_weight: bfloat16 [16, 2048, 1024], P(None, 'fsdp', 'tp'), may hold values from -0.125 to 0.125
- up_weight: bfloat16 [16, 2048, 1024], P(None, 'fsdp', 'tp'), may hold values from -0.125 to 0.125
- down_weight: bfloat16 [16, 1024, 2048], P(None, 'tp', 'fsdp'), may hold values from -1.5 to 1.5
- routes: int32 [8192, 8], P('fsdp'), may hold values from 0 to 15, all different within a row
- route_order: int32 [8, 8192], P('fsdp'), may hold values from 0 to 8191, each once within a row
- seg_ids: int32 [8192], P('fsdp'), may hold values from 0 to 8, as said below
- cotangent: bfloat16 [8192, 2048], P(('fsdp', 'tp')), may hold values from -6 to 6
Outputs:
- block_out: float32 [8192, 2048], P(('fsdp', 'tp'))
- grad_input: float32 [8192, 2048], P(('fsdp', 'tp'))
- grad_query: float32 [2048, 2048], P('fsdp', 'tp')
- grad_key: float32 [2048, 2048], P('fsdp', 'tp')
- grad_value: float32 [2048, 2048], P('fsdp', 'tp')
- grad_out_proj: float32 [2048, 2048], P('tp', 'fsdp')
- grad_query_gain: float32 [16, 128], P('tp', 'fsdp')
- grad_key_gain: float32 [16, 128], P('tp', 'fsdp')
- grad_attn_gain: float32 [2048], P('fsdp')
- grad_mlp_gain: float32 [2048], P('fsdp')
- grad_router: float32 [2048, 16], P('fsdp')
- grad_gate: float32 [16, 2048, 1024], P(None, 'fsdp', 'tp')
- grad_up: float32 [16, 2048, 1024], P(None, 'fsdp', 'tp')
- grad_down: float32 [16, 1024, 2048], P(None, 'tp', 'fsdp')
The draws below stay inside these ranges and needn't reach their ends.
Inputs may be any that keep to these rules, and one draw needn't show every extreme that they name: `routes`: each row names 8 different experts. `route_order`: each row is a permutation of the 8192 pairs of one block; pair p is token p // 8 of the block with its route p % 8. `seg_ids`: the first half of the blocks hold prompts (all 0); block g + 4 holds the 8 continuations of prompt g with ids 1 to 8 in order, each of 64 to 192 tokens, one exactly 192.
All inputs are finite; a program needn't handle non-finite values.
Results may differ from the reference program's by a relative error of at most 0.017.
Values may be sent and summed in bfloat16 or wider, within the bound.
No kernel may reach another device: no remote copies, remote signals or barrier semaphores. Data moves between devices by JAX's collectives and lax.ppermute only.
A program may use at most 256 MiB of HBM per device.

```python
import math
import jax
import jax.numpy as jnp
from jax import lax

D = 2048
HEADS = 16
HEAD_DIM = 128
FF = 1024
TOPK = 8
EXPERTS = 16
TOK_DEV = 1024
CLEN = 128
CONTS = 8
CAP = 512
GROUPS = 4
PIECES = 8
TOKENS = 8192


def draw_seg_ids(key, part):
    half_len = CLEN // 2
    spread = jax.random.randint(key, (GROUPS, CONTS // 2), 0, half_len + 1)
    spread = spread.at[:, 0].set(half_len)
    lengths = jnp.concatenate([CLEN + spread, CLEN - spread], axis=1)
    scores = jax.random.randint(jax.random.fold_in(key, 7), (GROUPS, CONTS), 0, 1 << 20) * CONTS + jnp.arange(CONTS)[None, :]
    ranking = jnp.argsort(scores, axis=1, stable=True)
    lengths = jnp.take_along_axis(lengths, ranking, axis=1)
    bounds = jnp.cumsum(lengths, axis=1)
    positions = jnp.arange(TOK_DEV)
    labels = jnp.sum((positions[None, :, None] >= bounds[:, None, :]).astype(jnp.int32), axis=2) + 1
    prompt = jnp.zeros((GROUPS, TOK_DEV), jnp.int32)
    return jnp.concatenate([prompt, labels.astype(jnp.int32)], axis=0).reshape(-1)


def block_scale(own_key, dims, pieces, smallest, largest):
    factor_of, own = 1.0, jax.random.fold_in(own_key, 6)
    for dim, shards_of in pieces:
        heights = jnp.exp(jax.random.uniform(jax.random.fold_in(own, dim), (shards_of,), jnp.float32, smallest / len(pieces), largest / len(pieces)))
        factor_of = factor_of * jnp.repeat(heights, dims[dim] // shards_of).reshape([-1 if axis == dim else 1 for axis in range(len(dims))])
    return factor_of


def picks_of(key, rows, amount, top, lift):
    order = jax.random.permutation(jax.random.fold_in(key, 1), amount)
    pull = order
    for power in range(3):
        pull = pull * pull // amount
    pull = pull * lift // amount
    chance = jax.random.randint(jax.random.fold_in(key, 2), (rows, amount), 0, 4096) + pull
    holders = jax.random.permutation(jax.random.fold_in(key, 3), rows)[jnp.arange(amount) % rows]
    chance = jnp.where(jnp.arange(rows)[:, None] == holders[None, :], 1 << 14, chance)
    score = chance * amount + jnp.arange(amount)
    return lax.top_k(score.astype(jnp.int32), top)[1].astype(jnp.int32)


def gaussian(rng, shape, deviation, reach, split=(), kind=jnp.bfloat16):
    entries = deviation * jax.random.normal(rng, shape, jnp.float32)
    if split:
        entries = entries * block_scale(rng, shape, split, -0.22, 0.18)
    return jnp.clip(entries, -reach, reach).astype(kind)


def setup_inputs(seed: int = 0) -> dict:
    key_of = jax.random.split(jax.random.key(seed), 18)
    residual = gaussian(key_of[0], (TOKENS, D), 1.0, 6.0, ((0, 32),))
    query_weight = gaussian(key_of[1], (D, D), D ** -0.5, 0.125, ((0, 8), (1, 4)))
    key_weight = gaussian(key_of[2], (D, D), D ** -0.5, 0.125, ((0, 8), (1, 4)))
    value_weight = gaussian(key_of[3], (D, D), D ** -0.5, 0.125, ((0, 8), (1, 4)))
    out_weight = gaussian(key_of[4], (D, D), (max(D // 256, 1)) ** -0.5, 2.0, ((0, 4), (1, 8)))
    query_gain = jnp.clip(1.0 + 0.1 * jax.random.normal(key_of[5], (HEADS, HEAD_DIM), jnp.float32), 0.5, 1.5).astype(jnp.bfloat16)
    key_gain = jnp.clip(1.0 + 0.1 * jax.random.normal(key_of[6], (HEADS, HEAD_DIM), jnp.float32), 0.5, 1.5).astype(jnp.bfloat16)
    attn_gain = jnp.clip(1.0 + 0.1 * jax.random.normal(key_of[7], (D,), jnp.float32), 0.5, 1.5).astype(jnp.bfloat16)
    mlp_gain = jnp.clip(1.0 + 0.1 * jax.random.normal(key_of[8], (D,), jnp.float32), 0.5, 1.5).astype(jnp.bfloat16)
    router_weight = gaussian(key_of[9], (D, EXPERTS), (2 * D) ** -0.5, 0.09375, ((0, 8),))
    gate_weight = gaussian(key_of[10], (EXPERTS, D, FF), D ** -0.5, 0.125, ((1, 8), (2, 4)))
    up_weight = gaussian(key_of[11], (EXPERTS, D, FF), D ** -0.5, 0.125, ((1, 8), (2, 4)))
    down_weight = gaussian(key_of[12], (EXPERTS, FF, D), (max(FF // 64, 1)) ** -0.5, 1.5, ((1, 4), (2, 8)))
    routes = picks_of(key_of[13], TOKENS, EXPERTS, TOPK, 0)
    route_order = jax.vmap(lambda own: jax.random.permutation(own, TOK_DEV * TOPK))(jax.random.split(key_of[14], PIECES)).reshape((PIECES, TOK_DEV * TOPK)).astype(jnp.int32)
    seg_ids = draw_seg_ids(jax.random.fold_in(key_of[17], 71), 0)
    cotangent = gaussian(key_of[16], (TOKENS, D), 1.0, 6.0, ((0, 32),))
    return dict(residual=residual, query_weight=query_weight, key_weight=key_weight, value_weight=value_weight, out_weight=out_weight, query_gain=query_gain, key_gain=key_gain, attn_gain=attn_gain, mlp_gain=mlp_gain, router_weight=router_weight, gate_weight=gate_weight, up_weight=up_weight, down_weight=down_weight, routes=routes, route_order=route_order, seg_ids=seg_ids, cotangent=cotangent)


EPS = 1e-05
NEG = -1e+30
HIGH = lax.Precision.HIGHEST

@jax.custom_vjp
def low(v):
    return lax.optimization_barrier(v.astype(jnp.bfloat16)).astype(jnp.float32)

@jax.custom_vjp
def low_back(v):
    return v

def low_keep(v):
    return (low(v), None)

def low_pass(kept, grad):
    return (grad,)

def back_keep(v):
    return (v, None)

def back_low(kept, grad):
    return (low(grad),)
low.defvjp(low_keep, low_pass)
low_back.defvjp(back_keep, back_low)

def norm_scale(values):
    return lax.rsqrt(lax.optimization_barrier(jnp.mean(values * values, axis=-1, keepdims=True)) + EPS)

def rope_angles(seg_block):
    row_count = seg_block.shape[0]
    labels = jnp.arange(CONTS + 1, dtype=jnp.int32)
    member = (seg_block[:, None] == labels[None, :]).astype(jnp.int32)
    counts = lax.optimization_barrier(jnp.sum(member, axis=0))
    starts = jnp.cumsum(counts) - counts
    seg_start = lax.optimization_barrier(jnp.sum(member * starts[None, :], axis=1))
    offset = TOK_DEV * (seg_block != 0).astype(jnp.int32)
    places = jnp.arange(row_count, dtype=jnp.int32) - seg_start + offset
    half_dim = HEAD_DIM // 2
    frequency = jnp.exp(jnp.arange(half_dim, dtype=jnp.float32) * (-2.0 * math.log(10000.0) / HEAD_DIM))
    angles = places.astype(jnp.float32)[:, None] * frequency[None, :]
    return (jnp.cos(angles), jnp.sin(angles))

def rotate(values, cosines, sines):
    row_count = values.shape[0]
    by_head = values.reshape(row_count, -1, HEAD_DIM)
    half_dim = HEAD_DIM // 2
    first_half = by_head[..., :half_dim]
    second_half = by_head[..., half_dim:]
    cos_wide = cosines[:, None, :]
    sin_wide = sines[:, None, :]
    turned = jnp.concatenate([first_half * cos_wide - second_half * sin_wide, second_half * cos_wide + first_half * sin_wide], axis=-1)
    return turned.reshape(row_count, -1)

def route_tables(block_routes, block_order):
    pair_expert = block_routes.reshape(-1)
    placed = pair_expert[block_order]
    member = (placed[:, None] == jnp.arange(EXPERTS, dtype=jnp.int32)[None, :]).astype(jnp.int32)
    pair_rank = lax.optimization_barrier(jnp.sum(member * jnp.cumsum(member, axis=0), axis=1)) - 1
    target = jnp.where(pair_rank < CAP, placed * CAP + pair_rank, EXPERTS * CAP).astype(jnp.int32)
    slot_of_pair = jnp.zeros_like(pair_expert).at[block_order].set(target)
    token_of_slot = jnp.full((EXPERTS * CAP + 1,), TOK_DEV, jnp.int32).at[target].set((block_order // TOPK).astype(jnp.int32))
    return (slot_of_pair, token_of_slot[:EXPERTS * CAP])

def to_groups(values):
    shaped = values.reshape((2, GROUPS) + values.shape[1:])
    return jnp.swapaxes(shaped, 0, 1)

def group_forward(weights, group_items):
    query_weight, key_weight, value_weight, out_weight, query_gain, key_gain, attn_gain, mlp_gain, router_weight, gate_weight, up_weight, down_weight = weights
    group_in, group_seg, cosines, sines, group_routes, slot_of_pair, token_of_slot = group_items
    length = group_in.shape[0]
    normed = low(group_in * norm_scale(group_in) * attn_gain)
    query_raw = low_back(jnp.dot(normed, query_weight, precision=HIGH))
    key_raw = low_back(jnp.dot(normed, key_weight, precision=HIGH))
    value_raw = low_back(jnp.dot(normed, value_weight, precision=HIGH))
    query_rot = low(rotate(query_raw * norm_scale(query_raw) * query_gain.reshape(-1), cosines, sines))
    key_rot = low(rotate(key_raw * norm_scale(key_raw) * key_gain.reshape(-1), cosines, sines))
    value_low = low(value_raw)
    places = jnp.arange(length, dtype=jnp.int32)
    visible = (group_seg[None, :] == 0) & (group_seg[:, None] != 0) | (group_seg[None, :] == group_seg[:, None]) & (places[None, :] <= places[:, None])

    def heads_first(values):
        return values.reshape(length, HEADS, HEAD_DIM).transpose(1, 0, 2)

    def attend(head_items):
        query_head, key_head, value_head = head_items
        scores = low_back(jnp.dot(query_head, key_head.T, precision=HIGH) * HEAD_DIM ** (-0.5))
        masked = jnp.where(visible, scores, NEG)
        row_peak = lax.optimization_barrier(jnp.max(masked, axis=-1, keepdims=True))
        exp_scores = jnp.exp(masked - row_peak)
        attn_probs = exp_scores / lax.optimization_barrier(jnp.sum(exp_scores, axis=-1, keepdims=True))
        return low_back(jnp.dot(low(attn_probs), value_head, precision=HIGH))
    attended = lax.map(jax.checkpoint(attend), (heads_first(query_rot), heads_first(key_rot), heads_first(value_low)))
    attended = low(attended.transpose(1, 0, 2).reshape(length, D))
    attn_out = low_back(jnp.dot(attended, out_weight, precision=HIGH))
    after_attn = group_in + attn_out
    normed_mlp = low(after_attn * norm_scale(after_attn) * mlp_gain)

    def experts_block(block_items):
        block_norm, block_routes, block_slots, block_tokens = block_items
        logits = jnp.dot(block_norm, router_weight, precision=HIGH)
        row_peak = lax.optimization_barrier(jnp.max(logits, axis=-1, keepdims=True))
        exp_logits = jnp.exp(logits - row_peak)
        router_probs = exp_logits / lax.optimization_barrier(jnp.sum(exp_logits, axis=-1, keepdims=True))
        gate_vals = jnp.take_along_axis(router_probs, block_routes, axis=1)
        padded = jnp.concatenate([block_norm, jnp.zeros((1, D), jnp.float32)], axis=0)
        dispatched = padded[block_tokens].reshape(EXPERTS, CAP, D)
        gate_hidden = low_back(jnp.einsum('ecd,edf->ecf', dispatched, gate_weight, precision=HIGH))
        up_hidden = low_back(jnp.einsum('ecd,edf->ecf', dispatched, up_weight, precision=HIGH))
        sigmoid_g = 1.0 / (1.0 + jnp.exp(-gate_hidden))
        activation = low(gate_hidden * sigmoid_g * up_hidden)
        expert_out = low_back(jnp.einsum('ecf,efd->ecd', activation, down_weight, precision=HIGH)).reshape(EXPERTS * CAP, D)
        padded_out = jnp.concatenate([expert_out, jnp.zeros((1, D), jnp.float32)], axis=0)
        picked = padded_out[block_slots].reshape(TOK_DEV, TOPK, D)
        return lax.optimization_barrier(jnp.sum(picked * gate_vals[:, :, None], axis=1))
    expert_sum = lax.map(jax.checkpoint(experts_block), (normed_mlp.reshape(2, TOK_DEV, D), group_routes, slot_of_pair, token_of_slot))
    return after_attn + expert_sum.reshape(length, D)

def reference(residual, query_weight, key_weight, value_weight, out_weight, query_gain, key_gain, attn_gain, mlp_gain, router_weight, gate_weight, up_weight, down_weight, routes, route_order, seg_ids, cotangent):
    floats = (query_weight.astype(jnp.float32), key_weight.astype(jnp.float32), value_weight.astype(jnp.float32), out_weight.astype(jnp.float32), query_gain.astype(jnp.float32), key_gain.astype(jnp.float32), attn_gain.astype(jnp.float32), mlp_gain.astype(jnp.float32), router_weight.astype(jnp.float32), gate_weight.astype(jnp.float32), up_weight.astype(jnp.float32), down_weight.astype(jnp.float32))
    inputs = residual.astype(jnp.float32)
    seg_blocks = seg_ids.reshape(PIECES, TOK_DEV)
    cosines, sines = jax.vmap(rope_angles)(seg_blocks)
    slot_tables, token_tables = jax.vmap(route_tables)(routes.reshape(PIECES, TOK_DEV, TOPK), route_order)
    group_items = (to_groups(seg_blocks).reshape(GROUPS, 2 * TOK_DEV), to_groups(cosines).reshape(GROUPS, 2 * TOK_DEV, HEAD_DIM // 2), to_groups(sines).reshape(GROUPS, 2 * TOK_DEV, HEAD_DIM // 2), to_groups(routes.reshape(PIECES, TOK_DEV, TOPK)), to_groups(slot_tables), to_groups(token_tables))

    def forward(inputs_f, weights):

        def group_step(step_items):
            return group_forward(weights, step_items)
        grouped = to_groups(inputs_f.reshape(PIECES, TOK_DEV, D)).reshape(GROUPS, 2 * TOK_DEV, D)
        outputs = lax.map(jax.checkpoint(group_step), (grouped,) + group_items)
        outputs = jnp.swapaxes(outputs.reshape(GROUPS, 2, TOK_DEV, D), 0, 1)
        return outputs.reshape(TOKENS, D)
    block_out, pullback = jax.vjp(forward, inputs, floats)
    grad_input, grads = pullback(cotangent.astype(jnp.float32))
    return (block_out, grad_input, grads[0], grads[1], grads[2], grads[3], grads[4], grads[5], grads[6], grads[7], grads[8], grads[9], grads[10], grads[11])
```

```python
import functools
import math

import jax
import jax.numpy as jnp
from jax import lax
from jax.experimental import pallas as pl
from jax.experimental.pallas import tpu as pltpu
from jax.sharding import PartitionSpec as P

HEAD_DIM = 128
CONTS = 8
CAP = 512
EPS = 1e-05
NEG = -1e30
QT = 256
BF = jnp.bfloat16
F32 = jnp.float32
NT = (((1,), (1,)), ((), ()))
TN = (((0,), (0,)), ((), ()))


def dot(a, b, dims=(((1,), (0,)), ((), ()))):
    return lax.dot_general(a, b, dims, preferred_element_type=F32)


def params(count=1):
    return pltpu.CompilerParams(
        dimension_semantics=("arbitrary",) * count, vmem_limit_bytes=56 << 20
    )


def cost(flops, nbytes, trans=0):
    return pl.CostEstimate(flops=int(flops), bytes_accessed=int(nbytes), transcendentals=int(trans))


def across(value, axis, pairs):
    return lax.ppermute(value, axis, pairs)


def swap_core(value):
    count = lax.axis_size("fsdp")
    return lax.ppermute(value, "fsdp", [(i, i ^ 1) for i in range(count)])


def swap_chip(value, bit):
    count = lax.axis_size("fsdp")
    return lax.ppermute(value, "fsdp", [(i, i ^ (2 * bit)) for i in range(count)])


def chip_bits():
    chips = lax.axis_size("fsdp") // 2
    return [1 << b for b in range(chips.bit_length() - 1)]


def spread(piece, bits):
    held = {0: piece}
    for bit in bits:
        held.update({r ^ bit: swap_chip(v, bit) for r, v in list(held.items())})
    return [held[r] for r in range(len(held))]


def collect(parts, bits):
    held = dict(enumerate(parts))
    for bit in bits:
        for r in [r for r in held if r & bit]:
            got = swap_chip(held.pop(r).astype(BF), bit)
            held[r ^ bit] = held[r ^ bit].astype(F32) + got.astype(F32)
    return held[0]


def line_gather(value):
    count = lax.axis_size("tp")
    place = lax.axis_index("tp")
    up, down = [value], [value]
    for s in range(1, count):
        up.append(lax.ppermute(up[-1], "tp", [(i, i + 1) for i in range(s - 1, count - 1)]))
        down.append(lax.ppermute(down[-1], "tp", [(i + 1, i) for i in range(count - s)]))
    return [value] + [jnp.where(place + d < count, down[d], up[count - d]) for d in range(1, count)]


def line_scatter(parts):
    count = lax.axis_size("tp")
    up = down = None
    for s in range(count - 1, 0, -1):
        send_up, send_down = parts[s].astype(F32), parts[count - s].astype(F32)
        if up is not None:
            send_up, send_down = send_up + up.astype(F32), send_down + down.astype(F32)
        up = lax.ppermute(send_up.astype(BF), "tp", [(i, i + 1) for i in range(count - s)])
        down = lax.ppermute(send_down.astype(BF), "tp", [(i + 1, i) for i in range(s - 1, count - 1)])
    return parts[0].astype(F32) + up.astype(F32) + down.astype(F32)


def total_tp(value):
    count = lax.axis_size("tp")
    out = value
    for s in range(1, count):
        out = out + lax.ppermute(value, "tp", [(i, (i + s) % count) for i in range(count)])
    return out


def to_rel(value, axis):
    chips = lax.axis_size("fsdp") // 2
    own = lax.axis_index("fsdp") // 2
    width = value.shape[axis] // chips
    return jnp.concatenate(
        [lax.dynamic_slice_in_dim(value, (own ^ r) * width, width, axis) for r in range(chips)], axis
    )


def rows_abs(pieces):
    count = len(pieces)
    place = lax.axis_index("tp")
    rows = pieces[0].shape[0]
    out = jnp.zeros((count * rows,) + pieces[0].shape[1:], pieces[0].dtype)
    for d, piece in enumerate(pieces):
        out = lax.dynamic_update_slice_in_dim(out, piece, ((place + d) % count) * rows, 0)
    return out


def rows_rel(value):
    count = lax.axis_size("tp")
    place = lax.axis_index("tp")
    rows = value.shape[0] // count
    return jnp.concatenate(
        [lax.dynamic_slice_in_dim(value, ((place + d) % count) * rows, rows, 0) for d in range(count)], 0
    )


def keep_kernel(pos_ref, keep_ref):
    pos = pos_ref[...]
    bound = jnp.zeros((1, pos.shape[1]), jnp.int32)
    for b in range(13, -1, -1):
        trial = bound + (1 << b)
        count = jnp.sum((pos <= trial).astype(F32), axis=0, keepdims=True)
        bound = jnp.where(count <= CAP, trial, bound)
    keep_ref[...] = (pos <= bound).astype(F32)


def kept_pairs(routes, order_row, experts):
    pairs = order_row.shape[0]
    tokens = routes.shape[0]
    step = jnp.arange(pairs, dtype=jnp.int32)
    high = (order_row[:, None] // 128 == jnp.arange(pairs // 128, dtype=jnp.int32)[None, :]).astype(BF)
    low = (order_row[:, None] % 128 == jnp.arange(128, dtype=jnp.int32)[None, :]).astype(BF)
    step_high = (step // 64).astype(BF)[:, None]
    step_low = (step % 64).astype(BF)[:, None]
    table = 64.0 * dot(high * step_high, low, TN) + dot(high * step_low, low, TN)
    place = table.astype(jnp.int32).reshape(tokens, -1) + 1
    hot = routes[:, :, None] == jnp.arange(experts, dtype=jnp.int32)[None, None, :]
    pos = jnp.sum(jnp.where(hot, place[:, :, None], 0), axis=1)
    pos = jnp.where(pos == 0, 1 << 20, pos)
    return pl.pallas_call(
        keep_kernel, out_shape=jax.ShapeDtypeStruct((tokens, experts), F32), name="keep"
    )(pos)


def turn_kernel(q_ref, k_ref, v_ref, norm_ref, cos_ref, sin_ref, gain_ref, q_out, k_out, v_out):
    cos, sin = cos_ref[...], sin_ref[...]
    for slot, (raw, out) in enumerate(((q_ref, q_out), (k_ref, k_out))):
        x = raw[...] * norm_ref[:, slot : slot + 1] * gain_ref[slot]
        out[...] = (x * cos + pltpu.roll(x, HEAD_DIM // 2, 1) * sin).astype(BF)
    v_out[...] = v_ref[...].astype(BF)


def turn(raw, norms, cos, sin, gains):
    rows = raw.shape[0]
    heads = raw.shape[1] // (3 * HEAD_DIM)
    part = lambda j: pl.BlockSpec((rows, HEAD_DIM), lambda h: (0, j * heads + h))
    whole = lambda shape: pl.BlockSpec(shape, lambda h: (0,) * len(shape))
    return pl.pallas_call(
        turn_kernel,
        grid=(heads,),
        in_specs=[
            part(0),
            part(1),
            part(2),
            whole(norms.shape),
            whole(cos.shape),
            whole(sin.shape),
            pl.BlockSpec((2, 1, HEAD_DIM), lambda h: (0, 0, h)),
        ],
        out_specs=[part(0)] * 3,
        out_shape=[jax.ShapeDtypeStruct((rows, heads * HEAD_DIM), BF)] * 3,
        compiler_params=params(),
        cost_estimate=cost(10 * raw.size, 6 * raw.size),
        name="turn",
    )(raw, raw, raw, norms, cos, sin, gains)


def turn_back_kernel(
    dq_ref, dk_ref, dkr_ref, q_ref, k_ref, norm_ref, cos_ref, sin_ref, gain_ref, uq_out, uk_out, dots_out, part_out
):
    cos, sin = cos_ref[...], sin_ref[...]
    grads = (dq_ref[...], dk_ref[...] + dkr_ref[...].astype(F32))
    lane = lax.broadcasted_iota(jnp.int32, dots_out.shape, 1)

    @pl.when(pl.program_id(0) == 0)
    def _():
        dots_out[...] = jnp.zeros_like(dots_out)

    for slot, (grad, raw, out) in enumerate(zip(grads, (q_ref, k_ref), (uq_out, uk_out))):
        back = grad * cos - pltpu.roll(grad, HEAD_DIM // 2, 1) * sin
        x = raw[...]
        part_out[slot] = jnp.sum(back * x * norm_ref[:, slot : slot + 1], axis=0, keepdims=True)
        u = back * gain_ref[slot]
        out[...] = u
        dots_out[...] += jnp.where(lane == slot, jnp.sum(u * x, axis=1, keepdims=True), 0.0)


def turn_back(dq, dk, dk_more, raw, norms, cos, sin, gains):
    rows = raw.shape[0]
    heads = raw.shape[1] // (3 * HEAD_DIM)
    part = lambda j: pl.BlockSpec((rows, HEAD_DIM), lambda h: (0, j * heads + h))
    whole = lambda shape: pl.BlockSpec(shape, lambda h: (0,) * len(shape))
    gain_spec = pl.BlockSpec((2, 1, HEAD_DIM), lambda h: (0, 0, h))
    wide = jax.ShapeDtypeStruct((rows, heads * HEAD_DIM), F32)
    return pl.pallas_call(
        turn_back_kernel,
        grid=(heads,),
        in_specs=[
            part(0),
            part(0),
            part(0),
            part(0),
            part(1),
            whole(norms.shape),
            whole(cos.shape),
            whole(sin.shape),
            gain_spec,
        ],
        out_specs=[part(0), part(0), whole((rows, 2)), gain_spec],
        out_shape=[
            wide,
            wide,
            jax.ShapeDtypeStruct((rows, 2), F32),
            jax.ShapeDtypeStruct((2, 1, heads * HEAD_DIM), F32),
        ],
        compiler_params=params(),
        cost_estimate=cost(10 * raw.size, 8 * raw.size),
        name="turn_back",
    )(dq, dk, dk_more, raw, raw, norms, cos, sin, gains)


def own_mask(seg_col, seg_row, first_row, row_count, first_key, key_count):
    rows = lax.broadcasted_iota(jnp.int32, (row_count, key_count), 0) + first_row
    keys = lax.broadcasted_iota(jnp.int32, (row_count, key_count), 1) + first_key
    same = seg_col[first_row : first_row + row_count, :] == seg_row[:, first_key : first_key + key_count]
    return same & (keys <= rows)


SCALE = HEAD_DIM ** (-0.5)


def tile_probs(q_tile, k_ref, seg_col, seg_row, first_row, first_key, keys, kr):
    own = dot(q_tile, k_ref[first_key : first_key + keys, :], NT)
    own = jnp.where(own_mask(seg_col, seg_row, first_row, QT, first_key, keys), own, NEG)
    peak = jnp.max(own, axis=1, keepdims=True)
    far = None
    if kr is not None:
        far = dot(q_tile, kr[...], NT)
        peak = jnp.maximum(peak, jnp.max(far, axis=1, keepdims=True))
        far = jnp.exp((far - peak) * SCALE)
    own = jnp.exp((own - peak) * SCALE)
    total = jnp.sum(own, axis=1, keepdims=True)
    if far is not None:
        total = total + jnp.sum(far, axis=1, keepdims=True)
    inverse = 1.0 / total
    return own * inverse, (None if far is None else far * inverse)


def attend_kernel(cont_ref, q_ref, k_ref, v_ref, kr_ref, vr_ref, col_ref, row_ref, out_ref):
    rows = q_ref.shape[0]

    def run(far):
        for first in range(0, rows, QT):
            start = max(0, first - QT) if far else 0
            keys = first + QT - start
            own, other = tile_probs(
                q_ref[first : first + QT, :], k_ref, col_ref, row_ref, first, start, keys, kr_ref if far else None
            )
            out = dot(own.astype(BF), v_ref[start : start + keys, :])
            if far:
                out = out + dot(other.astype(BF), vr_ref[...])
            out_ref[first : first + QT, :] = out.astype(BF)

    pl.when(cont_ref[0] == 0)(lambda: run(False))
    pl.when(cont_ref[0] != 0)(lambda: run(True))


def attend_specs(rows, count):
    head = pl.BlockSpec((rows, HEAD_DIM), lambda h, c: (0, h))
    return [head] * count + [
        pl.BlockSpec((rows, 1), lambda h, c: (0, 0)),
        pl.BlockSpec((1, rows), lambda h, c: (0, 0)),
    ], head


def attend(cont, q, k, v, kr, vr, seg_col, seg_row):
    rows, width = q.shape
    specs, head = attend_specs(rows, 5)
    return pl.pallas_call(
        attend_kernel,
        grid_spec=pltpu.PrefetchScalarGridSpec(
            num_scalar_prefetch=1, grid=(width // HEAD_DIM,), in_specs=specs, out_specs=head
        ),
        out_shape=jax.ShapeDtypeStruct((rows, width), BF),
        compiler_params=params(),
        cost_estimate=cost(6 * rows * rows * width, 12 * rows * width, rows * rows * 6),
        name="attend",
    )(cont, q, k, v, kr, vr, seg_col, seg_row)


def attend_back_kernel(
    cont_ref, q_ref, k_ref, v_ref, kr_ref, vr_ref, do_ref, col_ref, row_ref, dq_ref, dk_ref, dv_ref, dkr_ref, dvr_ref, far_dk, far_dv
):
    rows = q_ref.shape[0]
    dk_ref[...] = jnp.zeros_like(dk_ref)
    dv_ref[...] = jnp.zeros_like(dv_ref)

    def run(far):
        if far:
            far_dk[...] = jnp.zeros_like(far_dk)
            far_dv[...] = jnp.zeros_like(far_dv)
        for first in range(0, rows, QT):
            start = max(0, first - QT) if far else 0
            keys = first + QT - start
            here = slice(start, start + keys)
            q_tile = q_ref[first : first + QT, :]
            do_tile = do_ref[first : first + QT, :]
            own, other = tile_probs(q_tile, k_ref, col_ref, row_ref, first, start, keys, kr_ref if far else None)
            grad = dot(do_tile, v_ref[here, :], NT)
            mean = jnp.sum(own * grad, axis=1, keepdims=True)
            if far:
                grad_far = dot(do_tile, vr_ref[...], NT)
                mean = mean + jnp.sum(other * grad_far, axis=1, keepdims=True)
            slope = (own * (grad - mean)).astype(BF)
            dq = dot(slope, k_ref[here, :])
            dk_ref[here, :] += dot(slope, q_tile, TN) * SCALE
            dv_ref[here, :] += dot(own.astype(BF), do_tile, TN)
            if far:
                slope = (other * (grad_far - mean)).astype(BF)
                dq = dq + dot(slope, kr_ref[...])
                far_dk[...] += dot(slope, q_tile, TN) * SCALE
                far_dv[...] += dot(other.astype(BF), do_tile, TN)
            dq_ref[first : first + QT, :] = dq * SCALE
        if far:
            dkr_ref[...] = far_dk[...].astype(BF)
            dvr_ref[...] = far_dv[...].astype(BF)
        else:
            dkr_ref[...] = jnp.zeros_like(dkr_ref)
            dvr_ref[...] = jnp.zeros_like(dvr_ref)

    pl.when(cont_ref[0] == 0)(lambda: run(False))
    pl.when(cont_ref[0] != 0)(lambda: run(True))


def attend_back(cont, q, k, v, kr, vr, do, seg_col, seg_row):
    rows, width = q.shape
    specs, head = attend_specs(rows, 6)
    wide = jax.ShapeDtypeStruct((rows, width), F32)
    low = jax.ShapeDtypeStruct((rows, width), BF)
    return pl.pallas_call(
        attend_back_kernel,
        grid_spec=pltpu.PrefetchScalarGridSpec(
            num_scalar_prefetch=1,
            grid=(width // HEAD_DIM,),
            in_specs=specs,
            out_specs=[head] * 5,
            scratch_shapes=[pltpu.VMEM((rows, HEAD_DIM), F32)] * 2,
        ),
        out_shape=[wide, wide, wide, low, low],
        compiler_params=params(),
        cost_estimate=cost(15 * rows * rows * width, 30 * rows * width, rows * rows * 6),
        name="attend_back",
    )(cont, q, k, v, kr, vr, do, seg_col, seg_row)


def hidden_kernel(x_ref, c_ref, g_ref, u_ref, d_ref, w_ref, act_out, dg_out, du_out, s_out):
    expert = pl.program_id(0)
    gate = dot(x_ref[...], g_ref[...])
    up = dot(x_ref[...], u_ref[...])
    back = dot(c_ref[...], d_ref[...])
    lane = lax.broadcasted_iota(jnp.int32, s_out.shape, 1)
    weight = jnp.sum(jnp.where(lane == expert, w_ref[...], 0.0), axis=1, keepdims=True)
    sig = 1.0 / (1.0 + jnp.exp(-gate))
    swish = gate * sig
    act = swish * up
    act_out[...] = (act * weight).astype(BF)
    s = jnp.sum(act * back, axis=1, keepdims=True)
    back = back * weight
    dg_out[...] = (back * up * (sig + swish * (1.0 - sig))).astype(BF)
    du_out[...] = (back * swish).astype(BF)

    @pl.when(expert == 0)
    def _():
        s_out[...] = jnp.zeros_like(s_out)

    s_out[...] = jnp.where(lane == expert, s, s_out[...])


def hidden(x, c, wg, wu, wd, weight):
    rows, dim = x.shape
    experts = weight.shape[1]
    span = wg.shape[1] // experts
    full = pl.BlockSpec((rows, dim), lambda e: (0, 0))
    mat = pl.BlockSpec((dim, span), lambda e: (0, e))
    out = pl.BlockSpec((rows, span), lambda e: (0, e))
    small = pl.BlockSpec((rows, experts), lambda e: (0, 0))
    wide = jax.ShapeDtypeStruct((rows, experts * span), BF)
    return pl.pallas_call(
        hidden_kernel,
        grid=(experts,),
        in_specs=[full, full, mat, mat, mat, small],
        out_specs=[out, out, out, small],
        out_shape=[wide, wide, wide, jax.ShapeDtypeStruct((rows, experts), F32)],
        compiler_params=params(),
        cost_estimate=cost(6 * rows * dim * experts * span, 2 * (2 * rows * dim + 6 * dim * experts * span)),
        name="hidden",
    )(x, c, wg, wu, wd, weight)


def mix_kernel(*refs):
    count = (len(refs) - 1) // 2
    total = None
    for j in range(count):
        term = dot(refs[2 * j][...], refs[2 * j + 1][...], NT)
        total = term if total is None else total + term
    refs[-1][...] = total.astype(refs[-1].dtype)


def mix(pairs, dtype, tile=512):
    rows, cols = pairs[0][0].shape[0], pairs[0][1].shape[0]
    specs, flat, flops, nbytes = [], [], 0, 0
    for a, b in pairs:
        specs += [pl.BlockSpec(a.shape, lambda j: (0, 0)), pl.BlockSpec((tile, b.shape[1]), lambda j: (j, 0))]
        flat += [a, b]
        flops += 2 * rows * cols * a.shape[1]
        nbytes += 2 * (a.size + b.size)
    return pl.pallas_call(
        mix_kernel,
        grid=(cols // tile,),
        in_specs=specs,
        out_specs=pl.BlockSpec((rows, tile), lambda j: (0, j)),
        out_shape=jax.ShapeDtypeStruct((rows, cols), dtype),
        compiler_params=params(),
        cost_estimate=cost(flops, nbytes + 4 * rows * cols),
        name="mix",
    )(*flat)


def angles(seg_block):
    row_count = seg_block.shape[0]
    labels = jnp.arange(CONTS + 1, dtype=jnp.int32)
    member = (seg_block[:, None] == labels[None, :]).astype(jnp.int32)
    counts = jnp.sum(member, axis=0)
    starts = jnp.sum(jnp.where(labels[:, None] > labels[None, :], counts[None, :], 0), axis=1)
    seg_start = jnp.sum(member * starts[None, :], axis=1)
    offset = row_count * (seg_block != 0).astype(jnp.int32)
    places = jnp.arange(row_count, dtype=jnp.int32) - seg_start + offset
    half = HEAD_DIM // 2
    column = jnp.arange(HEAD_DIM, dtype=jnp.int32)
    frequency = jnp.exp((column % half).astype(F32) * (-2.0 * math.log(10000.0) / HEAD_DIM))
    angle = places.astype(F32)[:, None] * frequency[None, :]
    sign = jnp.where(column < half, -1.0, 1.0).astype(F32)
    return jnp.cos(angle), jnp.sin(angle) * sign[None, :]


def inverse_norm(values):
    return lax.rsqrt(jnp.mean(values * values, axis=-1, keepdims=True) + EPS)


def on_device(
    residual,
    query_weight,
    key_weight,
    value_weight,
    out_weight,
    query_gain,
    key_gain,
    attn_gain,
    mlp_gain,
    router_weight,
    gate_weight,
    up_weight,
    down_weight,
    routes,
    route_order,
    seg_ids,
    cotangent,
):
    fsdp, tp = lax.axis_size("fsdp"), lax.axis_size("tp")
    place = lax.axis_index("fsdp")
    core = place % 2
    dim = residual.shape[1]
    piece = dim // fsdp
    tokens = seg_ids.shape[0]
    experts, _, span = gate_weight.shape
    local = experts // 2
    cols = query_weight.shape[1]
    bits = chip_bits()
    back_bits = bits[::-1]
    cut = piece // 2

    a_gain = attn_gain.astype(F32)[:, None]
    m_gain = mlp_gain.astype(F32)[:, None]

    stream = to_rel(residual, 1).astype(F32)
    norm_first = inverse_norm(stream)
    hat_one = stream * norm_first
    normed = rows_abs(line_gather(hat_one.astype(BF)))

    attn_pack = jnp.concatenate(
        [
            (query_weight.astype(F32) * a_gain).astype(BF),
            (key_weight.astype(F32) * a_gain).astype(BF),
            (value_weight.astype(F32) * a_gain).astype(BF),
            out_weight.T,
            jnp.pad((router_weight.astype(F32) * m_gain).astype(BF), ((0, 0), (0, 128 - experts))),
        ],
        axis=1,
    )
    first_half = spread(attn_pack[:cut], bits)
    second_half = spread(attn_pack[cut:], back_bits)
    mine = jnp.stack([jnp.stack([a, b]) for a, b in zip(first_half, second_half)])
    theirs = swap_core(mine)
    pair = jnp.where(core == 0, jnp.stack([mine, theirs], 1), jnp.stack([theirs, mine], 1))
    attn_mat = pair.reshape(dim, -1)
    qkv_mat = attn_mat[:, : 3 * cols]
    out_mat = attn_mat[:, 3 * cols : 4 * cols]
    router_mat = attn_mat[:, 4 * cols :]
    gains = lax.all_gather(jnp.stack([query_gain, key_gain]), "fsdp", axis=2, tiled=True)
    gains = gains.astype(F32).reshape(2, 1, cols)

    def by_rows(weight):
        return weight.transpose(1, 0, 2).reshape(piece, experts, span)

    moe_pack = jnp.stack(
        [
            by_rows((gate_weight.astype(F32) * m_gain[None]).astype(BF)),
            by_rows((up_weight.astype(F32) * m_gain[None]).astype(BF)),
            down_weight.transpose(2, 0, 1),
        ]
    )
    keep_half = lax.dynamic_slice_in_dim(moe_pack, core * local, local, 2).reshape(3, piece, local * span)
    give_half = lax.dynamic_slice_in_dim(moe_pack, (1 - core) * local, local, 2).reshape(3, piece, local * span)
    got_half = swap_core(give_half)
    rows_low = jnp.where(core == 0, keep_half, got_half)
    rows_high = jnp.where(core == 0, got_half, keep_half)

    raw = dot(normed, qkv_mat)
    totals = total_tp(
        jnp.stack([jnp.sum(raw[:, :cols] ** 2, axis=1), jnp.sum(raw[:, cols : 2 * cols] ** 2, axis=1)])
    )
    norms = lax.rsqrt(totals / dim + EPS).T
    cos, sin = angles(seg_ids)
    query_rot, key_rot, value_low = turn(raw, norms, cos, sin, gains)
    half = fsdp // 2
    remote = lax.ppermute(jnp.stack([key_rot, value_low]), "fsdp", [(i, i + half) for i in range(half)])
    cont = (place >= half).astype(jnp.int32).reshape(1)
    seg_col, seg_row = seg_ids[:, None], seg_ids[None, :]

    low_parts = spread(rows_low, bits)
    high_parts = spread(rows_high, back_bits)
    mats = []
    for j in range(3):
        mats.append(jnp.concatenate([p[j] for lo, hi in zip(low_parts, high_parts) for p in (lo, hi)], axis=0))
    gate_mat, up_mat, down_mat = mats

    attended = attend(cont, query_rot, key_rot, value_low, remote[0], remote[1], seg_col, seg_row)
    attn_part = dot(attended, out_mat, NT)
    share = tokens // tp
    parts = rows_rel(attn_part)
    after_attn = stream + line_scatter([parts[d * share : (d + 1) * share] for d in range(tp)])
    norm_second = inverse_norm(after_attn)
    hat_two = after_attn * norm_second

    up_rel = to_rel(cotangent, 1)
    upstream = jnp.concatenate(line_gather(up_rel), axis=0)
    upstream_far = swap_core(upstream)
    mlp_own = jnp.concatenate(line_gather(hat_two.astype(BF)), axis=0)
    mlp_far = swap_core(mlp_own)
    keep = rows_rel(kept_pairs(routes, route_order[0], experts))
    keep_far = swap_core(keep)

    def routed(x, kept):
        logits = dot(x, router_mat)[:, :experts]
        peak = jnp.max(logits, axis=-1, keepdims=True)
        grown = jnp.exp(logits - peak)
        probs = grown / jnp.sum(grown, axis=-1, keepdims=True)
        weight = lax.dynamic_slice_in_dim(probs * kept, core * local, local, 1)
        return probs, weight

    probs_far, weight_far = routed(mlp_far, keep_far)
    probs_own, weight_own = routed(mlp_own, keep)
    act_far, dg_far, du_far, s_far = hidden(mlp_far, upstream_far, gate_mat, up_mat, down_mat, weight_far)
    act_own, dg_own, du_own, s_own = hidden(mlp_own, upstream, gate_mat, up_mat, down_mat, weight_own)

    def logits_back(s, kept, probs):
        zero = jnp.zeros_like(s)
        wide = jnp.where(core == 0, jnp.concatenate([s, zero], 1), jnp.concatenate([zero, s], 1)) * kept
        grad = probs * (wide - jnp.sum(probs * wide, axis=-1, keepdims=True))
        return jnp.pad(grad, ((0, 0), (0, 128 - experts))).astype(BF)

    gl_far = logits_back(s_far, keep_far, probs_far)
    gl_own = logits_back(s_own, keep, probs_own)
    back_far = mix([(dg_far, gate_mat), (du_far, up_mat), (gl_far, router_mat)], BF)
    back_got = swap_core(back_far)
    back_own = mix([(dg_own, gate_mat), (du_own, up_mat), (gl_own, router_mat)], F32)
    back_sum = back_own + back_got.astype(F32)
    grad_scaled = line_scatter([back_sum[d * share : (d + 1) * share] for d in range(tp)])

    out_far = mix([(act_far, down_mat)], BF)
    out_got = swap_core(out_far)
    out_own = mix([(act_own, down_mat)], F32)
    out_sum = out_own + out_got.astype(F32)

    wide_x = jnp.concatenate([mlp_own, mlp_far], axis=0)
    wide_c = jnp.concatenate([upstream, upstream_far], axis=0)
    act = jnp.concatenate([act_own, act_far], axis=0)
    dg = jnp.concatenate([dg_own, dg_far], axis=0)
    du = jnp.concatenate([du_own, du_far], axis=0)
    chips = fsdp // 2
    width = dim // chips
    half_cols = local * span // 2
    terms = []
    for left, right in ((wide_x, dg), (wide_x, du), (wide_c, act)):
        sums = []
        for h, order in ((0, back_bits), (1, bits)):
            pieces = [
                dot(
                    left[:, r * width : (r + 1) * width],
                    right[:, h * half_cols : (h + 1) * half_cols],
                    TN,
                ).astype(BF)
                for r in range(chips)
            ]
            sums.append(collect(pieces, order))
        terms.append(jnp.concatenate(sums, axis=1))
    moe_grad = jnp.stack(terms).reshape(3, 2, piece, local, span)
    mine = lax.dynamic_index_in_dim(moe_grad, core, 1, keepdims=False)
    others = swap_core(lax.dynamic_index_in_dim(moe_grad, 1 - core, 1, keepdims=False).astype(BF)).astype(F32)
    moe_grad = jnp.where(
        core == 0, jnp.concatenate([mine, others], 2), jnp.concatenate([others, mine], 2)
    )
    grad_gate = moe_grad[0].transpose(1, 0, 2) * m_gain[None]
    grad_up = moe_grad[1].transpose(1, 0, 2) * m_gain[None]
    grad_down = moe_grad[2].transpose(1, 2, 0)

    router_term = dot(wide_x, jnp.concatenate([gl_own, gl_far], axis=0), TN)[:, :experts]
    mlp_gain_part = jnp.sum(grad_scaled * hat_two, axis=0)
    grad_after = up_rel.astype(F32) + norm_second * (
        grad_scaled - hat_two * jnp.mean(grad_scaled * hat_two, axis=-1, keepdims=True)
    )
    grad_attn = rows_abs(line_gather(grad_after.astype(BF)))

    block_rel = after_attn + line_scatter([out_sum[d * share : (d + 1) * share] for d in range(tp)])
    block_out = to_rel(block_rel, 1)

    grad_attended = dot(grad_attn, out_mat).astype(BF)
    dq, dk, dv, dk_far, dv_far = attend_back(
        cont, query_rot, key_rot, value_low, remote[0], remote[1], grad_attended, seg_col, seg_row
    )
    returned = lax.ppermute(jnp.stack([dk_far, dv_far]), "fsdp", [(i + half, i) for i in range(half)])
    grad_value = (dv + returned[1].astype(F32)).astype(BF)
    u_query, u_key, dots, gain_parts = turn_back(dq, dk, returned[0], raw, norms, cos, sin, gains)
    dots = total_tp(dots.T).T

    def raw_back(u, x, j):
        n = norms[:, j : j + 1]
        return (n * u - x * (n * n * n * dots[:, j : j + 1] / dim)).astype(BF)

    grad_raw = jnp.concatenate(
        [raw_back(u_query, raw[:, :cols], 0), raw_back(u_key, raw[:, cols : 2 * cols], 1), grad_value], axis=1
    )
    normed_part = dot(grad_raw, qkv_mat, NT)
    parts = rows_rel(normed_part)
    grad_hat = line_scatter([parts[d * share : (d + 1) * share] for d in range(tp)])
    attn_gain_part = jnp.sum(normed_part * normed.astype(F32), axis=0)
    grad_input = to_rel(
        grad_after + norm_first * (grad_hat - hat_one * jnp.mean(grad_hat * hat_one, axis=-1, keepdims=True)), 1
    )

    def by_core(x, which):
        return lax.dynamic_index_in_dim(x.reshape(x.shape[0], chips, 2, piece), which, 2, keepdims=False).reshape(
            x.shape[0], -1
        )

    def weight_back(left, right):
        away = swap_core(dot(by_core(left, 1 - core), right, TN).astype(BF))
        both = (dot(by_core(left, core), right, TN) + away.astype(F32)).astype(BF)
        middle = right.shape[1] // 2
        rows = [both[r * piece : (r + 1) * piece] for r in range(chips)]
        return jnp.concatenate(
            [collect([r[:, :middle] for r in rows], back_bits), collect([r[:, middle:] for r in rows], bits)], axis=1
        )

    grad_out_proj = weight_back(grad_attn, attended).T
    grad_qkv = weight_back(normed, grad_raw) * a_gain

    small = to_rel(jnp.concatenate([mlp_gain_part[:, None], router_term], axis=1), 0)
    small = lax.psum(lax.psum_scatter(small, "fsdp", scatter_dimension=0, tiled=True), "tp")
    grad_mlp_gain = small[:, 0] / m_gain[:, 0]
    grad_router = small[:, 1:] * m_gain
    last = lax.psum_scatter(to_rel(attn_gain_part, 0), "fsdp", scatter_dimension=0, tiled=True)
    grad_attn_gain = lax.psum(last, "tp") / a_gain[:, 0]
    gain_grads = lax.psum_scatter(
        gain_parts.reshape(2, cols // HEAD_DIM, HEAD_DIM), "fsdp", scatter_dimension=2, tiled=True
    )
    return (
        block_out,
        grad_input,
        grad_qkv[:, :cols],
        grad_qkv[:, cols : 2 * cols],
        grad_qkv[:, 2 * cols :],
        grad_out_proj,
        gain_grads[0],
        gain_grads[1],
        grad_attn_gain,
        grad_mlp_gain,
        grad_router,
        grad_gate,
        grad_up,
        grad_down,
    )


def solution(mesh):
    rows = P(("fsdp", "tp"), None)
    in_specs = (
        rows,
        P("fsdp", "tp"),
        P("fsdp", "tp"),
        P("fsdp", "tp"),
        P("tp", "fsdp"),
        P("tp", "fsdp"),
        P("tp", "fsdp"),
        P("fsdp"),
        P("fsdp"),
        P("fsdp", None),
        P(None, "fsdp", "tp"),
        P(None, "fsdp", "tp"),
        P(None, "tp", "fsdp"),
        P("fsdp", None),
        P("fsdp", None),
        P("fsdp"),
        rows,
    )
    out_specs = (
        rows,
        rows,
        P("fsdp", "tp"),
        P("fsdp", "tp"),
        P("fsdp", "tp"),
        P("tp", "fsdp"),
        P("tp", "fsdp"),
        P("tp", "fsdp"),
        P("fsdp"),
        P("fsdp"),
        P("fsdp", None),
        P(None, "fsdp", "tp"),
        P(None, "fsdp", "tp"),
        P(None, "tp", "fsdp"),
    )
    return jax.shard_map(on_device, mesh=mesh, in_specs=in_specs, out_specs=out_specs, check_vma=False)
```

```python
import functools
import math

import jax
import jax.numpy as jnp
from jax import lax
from jax.experimental import pallas as pl
from jax.experimental.pallas import tpu as pltpu
from jax.sharding import PartitionSpec as P

HEAD_DIM = 128
CONTS = 8
CAP = 512
EPS = 1e-05
NEG = -1e30
QT = 256
BF = jnp.bfloat16
F32 = jnp.float32
NT = (((1,), (1,)), ((), ()))
TN = (((0,), (0,)), ((), ()))


def dot(a, b, dims=(((1,), (0,)), ((), ()))):
    return lax.dot_general(a, b, dims, preferred_element_type=F32)


def params(count=1):
    return pltpu.CompilerParams(
        dimension_semantics=("arbitrary",) * count, vmem_limit_bytes=56 << 20
    )


def cost(flops, nbytes, trans=0):
    return pl.CostEstimate(flops=int(flops), bytes_accessed=int(nbytes), transcendentals=int(trans))


def swap_core(value):
    count = lax.axis_size("fsdp")
    return lax.ppermute(value, "fsdp", [(i, i ^ 1) for i in range(count)])


def chip_groups():
    count = lax.axis_size("fsdp")
    return [list(range(c, count, 2)) for c in range(2)]


def after(value, *others):
    return lax.optimization_barrier((value,) + others)[0]


def line_gather(value, halves=2, gates=None):
    count = lax.axis_size("tp")
    gates = gates or {}
    rows = value.shape[0] // halves
    ups = [[value[h * rows : (h + 1) * rows]] for h in range(halves)]
    downs = [[u[0]] for u in ups]
    for s in range(1, count):
        for up, down in zip(ups, downs):
            ahead, behind = up[-1], down[-1]
            if s > 1 or s in gates:
                ahead, behind = lax.optimization_barrier((ahead, behind, *gates.get(s, ())))[:2]
            up.append(lax.ppermute(ahead, "tp", [(i, i + 1) for i in range(s - 1, count - 1)]))
            down.append(lax.ppermute(behind, "tp", [(i + 1, i) for i in range(count - s)]))
    arrivals = [[t[s] for t in ups + downs] for s in range(count)]
    return assemble(ups, downs), arrivals


def assemble_kernel(count, halves, place_ref, *refs):
    out, sems = refs[-2], refs[-1]
    place = place_ref[0]
    rows = out.shape[0] // (count * halves)
    stride = 2 * count - 1

    def each(action):
        for h in range(halves):
            mine = refs[h * stride : (h + 1) * stride]
            for j in range(count):
                target = out.at[pl.ds((j * halves + h) * rows, rows), :]
                for s in range(-(count - 1), count):
                    source = mine[s + count - 1]

                    @pl.when(place - j == s)
                    def _(source=source, target=target, h=h, j=j):
                        action(pltpu.make_async_copy(source, target, sems.at[h * count + j]))

    each(lambda copy: copy.start())
    each(lambda copy: copy.wait())


def assemble(ups, downs):
    count, halves = len(ups[0]), len(ups)
    rows, dim = ups[0][0].shape
    flat = []
    for up, down in zip(ups, downs):
        flat += down[:0:-1] + up
    anywhere = pl.BlockSpec(memory_space=pl.ANY)
    return pl.pallas_call(
        functools.partial(assemble_kernel, count, halves),
        in_specs=[pl.BlockSpec(memory_space=pltpu.SMEM)] + [anywhere] * len(flat),
        out_specs=pl.BlockSpec(memory_space=pltpu.VMEM),
        out_shape=jax.ShapeDtypeStruct((count * halves * rows, dim), ups[0][0].dtype),
        scratch_shapes=[pltpu.SemaphoreType.DMA((count * halves,))],
        cost_estimate=cost(1, 4 * count * halves * rows * dim),
        name="assemble",
    )(lax.axis_index("tp").astype(jnp.int32).reshape(1), *flat)


def line_scatter(parts, gates=None):
    count = lax.axis_size("tp")
    gates = gates or {}
    up = down = None
    arrivals, sends = [()], [()]
    for s in range(count - 1, 0, -1):
        send_up, send_down = parts[s].astype(F32), parts[count - s].astype(F32)
        if up is not None:
            send_up, send_down = send_up + up.astype(F32), send_down + down.astype(F32)
        step = count - s
        send_up, send_down = send_up.astype(BF), send_down.astype(BF)
        send_up, send_down = lax.optimization_barrier((send_up, send_down, *gates.get(step, ())))[:2]
        sends.append((send_up, send_down))
        up = lax.ppermute(send_up, "tp", [(i, i + 1) for i in range(count - s)])
        down = lax.ppermute(send_down, "tp", [(i + 1, i) for i in range(s - 1, count - 1)])
        arrivals.append((up, down))
    return parts[0].astype(F32) + up.astype(F32) + down.astype(F32), arrivals, sends


def total_fsdp(value):
    count = lax.axis_size("fsdp")
    bit = 1
    while bit < count:
        value = value + lax.ppermute(value, "fsdp", [(i, i ^ bit) for i in range(count)])
        bit *= 2
    return value


def total_tp(value):
    count = lax.axis_size("tp")
    out = flat = lax.optimization_barrier(value.reshape(-1, 128))
    for s in range(1, count):
        out = out + lax.ppermute(flat, "tp", [(i, (i + s) % count) for i in range(count)])
    return lax.optimization_barrier(out).reshape(value.shape)


def shares(value):
    count = lax.axis_size("tp")
    place = lax.axis_index("tp")
    rows = value.shape[0] // count
    return [lax.dynamic_slice_in_dim(value, ((place + d) % count) * rows, rows, 0) for d in range(count)]


def keep_kernel(pos_ref, keep_ref):
    pos = pos_ref[...]
    bound = jnp.zeros((1, pos.shape[1]), jnp.int32)
    for b in range(13, -1, -1):
        trial = bound + (1 << b)
        count = jnp.sum((pos <= trial).astype(F32), axis=0, keepdims=True)
        bound = jnp.where(count <= CAP, trial, bound)
    keep_ref[...] = (pos <= bound).astype(F32)


def kept_pairs(routes, order_row, experts):
    pairs = order_row.shape[0]
    tokens = routes.shape[0]
    step = jnp.arange(pairs, dtype=jnp.int32)
    high = (order_row[:, None] // 128 == jnp.arange(pairs // 128, dtype=jnp.int32)[None, :]).astype(BF)
    low = (order_row[:, None] % 128 == jnp.arange(128, dtype=jnp.int32)[None, :]).astype(BF)
    step_high = (step // 64).astype(BF)[:, None]
    step_low = (step % 64).astype(BF)[:, None]
    table = 64.0 * dot(high * step_high, low, TN) + dot(high * step_low, low, TN)
    place = table.astype(jnp.int32).reshape(tokens, -1) + 1
    hot = routes[:, :, None] == jnp.arange(experts, dtype=jnp.int32)[None, None, :]
    pos = jnp.sum(jnp.where(hot, place[:, :, None], 0), axis=1)
    pos = jnp.where(pos == 0, 1 << 20, pos)
    return pl.pallas_call(
        keep_kernel, out_shape=jax.ShapeDtypeStruct((tokens, experts), F32), name="keep"
    )(pos)


def turn_kernel(q_ref, k_ref, norm_ref, cos_ref, sin_ref, gain_ref, q_out, k_out):
    cos, sin = cos_ref[...], sin_ref[...]
    for slot, (raw, out) in enumerate(((q_ref, q_out), (k_ref, k_out))):
        x = raw[...] * norm_ref[:, slot : slot + 1] * gain_ref[slot]
        out[...] = (x * cos + pltpu.roll(x, HEAD_DIM // 2, 1) * sin).astype(BF)


def turn(raw, norms, cos, sin, gains):
    rows = raw.shape[0]
    heads = raw.shape[1] // (3 * HEAD_DIM)
    part = lambda j: pl.BlockSpec((rows, HEAD_DIM), lambda h: (0, j * heads + h))
    whole = lambda shape: pl.BlockSpec(shape, lambda h: (0,) * len(shape))
    return pl.pallas_call(
        turn_kernel,
        grid=(heads,),
        in_specs=[
            part(0),
            part(1),
            whole(norms.shape),
            whole(cos.shape),
            whole(sin.shape),
            pl.BlockSpec((2, 1, HEAD_DIM), lambda h: (0, 0, h)),
        ],
        out_specs=[part(0)] * 2,
        out_shape=[jax.ShapeDtypeStruct((rows, heads * HEAD_DIM), BF)] * 2,
        compiler_params=params(),
        cost_estimate=cost(10 * raw.size, 6 * raw.size),
        name="turn",
    )(raw, raw, norms, cos, sin, gains)


def turn_back_kernel(
    dq_ref, dk_ref, dkr_ref, q_ref, k_ref, norm_ref, cos_ref, sin_ref, gain_ref, uq_out, uk_out, dots_out, part_out
):
    cos, sin = cos_ref[...], sin_ref[...]
    grads = (dq_ref[...], dk_ref[...] + dkr_ref[...].astype(F32))
    lane = lax.broadcasted_iota(jnp.int32, dots_out.shape, 1)

    @pl.when(pl.program_id(0) == 0)
    def _():
        dots_out[...] = jnp.zeros_like(dots_out)

    for slot, (grad, raw, out) in enumerate(zip(grads, (q_ref, k_ref), (uq_out, uk_out))):
        back = grad * cos - pltpu.roll(grad, HEAD_DIM // 2, 1) * sin
        x = raw[...]
        part_out[slot] = jnp.sum(back * x * norm_ref[:, slot : slot + 1], axis=0, keepdims=True)
        u = back * gain_ref[slot]
        out[...] = u
        dots_out[...] += jnp.where(lane == slot, jnp.sum(u * x, axis=1, keepdims=True), 0.0)


def turn_back(dq, dk, dk_more, raw, norms, cos, sin, gains):
    rows = raw.shape[0]
    heads = raw.shape[1] // (3 * HEAD_DIM)
    part = lambda j: pl.BlockSpec((rows, HEAD_DIM), lambda h: (0, j * heads + h))
    whole = lambda shape: pl.BlockSpec(shape, lambda h: (0,) * len(shape))
    gain_spec = pl.BlockSpec((2, 1, HEAD_DIM), lambda h: (0, 0, h))
    wide = jax.ShapeDtypeStruct((rows, heads * HEAD_DIM), F32)
    return pl.pallas_call(
        turn_back_kernel,
        grid=(heads,),
        in_specs=[
            part(0),
            part(0),
            part(0),
            part(0),
            part(1),
            whole(norms.shape),
            whole(cos.shape),
            whole(sin.shape),
            gain_spec,
        ],
        out_specs=[part(0), part(0), whole((rows, 2)), gain_spec],
        out_shape=[
            wide,
            wide,
            jax.ShapeDtypeStruct((rows, 2), F32),
            jax.ShapeDtypeStruct((2, 1, heads * HEAD_DIM), F32),
        ],
        compiler_params=params(),
        cost_estimate=cost(10 * raw.size, 8 * raw.size),
        name="turn_back",
    )(dq, dk, dk_more, raw, raw, norms, cos, sin, gains)


def own_mask(seg_col, seg_row, first_row, row_count, first_key, key_count):
    rows = lax.broadcasted_iota(jnp.int32, (row_count, key_count), 0) + first_row
    keys = lax.broadcasted_iota(jnp.int32, (row_count, key_count), 1) + first_key
    same = seg_col[first_row : first_row + row_count, :] == seg_row[:, first_key : first_key + key_count]
    return same & (keys <= rows)


SCALE = HEAD_DIM ** (-0.5)


def tile_probs(q_tile, k_ref, seg_col, seg_row, first_row, first_key, keys, kr):
    own = dot(q_tile, k_ref[first_key : first_key + keys, :], NT)
    own = jnp.where(own_mask(seg_col, seg_row, first_row, QT, first_key, keys), own, NEG)
    peak = jnp.max(own, axis=1, keepdims=True)
    far = None
    if kr is not None:
        far = dot(q_tile, kr[...], NT)
        peak = jnp.maximum(peak, jnp.max(far, axis=1, keepdims=True))
        far = jnp.exp((far - peak) * SCALE)
    own = jnp.exp((own - peak) * SCALE)
    total = jnp.sum(own, axis=1, keepdims=True)
    if far is not None:
        total = total + jnp.sum(far, axis=1, keepdims=True)
    inverse = 1.0 / total
    return own * inverse, (None if far is None else far * inverse)


def attend_kernel(cont_ref, q_ref, k_ref, v_ref, kr_ref, vr_ref, col_ref, row_ref, out_ref):
    rows = q_ref.shape[0]

    def run(far):
        for first in range(0, rows, QT):
            start = max(0, first - QT) if far else 0
            keys = first + QT - start
            own, other = tile_probs(
                q_ref[first : first + QT, :], k_ref, col_ref, row_ref, first, start, keys, kr_ref if far else None
            )
            out = dot(own.astype(BF), v_ref[start : start + keys, :])
            if far:
                out = out + dot(other.astype(BF), vr_ref[...])
            out_ref[first : first + QT, :] = out.astype(BF)

    pl.when(cont_ref[0] == 0)(lambda: run(False))
    pl.when(cont_ref[0] != 0)(lambda: run(True))


def attend_specs(rows, count):
    head = pl.BlockSpec((rows, HEAD_DIM), lambda h, c: (0, h))
    return [head] * count + [
        pl.BlockSpec((rows, 1), lambda h, c: (0, 0)),
        pl.BlockSpec((1, rows), lambda h, c: (0, 0)),
    ], head


def attend(cont, q, k, v, kr, vr, seg_col, seg_row):
    rows, width = q.shape
    specs, head = attend_specs(rows, 5)
    return pl.pallas_call(
        attend_kernel,
        grid_spec=pltpu.PrefetchScalarGridSpec(
            num_scalar_prefetch=1, grid=(width // HEAD_DIM,), in_specs=specs, out_specs=head
        ),
        out_shape=jax.ShapeDtypeStruct((rows, width), BF),
        compiler_params=params(),
        cost_estimate=cost(6 * rows * rows * width, 12 * rows * width, rows * rows * 6),
        name="attend",
    )(cont, q, k, v, kr, vr, seg_col, seg_row)


def attend_back_kernel(
    cont_ref, q_ref, k_ref, v_ref, kr_ref, vr_ref, do_ref, col_ref, row_ref, dq_ref, dk_ref, dv_ref, dkr_ref, dvr_ref, far_dk, far_dv
):
    rows = q_ref.shape[0]
    dk_ref[...] = jnp.zeros_like(dk_ref)
    dv_ref[...] = jnp.zeros_like(dv_ref)

    def run(far):
        if far:
            far_dk[...] = jnp.zeros_like(far_dk)
            far_dv[...] = jnp.zeros_like(far_dv)
        for first in range(0, rows, QT):
            start = max(0, first - QT) if far else 0
            keys = first + QT - start
            here = slice(start, start + keys)
            q_tile = q_ref[first : first + QT, :]
            do_tile = do_ref[first : first + QT, :]
            own, other = tile_probs(q_tile, k_ref, col_ref, row_ref, first, start, keys, kr_ref if far else None)
            grad = dot(do_tile, v_ref[here, :], NT)
            mean = jnp.sum(own * grad, axis=1, keepdims=True)
            if far:
                grad_far = dot(do_tile, vr_ref[...], NT)
                mean = mean + jnp.sum(other * grad_far, axis=1, keepdims=True)
            slope = (own * (grad - mean)).astype(BF)
            dq = dot(slope, k_ref[here, :])
            dk_ref[here, :] += dot(slope, q_tile, TN) * SCALE
            dv_ref[here, :] += dot(own.astype(BF), do_tile, TN)
            if far:
                slope = (other * (grad_far - mean)).astype(BF)
                dq = dq + dot(slope, kr_ref[...])
                far_dk[...] += dot(slope, q_tile, TN) * SCALE
                far_dv[...] += dot(other.astype(BF), do_tile, TN)
            dq_ref[first : first + QT, :] = dq * SCALE
        if far:
            dkr_ref[...] = far_dk[...].astype(BF)
            dvr_ref[...] = far_dv[...].astype(BF)
        else:
            dkr_ref[...] = jnp.zeros_like(dkr_ref)
            dvr_ref[...] = jnp.zeros_like(dvr_ref)

    pl.when(cont_ref[0] == 0)(lambda: run(False))
    pl.when(cont_ref[0] != 0)(lambda: run(True))


def attend_back(cont, q, k, v, kr, vr, do, seg_col, seg_row):
    rows, width = q.shape
    specs, head = attend_specs(rows, 6)
    wide = jax.ShapeDtypeStruct((rows, width), F32)
    low = jax.ShapeDtypeStruct((rows, width), BF)
    return pl.pallas_call(
        attend_back_kernel,
        grid_spec=pltpu.PrefetchScalarGridSpec(
            num_scalar_prefetch=1,
            grid=(width // HEAD_DIM,),
            in_specs=specs,
            out_specs=[head] * 5,
            scratch_shapes=[pltpu.VMEM((rows, HEAD_DIM), F32)] * 2,
        ),
        out_shape=[wide, wide, wide, low, low],
        compiler_params=params(),
        cost_estimate=cost(15 * rows * rows * width, 30 * rows * width, rows * rows * 6),
        name="attend_back",
    )(cont, q, k, v, kr, vr, do, seg_col, seg_row)


def hidden_kernel(x_ref, c_ref, g_ref, u_ref, d_ref, w_ref, act_out, dg_out, du_out, s_out):
    expert = pl.program_id(0)
    gate = dot(x_ref[...], g_ref[...])
    up = dot(x_ref[...], u_ref[...])
    back = dot(c_ref[...], d_ref[...])
    lane = lax.broadcasted_iota(jnp.int32, s_out.shape, 1)
    weight = jnp.sum(jnp.where(lane == expert, w_ref[...], 0.0), axis=1, keepdims=True)
    sig = 1.0 / (1.0 + jnp.exp(-gate))
    swish = gate * sig
    act = swish * up
    act_out[...] = (act * weight).astype(BF)
    s = jnp.sum(act * back, axis=1, keepdims=True)
    back = back * weight
    dg_out[...] = (back * up * (sig + swish * (1.0 - sig))).astype(BF)
    du_out[...] = (back * swish).astype(BF)

    @pl.when(expert == 0)
    def _():
        s_out[...] = jnp.zeros_like(s_out)

    s_out[...] = jnp.where(lane == expert, s, s_out[...])


def hidden(x, c, mats, low_mat, weight, block, held=None):
    rows, dim = x.shape
    experts = weight.shape[1]
    span = low_mat.shape[1] // experts
    full = pl.BlockSpec((rows, dim), lambda e: (0, 0))
    mat = lambda j: pl.BlockSpec((dim, span), lambda e: (0, j * experts + e))
    out = pl.BlockSpec((rows, span), lambda e: (block, e))
    wide = jax.ShapeDtypeStruct((2 * rows, experts * span), BF)
    wider = jax.ShapeDtypeStruct((2 * rows, experts * span + 128), BF)
    held = [] if held is None else list(held)
    kernel = hidden_kernel if not held else lambda *refs: hidden_kernel(*refs[:6], *refs[9:])
    return pl.pallas_call(
        kernel,
        grid=(experts,),
        in_specs=[full, full, mat(0), mat(1), mat(0), pl.BlockSpec((rows, experts), lambda e: (0, 0))]
        + [pl.BlockSpec(memory_space=pl.ANY)] * len(held),
        out_specs=[out, out, out, pl.BlockSpec((rows, experts), lambda e: (0, 0))],
        out_shape=[wide, wider, wide, jax.ShapeDtypeStruct((rows, experts), F32)],
        input_output_aliases={6: 0, 7: 1, 8: 2} if held else {},
        compiler_params=params(),
        cost_estimate=cost(6 * rows * dim * experts * span, 2 * (2 * rows * dim + 6 * dim * experts * span)),
        name="hidden",
    )(x, c, mats, mats, low_mat, weight, *held)


def mix_kernel(*refs):
    count = (len(refs) - 1) // 2
    total = None
    for j in range(count):
        term = dot(refs[2 * j][...], refs[2 * j + 1][...], NT)
        total = term if total is None else total + term
    refs[-1][...] = total.astype(refs[-1].dtype)


def mix(pairs, dtype, rows, tile=512):
    cols = pairs[0][1].shape[0]
    specs, flat, flops, nbytes = [], [], 0, 0
    for a, b, j, k in pairs:
        deep = min(a.shape[1], b.shape[1], b.shape[0])
        specs += [
            pl.BlockSpec((rows, deep), lambda i, k=k: (k, 0)),
            pl.BlockSpec((tile, deep), lambda i, j=j: (i, j)),
        ]
        flat += [a, b]
        flops += 2 * rows * cols * deep
        nbytes += 2 * deep * (rows + cols)
    return pl.pallas_call(
        mix_kernel,
        grid=(cols // tile,),
        in_specs=specs,
        out_specs=pl.BlockSpec((rows, tile), lambda i: (0, i)),
        out_shape=jax.ShapeDtypeStruct((rows, cols), dtype),
        compiler_params=params(),
        cost_estimate=cost(flops, nbytes + 4 * rows * cols),
        name="mix",
    )(*flat)


def attn_pack_kernel(experts, q_ref, k_ref, v_ref, o_ref, r_ref, gain_ref, out_ref):
    cols = q_ref.shape[1]
    for j, ref in enumerate((q_ref, k_ref, v_ref)):
        out_ref[:, j * cols : (j + 1) * cols] = (ref[...].astype(F32) * gain_ref[:, 0:1]).astype(BF)
    out_ref[:, 3 * cols : 4 * cols] = o_ref[...].astype(F32).T.astype(BF)
    rest = r_ref[...].astype(F32)
    lane = lax.broadcasted_iota(jnp.int32, rest.shape, 1)
    out_ref[:, 4 * cols :] = jnp.where(lane < experts, rest * gain_ref[:, 1:2], rest).astype(BF)


def attn_pack(q, k, v, o, r, gains, experts):
    return pl.pallas_call(
        functools.partial(attn_pack_kernel, experts),
        out_shape=jax.ShapeDtypeStruct((q.shape[0], 4 * q.shape[1] + r.shape[1]), BF),
        cost_estimate=cost(1, 4 << 20),
        name="attn_pack",
    )(q, k, v, o, r, gains)


PACK = 4


def moe_pack_kernel(core_ref, g_ref, u_ref, d_ref, gain_ref, g_out, u_out, d_out):
    gain = gain_ref[:, 1:2]
    span = g_ref.shape[2]
    for i in range(PACK):
        here = slice(i * span, (i + 1) * span)
        g_out[0, :, here] = (g_ref[i].astype(F32) * gain).astype(BF)
        u_out[0, :, here] = (u_ref[i].astype(F32) * gain).astype(BF)
        d_out[0, :, here] = d_ref[i].astype(F32).T.astype(BF)


def moe_pack(core, gate, up, down, gains):
    experts, piece, span = gate.shape
    local = experts // 2
    steps = local // PACK
    block = pl.BlockSpec((PACK, piece, span), lambda e, c: (e, 0, 0))
    out = pl.BlockSpec((1, piece, PACK * span), lambda e, c: ((e // steps) ^ c[0], 0, e % steps))
    return pl.pallas_call(
        moe_pack_kernel,
        grid_spec=pltpu.PrefetchScalarGridSpec(
            num_scalar_prefetch=1,
            grid=(experts // PACK,),
            in_specs=[
                block,
                block,
                pl.BlockSpec((PACK, span, piece), lambda e, c: (e, 0, 0)),
                pl.BlockSpec(gains.shape, lambda e, c: (0, 0)),
            ],
            out_specs=[out] * 3,
        ),
        out_shape=[jax.ShapeDtypeStruct((2, piece, local * span), BF)] * 3,
        compiler_params=params(),
        cost_estimate=cost(1, 12 * gate.size),
        name="moe_pack",
    )(core, gate, up, down, gains)


def moe_unpack_kernel(core_ref, *refs):
    mine, theirs, gain_ref, outs = refs[:3], refs[3:6], refs[6], refs[7:]
    steps = pl.num_programs(0) // 2
    here = pl.program_id(0) // steps == core_ref[0]
    gain = gain_ref[:, 1:2]
    span = outs[0].shape[2]
    for i in range(PACK):
        part = slice(i * span, (i + 1) * span)
        g, u, d = (jnp.where(here, a[:, part], b[:, part]).astype(F32) for a, b in zip(mine, theirs))
        outs[0][i] = g * gain
        outs[1][i] = u * gain
        outs[2][i] = d.T


def moe_unpack(core, mine, theirs, gains, experts, local):
    piece = mine[0].shape[0]
    span = mine[1].shape[1] // local
    steps = local // PACK
    block = pl.BlockSpec((piece, PACK * span), lambda e, c: (0, e % steps))
    wide = pl.BlockSpec((PACK, piece, span), lambda e, c: (e, 0, 0))
    return pl.pallas_call(
        moe_unpack_kernel,
        grid_spec=pltpu.PrefetchScalarGridSpec(
            num_scalar_prefetch=1,
            grid=(experts // PACK,),
            in_specs=[block] * 6 + [pl.BlockSpec(gains.shape, lambda e, c: (0, 0))],
            out_specs=[wide, wide, pl.BlockSpec((PACK, span, piece), lambda e, c: (e, 0, 0))],
        ),
        out_shape=[
            jax.ShapeDtypeStruct((experts, piece, span), F32),
            jax.ShapeDtypeStruct((experts, piece, span), F32),
            jax.ShapeDtypeStruct((experts, span, piece), F32),
        ],
        compiler_params=params(),
        cost_estimate=cost(1, 24 * experts * piece * span),
        name="moe_unpack",
    )(core, *mine, *theirs, gains)


def angles(seg_block):
    row_count = seg_block.shape[0]
    labels = jnp.arange(CONTS + 1, dtype=jnp.int32)
    member = (seg_block[:, None] == labels[None, :]).astype(jnp.int32)
    counts = jnp.sum(member, axis=0)
    starts = jnp.sum(jnp.where(labels[:, None] > labels[None, :], counts[None, :], 0), axis=1)
    seg_start = jnp.sum(member * starts[None, :], axis=1)
    offset = row_count * (seg_block != 0).astype(jnp.int32)
    places = jnp.arange(row_count, dtype=jnp.int32) - seg_start + offset
    half = HEAD_DIM // 2
    column = jnp.arange(HEAD_DIM, dtype=jnp.int32)
    frequency = jnp.exp((column % half).astype(F32) * (-2.0 * math.log(10000.0) / HEAD_DIM))
    angle = places.astype(F32)[:, None] * frequency[None, :]
    sign = jnp.where(column < half, -1.0, 1.0).astype(F32)
    return jnp.cos(angle), jnp.sin(angle) * sign[None, :]


def inverse_norm(values):
    return lax.rsqrt(jnp.mean(values * values, axis=-1, keepdims=True) + EPS)


def on_device(
    residual,
    query_weight,
    key_weight,
    value_weight,
    out_weight,
    query_gain,
    key_gain,
    attn_gain,
    mlp_gain,
    router_weight,
    gate_weight,
    up_weight,
    down_weight,
    routes,
    route_order,
    seg_ids,
    cotangent,
):
    fsdp, tp = lax.axis_size("fsdp"), lax.axis_size("tp")
    place = lax.axis_index("fsdp")
    core = place % 2
    core_arg = core.astype(jnp.int32).reshape(1)
    dim = residual.shape[1]
    piece = dim // fsdp
    tokens = seg_ids.shape[0]
    share = tokens // tp
    experts, _, span = gate_weight.shape
    local = experts // 2
    cols = query_weight.shape[1]
    heads = cols // HEAD_DIM
    groups = chip_groups()

    norm_gains = jnp.stack([attn_gain, mlp_gain], axis=1).astype(F32)

    stream = residual.astype(F32)
    norm_first = inverse_norm(stream)
    hat_one = stream * norm_first
    hat_low = hat_one.astype(BF)
    normed, steps_one = line_gather(hat_low)

    narrow = HEAD_DIM // fsdp
    gain_col = jnp.stack([query_gain, key_gain]).reshape(-1, 1)
    gain_col = jnp.pad(gain_col, ((0, piece - gain_col.shape[0]), (0, 127 - experts)))
    attn_mat = lax.all_gather(
        attn_pack(
            after(query_weight, hat_low),
            key_weight,
            value_weight,
            out_weight,
            jnp.concatenate([router_weight, gain_col], axis=1),
            norm_gains,
            experts,
        ),
        "fsdp",
        axis=0,
        tiled=True,
    )
    qkv_mat = attn_mat[:, : 3 * cols]
    out_mat = attn_mat[:, 3 * cols : 4 * cols]
    router_mat = attn_mat[:, 4 * cols :]
    gains = router_mat[:, experts].astype(F32).reshape(fsdp, piece)[:, : 2 * heads * narrow]
    gains = gains.reshape(fsdp, 2, heads, narrow).transpose(1, 2, 0, 3).reshape(2, 1, cols)
    lane = jnp.arange(128, dtype=jnp.int32)[None, :]
    router_mat = jnp.where(lane < experts, router_mat, 0)

    packs = moe_pack(core_arg, after(gate_weight, hat_low), up_weight, down_weight, norm_gains)

    def both_rows(kept, given):
        got = swap_core(given)
        return jnp.concatenate([jnp.where(core == 0, kept, got), jnp.where(core == 0, got, kept)], axis=0)

    def over_chips(value):
        return lax.all_gather(value, "fsdp", axis=0, tiled=True, axis_index_groups=groups)

    low_rows = both_rows(packs[2][0], packs[2][1])
    low_mat = over_chips(after(low_rows, attn_mat, *steps_one[2]))
    rows = both_rows(*[jnp.concatenate([packs[0][h], packs[1][h]], axis=1) for h in range(2)])

    raw = dot(normed, qkv_mat)
    half = fsdp // 2
    forth = [(i, i + half) for i in range(half)]
    value_low = raw[:, 2 * cols :].astype(BF)
    value_far = lax.ppermute(value_low, "fsdp", forth)
    upstream, steps_up = line_gather(cotangent, gates={1: steps_one[3]})
    query_key = after(raw, value_low)
    totals = jnp.stack(
        [jnp.sum(query_key[:, :cols] ** 2, axis=1), jnp.sum(query_key[:, cols : 2 * cols] ** 2, axis=1)]
    )
    totals = total_tp(after(totals, *steps_up[1]))
    norms = lax.rsqrt(totals / dim + EPS).T
    cos, sin = angles(seg_ids)
    query_rot, key_rot = turn(raw, after(norms, value_far, *steps_up[2]), cos, sin, gains)
    key_far = lax.ppermute(key_rot, "fsdp", forth)
    cont = (place >= half).astype(jnp.int32).reshape(1)
    seg_col, seg_row = seg_ids[:, None], seg_ids[None, :]
    mats = over_chips(after(rows, key_far, value_far))

    upstream_far = swap_core(upstream)

    attended = attend(
        cont, after(query_rot, *steps_up[3]), key_rot, value_low, key_far, value_far, seg_col, seg_row
    )
    attn_part = dot(attended, out_mat, NT).astype(BF)
    attn_out, _, _ = line_scatter(shares(attn_part))
    after_attn = stream + attn_out
    norm_second = inverse_norm(after_attn)
    hat_two = after_attn * norm_second

    keep = kept_pairs(routes, route_order[0], experts)
    keep_far = swap_core(keep)
    wide_c = jnp.concatenate([upstream, upstream_far], axis=0)
    mlp_own, _ = line_gather(hat_two.astype(BF), gates={2: [keep_far], 3: [wide_c]})
    mlp_far = swap_core(mlp_own)

    def routed(x, kept):
        logits = dot(x, router_mat)[:, :experts]
        grown = jnp.exp(logits - jnp.max(logits, axis=-1, keepdims=True))
        probs = grown / jnp.sum(grown, axis=-1, keepdims=True)
        return probs, lax.dynamic_slice_in_dim(probs * kept, core * local, local, 1)

    def logits_back(s, kept, probs):
        zero = jnp.zeros_like(s)
        pair = kept * jnp.where(core == 0, jnp.concatenate([s, zero], 1), jnp.concatenate([zero, s], 1))
        grad = probs * (pair - jnp.sum(probs * pair, axis=-1, keepdims=True))
        return jnp.pad(grad, ((0, 0), (0, 128 - experts))).astype(BF)

    probs_own, weight_own = routed(mlp_own, keep)
    *held, s_own = hidden(mlp_own, upstream, mats, low_mat, weight_own, 0)
    probs_far, weight_far = routed(mlp_far, keep_far)
    act, dg, du, s_far = hidden(mlp_far, upstream_far, mats, low_mat, weight_far, 1, held)
    gl_own = logits_back(s_own, keep, probs_own)
    gl_far = logits_back(s_far, keep_far, probs_far)

    def both_cores(own, got):
        return [a.astype(F32) + b.astype(F32) for a, b in zip(shares(own), shares(got))]

    back_far = mix([(dg, mats, 0, 1), (du, mats, 1, 1), (gl_far, router_mat, 0, 0)], BF, tokens)
    back_got = swap_core(back_far)
    back_own = mix([(dg, mats, 0, 0), (du, mats, 1, 0), (gl_own, router_mat, 0, 0)], BF, tokens)
    grad_scaled, _, back_sends = line_scatter(both_cores(back_own, back_got))

    def scattered(value):
        return lax.psum_scatter(value, "fsdp", scatter_dimension=0, tiled=True, axis_index_groups=groups)

    dg = lax.dynamic_update_slice(
        after(dg, back_own, back_got), jnp.concatenate([gl_own, gl_far], axis=0), (0, local * span)
    )
    wide_x = jnp.concatenate([after(mlp_own, back_own), mlp_far], axis=0)
    terms = [
        dot(left, after(right, *gate), TN).astype(BF)
        for left, right, gate in zip((wide_c, wide_x, wide_x), (act, dg, du), back_sends[1:])
    ]
    terms = [terms[1], terms[2], terms[0]]
    sums = [scattered(t) for t in terms]
    out_far = mix([(act, low_mat, 0, 1)], BF, tokens)
    out_own = mix([(act, low_mat, 0, 0)], BF, tokens)
    out_got = swap_core(out_far)

    grad_after = cotangent.astype(F32) + norm_second * (
        grad_scaled - hat_two * jnp.mean(grad_scaled * hat_two, axis=-1, keepdims=True)
    )
    grad_attn, _ = line_gather(after(grad_after.astype(BF), *terms))

    grad_attended = after(dot(grad_attn, out_mat).astype(BF), out_far, out_own)
    dq, dk, dv, dk_far, dv_far = attend_back(
        cont, query_rot, key_rot, value_low, key_far, value_far, grad_attended, seg_col, seg_row
    )
    out_total, out_steps, _ = line_scatter(both_cores(out_own, out_got), {1: [grad_attended], 2: [dk_far]})
    block_out = after_attn + out_total
    back_pairs = [(i + half, i) for i in range(half)]
    dk_got, dv_got = lax.ppermute(dk_far, "fsdp", back_pairs), lax.ppermute(dv_far, "fsdp", back_pairs)
    u_query, u_key, dots, gain_parts = turn_back(
        dq, after(dk, *out_steps[1], sums[2]), dk_got, raw, norms, cos, sin, gains
    )
    dots = total_tp(dots.T).T
    grad_value = (dv + dv_got.astype(F32)).astype(BF)

    def raw_back(u, x, j):
        n = norms[:, j : j + 1]
        return (n * u - x * (n * n * n * dots[:, j : j + 1] / dim)).astype(BF)

    grad_raw = jnp.concatenate(
        [raw_back(u_query, raw[:, :cols], 0), raw_back(u_key, raw[:, cols : 2 * cols], 1), grad_value], axis=1
    )
    normed_part = dot(after(grad_raw, block_out, sums[0]), qkv_mat, NT).astype(BF)
    small = gain_parts.reshape(2, heads, fsdp, narrow).transpose(2, 0, 1, 3).reshape(fsdp, -1)
    grad_raw_later = after(grad_raw, normed_part)
    qkv_term = dot(normed, grad_raw_later, TN).astype(BF)
    late = []
    grad_hat, _, last_sends = line_scatter(shares(normed_part), {3: late})

    sums = [after(t, *last_sends[1]) for t in sums]
    mine = [lax.dynamic_slice_in_dim(t, core * piece, piece, 0) for t in sums]
    theirs = [swap_core(lax.dynamic_slice_in_dim(t, (1 - core) * piece, piece, 0)) for t in sums]
    grad_gate, grad_up, grad_down = moe_unpack(core_arg, mine, theirs, norm_gains, experts, local)
    router_hat = total_tp(sum(t[0][:, local * span :].astype(F32) for t in (mine, theirs)))[:, :experts]
    grad_router = router_hat * norm_gains[:, 1:2]
    gate_term = jnp.sum(gate_weight.astype(F32) * grad_gate + up_weight.astype(F32) * grad_up, axis=(0, 2))
    small = total_fsdp(after(small, *last_sends[1]))

    def summed(value):
        return lax.psum_scatter(value, "fsdp", scatter_dimension=0, tiled=True).astype(F32)

    grad_out_proj = summed(dot(grad_attn, after(attended, dk_far), TN).astype(BF)).T
    attn_sum = summed(qkv_term)
    qkv_hat = [attn_sum[:, j * cols : (j + 1) * cols] for j in range(3)]
    qkv_grad = [norm_gains[:, 0:1] * t for t in qkv_hat]
    small = lax.dynamic_index_in_dim(small, place, 0, keepdims=False)
    small = small.reshape(2, heads, narrow)

    attn_dots = sum(jnp.sum(w.astype(F32) * t, axis=1) for w, t in zip((query_weight, key_weight, value_weight), qkv_hat))
    both_dots = total_tp(jnp.stack([attn_dots, gate_term / norm_gains[:, 1]]))
    grad_attn_gain = both_dots[0]
    grad_mlp_gain = both_dots[1] + jnp.sum(router_weight.astype(F32) * router_hat, axis=1)
    grad_hat = after(grad_hat, both_dots, grad_out_proj, *qkv_grad)
    grad_input = grad_after + norm_first * (grad_hat - hat_one * jnp.mean(grad_hat * hat_one, axis=-1, keepdims=True))
    return (
        block_out,
        grad_input,
        qkv_grad[0],
        qkv_grad[1],
        qkv_grad[2],
        grad_out_proj,
        small[0],
        small[1],
        grad_attn_gain,
        grad_mlp_gain,
        grad_router,
        grad_gate,
        grad_up,
        grad_down,
    )


def solution(mesh):
    rows = P(("fsdp", "tp"), None)
    in_specs = (
        rows,
        P("fsdp", "tp"),
        P("fsdp", "tp"),
        P("fsdp", "tp"),
        P("tp", "fsdp"),
        P("tp", "fsdp"),
        P("tp", "fsdp"),
        P("fsdp"),
        P("fsdp"),
        P("fsdp", None),
        P(None, "fsdp", "tp"),
        P(None, "fsdp", "tp"),
        P(None, "tp", "fsdp"),
        P("fsdp", None),
        P("fsdp", None),
        P("fsdp"),
        rows,
    )
    out_specs = (
        rows,
        rows,
        P("fsdp", "tp"),
        P("fsdp", "tp"),
        P("fsdp", "tp"),
        P("tp", "fsdp"),
        P("tp", "fsdp"),
        P("tp", "fsdp"),
        P("fsdp"),
        P("fsdp"),
        P("fsdp", None),
        P(None, "fsdp", "tp"),
        P(None, "fsdp", "tp"),
        P(None, "tp", "fsdp"),
    )
    return jax.shard_map(on_device, mesh=mesh, in_specs=in_specs, out_specs=out_specs, check_vma=False)
```

```python
import functools
import math

import jax
import jax.numpy as jnp
from jax import lax
from jax.experimental import pallas as pl
from jax.experimental.pallas import tpu as pltpu
from jax.sharding import PartitionSpec as P

HEAD_DIM = 128
CONTS = 8
CAP = 512
EPS = 1e-05
NEG = -1e30
QT = 256
BF = jnp.bfloat16
F32 = jnp.float32
NT = (((1,), (1,)), ((), ()))
TN = (((0,), (0,)), ((), ()))


def dot(a, b, dims=(((1,), (0,)), ((), ()))):
    return lax.dot_general(a, b, dims, preferred_element_type=F32)


def params(count=1):
    return pltpu.CompilerParams(
        dimension_semantics=("arbitrary",) * count, vmem_limit_bytes=56 << 20
    )


def cost(flops, nbytes, trans=0):
    return pl.CostEstimate(flops=int(flops), bytes_accessed=int(nbytes), transcendentals=int(trans))


def swap_core(value):
    count = lax.axis_size("fsdp")
    return lax.ppermute(value, "fsdp", [(i, i ^ 1) for i in range(count)])


def chip_groups():
    count = lax.axis_size("fsdp")
    return [list(range(c, count, 2)) for c in range(2)]


def after(value, *others):
    return lax.optimization_barrier((value,) + others)[0]


def line_gather(value, halves=2, gates=None):
    count = lax.axis_size("tp")
    gates = gates or {}
    rows = value.shape[0] // halves
    ups = [[value[h * rows : (h + 1) * rows]] for h in range(halves)]
    downs = [[u[0]] for u in ups]
    for s in range(1, count):
        for up, down in zip(ups, downs):
            ahead, behind = up[-1], down[-1]
            if s > 1 or s in gates:
                ahead, behind = lax.optimization_barrier((ahead, behind, *gates.get(s, ())))[:2]
            up.append(lax.ppermute(ahead, "tp", [(i, i + 1) for i in range(s - 1, count - 1)]))
            down.append(lax.ppermute(behind, "tp", [(i + 1, i) for i in range(count - s)]))
    arrivals = [[t[s] for t in ups + downs] for s in range(count)]
    return assemble(ups, downs), arrivals


def assemble_kernel(count, halves, place_ref, *refs):
    out, sems = refs[-2], refs[-1]
    place = place_ref[0]
    rows = out.shape[0] // (count * halves)
    stride = 2 * count - 1

    def each(action):
        for h in range(halves):
            mine = refs[h * stride : (h + 1) * stride]
            for j in range(count):
                target = out.at[pl.ds((j * halves + h) * rows, rows), :]
                for s in range(-(count - 1), count):
                    source = mine[s + count - 1]

                    @pl.when(place - j == s)
                    def _(source=source, target=target, h=h, j=j):
                        action(pltpu.make_async_copy(source, target, sems.at[h * count + j]))

    each(lambda copy: copy.start())
    each(lambda copy: copy.wait())


def assemble(ups, downs):
    count, halves = len(ups[0]), len(ups)
    rows, dim = ups[0][0].shape
    flat = []
    for up, down in zip(ups, downs):
        flat += down[:0:-1] + up
    anywhere = pl.BlockSpec(memory_space=pl.ANY)
    return pl.pallas_call(
        functools.partial(assemble_kernel, count, halves),
        in_specs=[pl.BlockSpec(memory_space=pltpu.SMEM)] + [anywhere] * len(flat),
        out_specs=pl.BlockSpec(memory_space=pltpu.VMEM),
        out_shape=jax.ShapeDtypeStruct((count * halves * rows, dim), ups[0][0].dtype),
        scratch_shapes=[pltpu.SemaphoreType.DMA((count * halves,))],
        cost_estimate=cost(1, 4 * count * halves * rows * dim),
        name="assemble",
    )(lax.axis_index("tp").astype(jnp.int32).reshape(1), *flat)


def line_scatter(parts, gates=None):
    count = lax.axis_size("tp")
    gates = gates or {}
    up = down = None
    arrivals, sends = [()], [()]
    for s in range(count - 1, 0, -1):
        send_up, send_down = parts[s].astype(F32), parts[count - s].astype(F32)
        if up is not None:
            send_up, send_down = send_up + up.astype(F32), send_down + down.astype(F32)
        step = count - s
        send_up, send_down = send_up.astype(BF), send_down.astype(BF)
        send_up, send_down = lax.optimization_barrier((send_up, send_down, *gates.get(step, ())))[:2]
        sends.append((send_up, send_down))
        up = lax.ppermute(send_up, "tp", [(i, i + 1) for i in range(count - s)])
        down = lax.ppermute(send_down, "tp", [(i + 1, i) for i in range(s - 1, count - 1)])
        arrivals.append((up, down))
    return parts[0].astype(F32) + up.astype(F32) + down.astype(F32), arrivals, sends


def total_fsdp(value):
    count = lax.axis_size("fsdp")
    bit = 1
    while bit < count:
        value = value + lax.ppermute(value, "fsdp", [(i, i ^ bit) for i in range(count)])
        bit *= 2
    return value


def total_tp(value):
    count = lax.axis_size("tp")
    out = flat = lax.optimization_barrier(value.reshape(-1, 128))
    for s in range(1, count):
        out = out + lax.ppermute(flat, "tp", [(i, (i + s) % count) for i in range(count)])
    return lax.optimization_barrier(out).reshape(value.shape)


def shares(value):
    count = lax.axis_size("tp")
    place = lax.axis_index("tp")
    rows = value.shape[0] // count
    return [lax.dynamic_slice_in_dim(value, ((place + d) % count) * rows, rows, 0) for d in range(count)]


def keep_kernel(pos_ref, keep_ref):
    pos = pos_ref[...]
    bound = jnp.zeros((1, pos.shape[1]), jnp.int32)
    for b in range(13, -1, -1):
        trial = bound + (1 << b)
        count = jnp.sum((pos <= trial).astype(F32), axis=0, keepdims=True)
        bound = jnp.where(count <= CAP, trial, bound)
    keep_ref[...] = (pos <= bound).astype(F32)


def kept_pairs(routes, order_row, experts):
    pairs = order_row.shape[0]
    tokens = routes.shape[0]
    step = jnp.arange(pairs, dtype=jnp.int32)
    high = (order_row[:, None] // 128 == jnp.arange(pairs // 128, dtype=jnp.int32)[None, :]).astype(BF)
    low = (order_row[:, None] % 128 == jnp.arange(128, dtype=jnp.int32)[None, :]).astype(BF)
    step_high = (step // 64).astype(BF)[:, None]
    step_low = (step % 64).astype(BF)[:, None]
    table = 64.0 * dot(high * step_high, low, TN) + dot(high * step_low, low, TN)
    place = table.astype(jnp.int32).reshape(tokens, -1) + 1
    hot = routes[:, :, None] == jnp.arange(experts, dtype=jnp.int32)[None, None, :]
    pos = jnp.sum(jnp.where(hot, place[:, :, None], 0), axis=1)
    pos = jnp.where(pos == 0, 1 << 20, pos)
    return pl.pallas_call(
        keep_kernel, out_shape=jax.ShapeDtypeStruct((tokens, experts), F32), name="keep"
    )(pos)


def turn_kernel(q_ref, k_ref, norm_ref, cos_ref, sin_ref, gain_ref, q_out, k_out):
    cos, sin = cos_ref[...], sin_ref[...]
    for slot, (raw, out) in enumerate(((q_ref, q_out), (k_ref, k_out))):
        x = raw[...] * norm_ref[:, slot : slot + 1] * gain_ref[slot]
        out[...] = (x * cos + pltpu.roll(x, HEAD_DIM // 2, 1) * sin).astype(BF)


def turn(raw, norms, cos, sin, gains):
    rows = raw.shape[0]
    heads = raw.shape[1] // (3 * HEAD_DIM)
    part = lambda j: pl.BlockSpec((rows, HEAD_DIM), lambda h: (0, j * heads + h))
    whole = lambda shape: pl.BlockSpec(shape, lambda h: (0,) * len(shape))
    return pl.pallas_call(
        turn_kernel,
        grid=(heads,),
        in_specs=[
            part(0),
            part(1),
            whole(norms.shape),
            whole(cos.shape),
            whole(sin.shape),
            pl.BlockSpec((2, 1, HEAD_DIM), lambda h: (0, 0, h)),
        ],
        out_specs=[part(0)] * 2,
        out_shape=[jax.ShapeDtypeStruct((rows, heads * HEAD_DIM), BF)] * 2,
        compiler_params=params(),
        cost_estimate=cost(10 * raw.size, 6 * raw.size),
        name="turn",
    )(raw, raw, norms, cos, sin, gains)


def turn_back_kernel(
    dq_ref, dk_ref, dkr_ref, q_ref, k_ref, norm_ref, cos_ref, sin_ref, gain_ref, uq_out, uk_out, dots_out, part_out
):
    cos, sin = cos_ref[...], sin_ref[...]
    grads = (dq_ref[...], dk_ref[...] + dkr_ref[...].astype(F32))
    lane = lax.broadcasted_iota(jnp.int32, dots_out.shape, 1)

    @pl.when(pl.program_id(0) == 0)
    def _():
        dots_out[...] = jnp.zeros_like(dots_out)

    for slot, (grad, raw, out) in enumerate(zip(grads, (q_ref, k_ref), (uq_out, uk_out))):
        back = grad * cos - pltpu.roll(grad, HEAD_DIM // 2, 1) * sin
        x = raw[...]
        part_out[slot] = jnp.sum(back * x * norm_ref[:, slot : slot + 1], axis=0, keepdims=True)
        u = back * gain_ref[slot]
        out[...] = u
        dots_out[...] += jnp.where(lane == slot, jnp.sum(u * x, axis=1, keepdims=True), 0.0)


def turn_back(dq, dk, dk_more, raw, norms, cos, sin, gains):
    rows = raw.shape[0]
    heads = raw.shape[1] // (3 * HEAD_DIM)
    part = lambda j: pl.BlockSpec((rows, HEAD_DIM), lambda h: (0, j * heads + h))
    whole = lambda shape: pl.BlockSpec(shape, lambda h: (0,) * len(shape))
    gain_spec = pl.BlockSpec((2, 1, HEAD_DIM), lambda h: (0, 0, h))
    wide = jax.ShapeDtypeStruct((rows, heads * HEAD_DIM), F32)
    return pl.pallas_call(
        turn_back_kernel,
        grid=(heads,),
        in_specs=[
            part(0),
            part(0),
            part(0),
            part(0),
            part(1),
            whole(norms.shape),
            whole(cos.shape),
            whole(sin.shape),
            gain_spec,
        ],
        out_specs=[part(0), part(0), whole((rows, 2)), gain_spec],
        out_shape=[
            wide,
            wide,
            jax.ShapeDtypeStruct((rows, 2), F32),
            jax.ShapeDtypeStruct((2, 1, heads * HEAD_DIM), F32),
        ],
        compiler_params=params(),
        cost_estimate=cost(10 * raw.size, 8 * raw.size),
        name="turn_back",
    )(dq, dk, dk_more, raw, raw, norms, cos, sin, gains)


def own_mask(seg_col, seg_row, first_row, row_count, first_key, key_count):
    rows = lax.broadcasted_iota(jnp.int32, (row_count, key_count), 0) + first_row
    keys = lax.broadcasted_iota(jnp.int32, (row_count, key_count), 1) + first_key
    same = seg_col[first_row : first_row + row_count, :] == seg_row[:, first_key : first_key + key_count]
    return same & (keys <= rows)


SCALE = HEAD_DIM ** (-0.5)


def tile_probs(q_tile, k_ref, seg_col, seg_row, first_row, first_key, keys, kr):
    own = dot(q_tile, k_ref[first_key : first_key + keys, :], NT)
    own = jnp.where(own_mask(seg_col, seg_row, first_row, QT, first_key, keys), own, NEG)
    peak = jnp.max(own, axis=1, keepdims=True)
    far = None
    if kr is not None:
        far = dot(q_tile, kr[...], NT)
        peak = jnp.maximum(peak, jnp.max(far, axis=1, keepdims=True))
        far = jnp.exp((far - peak) * SCALE)
    own = jnp.exp((own - peak) * SCALE)
    total = jnp.sum(own, axis=1, keepdims=True)
    if far is not None:
        total = total + jnp.sum(far, axis=1, keepdims=True)
    inverse = 1.0 / total
    return own * inverse, (None if far is None else far * inverse)


def attend_kernel(cont_ref, q_ref, k_ref, v_ref, kr_ref, vr_ref, col_ref, row_ref, out_ref):
    rows = q_ref.shape[0]

    def run(far):
        for first in range(0, rows, QT):
            start = max(0, first - QT) if far else 0
            keys = first + QT - start
            own, other = tile_probs(
                q_ref[first : first + QT, :], k_ref, col_ref, row_ref, first, start, keys, kr_ref if far else None
            )
            out = dot(own.astype(BF), v_ref[start : start + keys, :])
            if far:
                out = out + dot(other.astype(BF), vr_ref[...])
            out_ref[first : first + QT, :] = out.astype(BF)

    pl.when(cont_ref[0] == 0)(lambda: run(False))
    pl.when(cont_ref[0] != 0)(lambda: run(True))


def attend_specs(rows, count):
    head = pl.BlockSpec((rows, HEAD_DIM), lambda h, c: (0, h))
    return [head] * count + [
        pl.BlockSpec((rows, 1), lambda h, c: (0, 0)),
        pl.BlockSpec((1, rows), lambda h, c: (0, 0)),
    ], head


def attend(cont, q, k, v, kr, vr, seg_col, seg_row):
    rows, width = q.shape
    specs, head = attend_specs(rows, 5)
    return pl.pallas_call(
        attend_kernel,
        grid_spec=pltpu.PrefetchScalarGridSpec(
            num_scalar_prefetch=1, grid=(width // HEAD_DIM,), in_specs=specs, out_specs=head
        ),
        out_shape=jax.ShapeDtypeStruct((rows, width), BF),
        compiler_params=params(),
        cost_estimate=cost(6 * rows * rows * width, 12 * rows * width, rows * rows * 6),
        name="attend",
    )(cont, q, k, v, kr, vr, seg_col, seg_row)


def attend_back_kernel(
    cont_ref, q_ref, k_ref, v_ref, kr_ref, vr_ref, do_ref, col_ref, row_ref, dq_ref, dk_ref, dv_ref, dkr_ref, dvr_ref, far_dk, far_dv
):
    rows = q_ref.shape[0]
    dk_ref[...] = jnp.zeros_like(dk_ref)
    dv_ref[...] = jnp.zeros_like(dv_ref)

    def run(far):
        if far:
            far_dk[...] = jnp.zeros_like(far_dk)
            far_dv[...] = jnp.zeros_like(far_dv)
        for first in range(0, rows, QT):
            start = max(0, first - QT) if far else 0
            keys = first + QT - start
            here = slice(start, start + keys)
            q_tile = q_ref[first : first + QT, :]
            do_tile = do_ref[first : first + QT, :]
            own, other = tile_probs(q_tile, k_ref, col_ref, row_ref, first, start, keys, kr_ref if far else None)
            grad = dot(do_tile, v_ref[here, :], NT)
            mean = jnp.sum(own * grad, axis=1, keepdims=True)
            if far:
                grad_far = dot(do_tile, vr_ref[...], NT)
                mean = mean + jnp.sum(other * grad_far, axis=1, keepdims=True)
            slope = (own * (grad - mean)).astype(BF)
            dq = dot(slope, k_ref[here, :])
            dk_ref[here, :] += dot(slope, q_tile, TN) * SCALE
            dv_ref[here, :] += dot(own.astype(BF), do_tile, TN)
            if far:
                slope = (other * (grad_far - mean)).astype(BF)
                dq = dq + dot(slope, kr_ref[...])
                far_dk[...] += dot(slope, q_tile, TN) * SCALE
                far_dv[...] += dot(other.astype(BF), do_tile, TN)
            dq_ref[first : first + QT, :] = dq * SCALE
        if far:
            dkr_ref[...] = far_dk[...].astype(BF)
            dvr_ref[...] = far_dv[...].astype(BF)
        else:
            dkr_ref[...] = jnp.zeros_like(dkr_ref)
            dvr_ref[...] = jnp.zeros_like(dvr_ref)

    pl.when(cont_ref[0] == 0)(lambda: run(False))
    pl.when(cont_ref[0] != 0)(lambda: run(True))


def attend_back(cont, q, k, v, kr, vr, do, seg_col, seg_row):
    rows, width = q.shape
    specs, head = attend_specs(rows, 6)
    wide = jax.ShapeDtypeStruct((rows, width), F32)
    low = jax.ShapeDtypeStruct((rows, width), BF)
    return pl.pallas_call(
        attend_back_kernel,
        grid_spec=pltpu.PrefetchScalarGridSpec(
            num_scalar_prefetch=1,
            grid=(width // HEAD_DIM,),
            in_specs=specs,
            out_specs=[head] * 5,
            scratch_shapes=[pltpu.VMEM((rows, HEAD_DIM), F32)] * 2,
        ),
        out_shape=[wide, wide, wide, low, low],
        compiler_params=params(),
        cost_estimate=cost(15 * rows * rows * width, 30 * rows * width, rows * rows * 6),
        name="attend_back",
    )(cont, q, k, v, kr, vr, do, seg_col, seg_row)


def hidden_kernel(x_ref, c_ref, g_ref, u_ref, d_ref, w_ref, act_out, dg_out, du_out, s_out):
    expert = pl.program_id(0)
    gate = dot(x_ref[...], g_ref[...])
    up = dot(x_ref[...], u_ref[...])
    back = dot(c_ref[...], d_ref[...])
    lane = lax.broadcasted_iota(jnp.int32, s_out.shape, 1)
    weight = jnp.sum(jnp.where(lane == expert, w_ref[...], 0.0), axis=1, keepdims=True)
    sig = 1.0 / (1.0 + jnp.exp(-gate))
    swish = gate * sig
    act = swish * up
    act_out[...] = (act * weight).astype(BF)
    s = jnp.sum(act * back, axis=1, keepdims=True)
    back = back * weight
    dg_out[...] = (back * up * (sig + swish * (1.0 - sig))).astype(BF)
    du_out[...] = (back * swish).astype(BF)

    @pl.when(expert == 0)
    def _():
        s_out[...] = jnp.zeros_like(s_out)

    s_out[...] = jnp.where(lane == expert, s, s_out[...])


def hidden(x, c, mats, low_mat, weight, block, held=None):
    rows, dim = x.shape
    experts = weight.shape[1]
    span = low_mat.shape[1] // experts
    full = pl.BlockSpec((rows, dim), lambda e: (0, 0))
    mat = lambda j: pl.BlockSpec((dim, span), lambda e: (0, j * experts + e))
    out = pl.BlockSpec((rows, span), lambda e: (block, e))
    wide = jax.ShapeDtypeStruct((2 * rows, experts * span), BF)
    wider = jax.ShapeDtypeStruct((2 * rows, experts * span + 128), BF)
    held = [] if held is None else list(held)
    kernel = hidden_kernel if not held else lambda *refs: hidden_kernel(*refs[:6], *refs[9:])
    return pl.pallas_call(
        kernel,
        grid=(experts,),
        in_specs=[full, full, mat(0), mat(1), mat(0), pl.BlockSpec((rows, experts), lambda e: (0, 0))]
        + [pl.BlockSpec(memory_space=pl.ANY)] * len(held),
        out_specs=[out, out, out, pl.BlockSpec((rows, experts), lambda e: (0, 0))],
        out_shape=[wide, wider, wide, jax.ShapeDtypeStruct((rows, experts), F32)],
        input_output_aliases={6: 0, 7: 1, 8: 2} if held else {},
        compiler_params=params(),
        cost_estimate=cost(6 * rows * dim * experts * span, 2 * (2 * rows * dim + 6 * dim * experts * span)),
        name="hidden",
    )(x, c, mats, mats, low_mat, weight, *held)


def mix_kernel(*refs):
    count = (len(refs) - 1) // 2
    total = None
    for j in range(count):
        term = dot(refs[2 * j][...], refs[2 * j + 1][...], NT)
        total = term if total is None else total + term
    refs[-1][...] = total.astype(refs[-1].dtype)


def mix(pairs, dtype, rows, tile=512):
    cols = pairs[0][1].shape[0]
    specs, flat, flops, nbytes = [], [], 0, 0
    for a, b, j, k in pairs:
        deep = min(a.shape[1], b.shape[1], b.shape[0])
        specs += [
            pl.BlockSpec((rows, deep), lambda i, k=k: (k, 0)),
            pl.BlockSpec((tile, deep), lambda i, j=j: (i, j)),
        ]
        flat += [a, b]
        flops += 2 * rows * cols * deep
        nbytes += 2 * deep * (rows + cols)
    return pl.pallas_call(
        mix_kernel,
        grid=(cols // tile,),
        in_specs=specs,
        out_specs=pl.BlockSpec((rows, tile), lambda i: (0, i)),
        out_shape=jax.ShapeDtypeStruct((rows, cols), dtype),
        compiler_params=params(),
        cost_estimate=cost(flops, nbytes + 4 * rows * cols),
        name="mix",
    )(*flat)


def attn_pack_kernel(experts, q_ref, k_ref, v_ref, o_ref, r_ref, gain_ref, out_ref):
    cols = q_ref.shape[1]
    for j, ref in enumerate((q_ref, k_ref, v_ref)):
        out_ref[:, j * cols : (j + 1) * cols] = (ref[...].astype(F32) * gain_ref[:, 0:1]).astype(BF)
    out_ref[:, 3 * cols : 4 * cols] = o_ref[...].astype(F32).T.astype(BF)
    rest = r_ref[...].astype(F32)
    lane = lax.broadcasted_iota(jnp.int32, rest.shape, 1)
    out_ref[:, 4 * cols :] = jnp.where(lane < experts, rest * gain_ref[:, 1:2], rest).astype(BF)


def attn_pack(q, k, v, o, r, gains, experts):
    return pl.pallas_call(
        functools.partial(attn_pack_kernel, experts),
        out_shape=jax.ShapeDtypeStruct((q.shape[0], 4 * q.shape[1] + r.shape[1]), BF),
        cost_estimate=cost(1, 4 << 20),
        name="attn_pack",
    )(q, k, v, o, r, gains)


PACK = 4


def moe_pack_kernel(core_ref, g_ref, u_ref, d_ref, gain_ref, g_out, u_out, d_out):
    gain = gain_ref[:, 1:2]
    span = g_ref.shape[2]
    for i in range(PACK):
        here = slice(i * span, (i + 1) * span)
        g_out[0, :, here] = (g_ref[i].astype(F32) * gain).astype(BF)
        u_out[0, :, here] = (u_ref[i].astype(F32) * gain).astype(BF)
        d_out[0, :, here] = d_ref[i].astype(F32).T.astype(BF)


def moe_pack(core, gate, up, down, gains):
    experts, piece, span = gate.shape
    local = experts // 2
    steps = local // PACK
    block = pl.BlockSpec((PACK, piece, span), lambda e, c: (e, 0, 0))
    out = pl.BlockSpec((1, piece, PACK * span), lambda e, c: ((e // steps) ^ c[0], 0, e % steps))
    return pl.pallas_call(
        moe_pack_kernel,
        grid_spec=pltpu.PrefetchScalarGridSpec(
            num_scalar_prefetch=1,
            grid=(experts // PACK,),
            in_specs=[
                block,
                block,
                pl.BlockSpec((PACK, span, piece), lambda e, c: (e, 0, 0)),
                pl.BlockSpec(gains.shape, lambda e, c: (0, 0)),
            ],
            out_specs=[out] * 3,
        ),
        out_shape=[jax.ShapeDtypeStruct((2, piece, local * span), BF)] * 3,
        compiler_params=params(),
        cost_estimate=cost(1, 12 * gate.size),
        name="moe_pack",
    )(core, gate, up, down, gains)


def moe_unpack_kernel(core_ref, *refs):
    mine, theirs, gain_ref, outs = refs[:3], refs[3:6], refs[6], refs[7:]
    steps = pl.num_programs(0) // 2
    here = pl.program_id(0) // steps == core_ref[0]
    gain = gain_ref[:, 1:2]
    span = outs[0].shape[2]
    for i in range(PACK):
        part = slice(i * span, (i + 1) * span)
        g, u, d = (jnp.where(here, a[:, part], b[:, part]).astype(F32) for a, b in zip(mine, theirs))
        outs[0][i] = g * gain
        outs[1][i] = u * gain
        outs[2][i] = d.T


def moe_unpack(core, mine, theirs, gains, experts, local):
    piece = mine[0].shape[0]
    span = mine[1].shape[1] // local
    steps = local // PACK
    block = pl.BlockSpec((piece, PACK * span), lambda e, c: (0, e % steps))
    wide = pl.BlockSpec((PACK, piece, span), lambda e, c: (e, 0, 0))
    return pl.pallas_call(
        moe_unpack_kernel,
        grid_spec=pltpu.PrefetchScalarGridSpec(
            num_scalar_prefetch=1,
            grid=(experts // PACK,),
            in_specs=[block] * 6 + [pl.BlockSpec(gains.shape, lambda e, c: (0, 0))],
            out_specs=[wide, wide, pl.BlockSpec((PACK, span, piece), lambda e, c: (e, 0, 0))],
        ),
        out_shape=[
            jax.ShapeDtypeStruct((experts, piece, span), F32),
            jax.ShapeDtypeStruct((experts, piece, span), F32),
            jax.ShapeDtypeStruct((experts, span, piece), F32),
        ],
        compiler_params=params(),
        cost_estimate=cost(1, 24 * experts * piece * span),
        name="moe_unpack",
    )(core, *mine, *theirs, gains)


def angles(seg_block):
    row_count = seg_block.shape[0]
    labels = jnp.arange(CONTS + 1, dtype=jnp.int32)
    member = (seg_block[:, None] == labels[None, :]).astype(jnp.int32)
    counts = jnp.sum(member, axis=0)
    starts = jnp.sum(jnp.where(labels[:, None] > labels[None, :], counts[None, :], 0), axis=1)
    seg_start = jnp.sum(member * starts[None, :], axis=1)
    offset = row_count * (seg_block != 0).astype(jnp.int32)
    places = jnp.arange(row_count, dtype=jnp.int32) - seg_start + offset
    half = HEAD_DIM // 2
    column = jnp.arange(HEAD_DIM, dtype=jnp.int32)
    frequency = jnp.exp((column % half).astype(F32) * (-2.0 * math.log(10000.0) / HEAD_DIM))
    angle = places.astype(F32)[:, None] * frequency[None, :]
    sign = jnp.where(column < half, -1.0, 1.0).astype(F32)
    return jnp.cos(angle), jnp.sin(angle) * sign[None, :]


def inverse_norm(values):
    return lax.rsqrt(jnp.mean(values * values, axis=-1, keepdims=True) + EPS)


def on_device(
    residual,
    query_weight,
    key_weight,
    value_weight,
    out_weight,
    query_gain,
    key_gain,
    attn_gain,
    mlp_gain,
    router_weight,
    gate_weight,
    up_weight,
    down_weight,
    routes,
    route_order,
    seg_ids,
    cotangent,
):
    fsdp, tp = lax.axis_size("fsdp"), lax.axis_size("tp")
    place = lax.axis_index("fsdp")
    core = place % 2
    core_arg = core.astype(jnp.int32).reshape(1)
    dim = residual.shape[1]
    piece = dim // fsdp
    tokens = seg_ids.shape[0]
    share = tokens // tp
    experts, _, span = gate_weight.shape
    local = experts // 2
    cols = query_weight.shape[1]
    heads = cols // HEAD_DIM
    groups = chip_groups()

    norm_gains = jnp.stack([attn_gain, mlp_gain], axis=1).astype(F32)

    stream = residual.astype(F32)
    norm_first = inverse_norm(stream)
    hat_one = stream * norm_first
    hat_low = hat_one.astype(BF)
    normed, steps_one = line_gather(hat_low)

    narrow = HEAD_DIM // fsdp
    gain_col = jnp.stack([query_gain, key_gain]).reshape(-1, 1)
    gain_col = jnp.pad(gain_col, ((0, piece - gain_col.shape[0]), (0, 127 - experts)))
    attn_mat = lax.all_gather(
        attn_pack(
            after(query_weight, hat_low),
            key_weight,
            value_weight,
            out_weight,
            jnp.concatenate([router_weight, gain_col], axis=1),
            norm_gains,
            experts,
        ),
        "fsdp",
        axis=0,
        tiled=True,
    )
    qkv_mat = attn_mat[:, : 3 * cols]
    out_mat = attn_mat[:, 3 * cols : 4 * cols]
    router_mat = attn_mat[:, 4 * cols :]
    gains = router_mat[:, experts].astype(F32).reshape(fsdp, piece)[:, : 2 * heads * narrow]
    gains = gains.reshape(fsdp, 2, heads, narrow).transpose(1, 2, 0, 3).reshape(2, 1, cols)
    lane = jnp.arange(128, dtype=jnp.int32)[None, :]
    router_mat = jnp.where(lane < experts, router_mat, 0)

    packs = moe_pack(core_arg, after(gate_weight, hat_low), up_weight, down_weight, norm_gains)

    def both_rows(kept, given):
        got = swap_core(given)
        return jnp.concatenate([jnp.where(core == 0, kept, got), jnp.where(core == 0, got, kept)], axis=0)

    def over_chips(value):
        return lax.all_gather(value, "fsdp", axis=0, tiled=True, axis_index_groups=groups)

    low_rows = both_rows(packs[2][0], packs[2][1])
    low_mat = over_chips(after(low_rows, attn_mat, *steps_one[2]))
    rows = both_rows(*[jnp.concatenate([packs[0][h], packs[1][h]], axis=1) for h in range(2)])

    raw = dot(normed, qkv_mat)
    half = fsdp // 2
    forth = [(i, i + half) for i in range(half)]
    value_low = raw[:, 2 * cols :].astype(BF)
    value_far = lax.ppermute(value_low, "fsdp", forth)
    query_key = after(raw, value_low)
    totals = jnp.stack(
        [jnp.sum(query_key[:, :cols] ** 2, axis=1), jnp.sum(query_key[:, cols : 2 * cols] ** 2, axis=1)]
    )
    totals = total_tp(totals)
    norms = lax.rsqrt(totals / dim + EPS).T
    upstream, steps_up = line_gather(cotangent, gates={1: [norms]})
    cos, sin = angles(seg_ids)
    query_rot, key_rot = turn(raw, norms, cos, sin, gains)
    key_far = lax.ppermute(key_rot, "fsdp", forth)
    cont = (place >= half).astype(jnp.int32).reshape(1)
    seg_col, seg_row = seg_ids[:, None], seg_ids[None, :]
    mats = over_chips(after(rows, key_far, value_far, *steps_up[3]))

    upstream_far = swap_core(upstream)

    attended = attend(
        cont, after(query_rot, *steps_up[1]), key_rot, value_low, key_far, value_far, seg_col, seg_row
    )
    attn_part = dot(attended, out_mat, NT).astype(BF)
    attn_out, _, _ = line_scatter(shares(attn_part), {1: steps_up[3]})
    after_attn = stream + attn_out
    norm_second = inverse_norm(after_attn)
    hat_two = after_attn * norm_second

    keep = kept_pairs(routes, route_order[0], experts)
    keep_far = swap_core(keep)
    wide_c = jnp.concatenate([upstream, upstream_far], axis=0)
    mlp_own, _ = line_gather(hat_two.astype(BF), gates={2: [keep_far], 3: [wide_c]})
    mlp_far = swap_core(mlp_own)

    def routed(x, kept):
        logits = dot(x, router_mat)[:, :experts]
        grown = jnp.exp(logits - jnp.max(logits, axis=-1, keepdims=True))
        probs = grown / jnp.sum(grown, axis=-1, keepdims=True)
        return probs, lax.dynamic_slice_in_dim(probs * kept, core * local, local, 1)

    def logits_back(s, kept, probs):
        zero = jnp.zeros_like(s)
        pair = kept * jnp.where(core == 0, jnp.concatenate([s, zero], 1), jnp.concatenate([zero, s], 1))
        grad = probs * (pair - jnp.sum(probs * pair, axis=-1, keepdims=True))
        return jnp.pad(grad, ((0, 0), (0, 128 - experts))).astype(BF)

    probs_own, weight_own = routed(mlp_own, keep)
    *held, s_own = hidden(mlp_own, upstream, mats, low_mat, weight_own, 0)
    probs_far, weight_far = routed(mlp_far, keep_far)
    act, dg, du, s_far = hidden(mlp_far, upstream_far, mats, low_mat, weight_far, 1, held)
    gl_own = logits_back(s_own, keep, probs_own)
    gl_far = logits_back(s_far, keep_far, probs_far)

    def both_cores(own, got):
        return [a.astype(F32) + b.astype(F32) for a, b in zip(shares(own), shares(got))]

    def scattered(value):
        return lax.psum_scatter(value, "fsdp", scatter_dimension=0, tiled=True, axis_index_groups=groups)

    dg = lax.dynamic_update_slice(dg, jnp.concatenate([gl_own, gl_far], axis=0), (0, local * span))
    wide_x = jnp.concatenate([mlp_own, mlp_far], axis=0)
    down_term = dot(wide_c, act, TN).astype(BF)
    down_sum = scattered(down_term)

    gl_far = after(gl_far, down_term)
    back_far = mix([(dg, mats, 0, 1), (du, mats, 1, 1), (gl_far, router_mat, 0, 0)], BF, tokens)
    back_got = swap_core(back_far)
    gl_own = after(gl_own, back_far)
    back_own = mix([(dg, mats, 0, 0), (du, mats, 1, 0), (gl_own, router_mat, 0, 0)], BF, tokens)
    grad_scaled, _, back_sends = line_scatter(both_cores(back_own, back_got), {2: [down_sum]})
    gate_term = dot(wide_x, after(dg, back_own, back_got), TN).astype(BF)
    gate_sum = scattered(gate_term)
    up_term = dot(wide_x, after(du, gate_term, *back_sends[2]), TN).astype(BF)
    up_sum = scattered(up_term)
    sums = [gate_sum, up_sum, down_sum]

    grad_after = cotangent.astype(F32) + norm_second * (
        grad_scaled - hat_two * jnp.mean(grad_scaled * hat_two, axis=-1, keepdims=True)
    )
    grad_after_low = after(grad_after.astype(BF), up_term)
    grad_attn, _ = line_gather(grad_after_low, gates={2: [gate_sum]})

    act = after(act, back_own, *back_sends[1])
    out_far = mix([(act, low_mat, 0, 1)], BF, tokens)
    out_got = swap_core(out_far)
    out_own = mix([(act, low_mat, 0, 0)], BF, tokens)
    out_low = (out_own.astype(F32) + out_got.astype(F32)).astype(BF)
    out_total = lax.psum_scatter(after(out_low, up_sum, grad_attn), "tp", scatter_dimension=0, tiled=True)
    block_out = after_attn + out_total.astype(F32)

    grad_attended = after(dot(grad_attn, out_mat).astype(BF), out_low)
    dq, dk, dv, dk_far, dv_far = attend_back(
        cont, query_rot, key_rot, value_low, key_far, value_far, grad_attended, seg_col, seg_row
    )
    back_pairs = [(i + half, i) for i in range(half)]
    dk_got, dv_got = lax.ppermute(dk_far, "fsdp", back_pairs), lax.ppermute(dv_far, "fsdp", back_pairs)

    sums = [after(t, dk_far) for t in sums]
    mine = [lax.dynamic_slice_in_dim(t, core * piece, piece, 0) for t in sums]
    theirs = [swap_core(lax.dynamic_slice_in_dim(t, (1 - core) * piece, piece, 0)) for t in sums]
    grad_gate, grad_up, grad_down = moe_unpack(core_arg, mine, theirs, norm_gains, experts, local)
    router_hat = total_tp(sum(t[0][:, local * span : local * span + experts].astype(F32) for t in (mine, theirs)))
    grad_router = router_hat * norm_gains[:, 1:2]
    gain_term = jnp.sum(gate_weight.astype(F32) * grad_gate + up_weight.astype(F32) * grad_up, axis=(0, 2))
    u_query, u_key, dots, gain_parts = turn_back(
        dq, after(dk, sums[1], grad_gate, grad_up, grad_down), dk_got, raw, norms, cos, sin, gains
    )
    dots = total_tp(dots.T).T
    grad_value = (dv + dv_got.astype(F32)).astype(BF)

    def raw_back(u, x, j):
        n = norms[:, j : j + 1]
        return (n * u - x * (n * n * n * dots[:, j : j + 1] / dim)).astype(BF)

    grad_raw = jnp.concatenate(
        [raw_back(u_query, raw[:, :cols], 0), raw_back(u_key, raw[:, cols : 2 * cols], 1), grad_value], axis=1
    )
    normed_part = dot(after(grad_raw, out_total), qkv_mat, NT).astype(BF)
    small = gain_parts.reshape(2, heads, fsdp, narrow).transpose(2, 0, 1, 3).reshape(fsdp, -1)
    small = total_fsdp(small)
    grad_raw_later = after(grad_raw, normed_part)
    qkv_term = dot(normed, grad_raw_later, TN).astype(BF)
    grad_hat, _, last_sends = line_scatter(shares(normed_part), {3: [router_hat, gain_term, small]})


    def summed(value):
        return lax.psum_scatter(value, "fsdp", scatter_dimension=0, tiled=True).astype(F32)

    grad_out_proj = summed(dot(grad_attn, after(attended, dk_far), TN).astype(BF)).T
    attn_sum = summed(qkv_term)
    qkv_hat = [attn_sum[:, j * cols : (j + 1) * cols] for j in range(3)]
    qkv_grad = [norm_gains[:, 0:1] * t for t in qkv_hat]
    small = lax.dynamic_index_in_dim(small, place, 0, keepdims=False)
    small = small.reshape(2, heads, narrow)

    attn_dots = sum(jnp.sum(w.astype(F32) * t, axis=1) for w, t in zip((query_weight, key_weight, value_weight), qkv_hat))
    both_dots = total_tp(jnp.stack([attn_dots, gain_term / norm_gains[:, 1]]))
    grad_attn_gain = both_dots[0]
    grad_mlp_gain = both_dots[1] + jnp.sum(router_weight.astype(F32) * router_hat, axis=1)
    grad_hat = after(grad_hat, both_dots, grad_out_proj, *qkv_grad)
    grad_input = grad_after + norm_first * (grad_hat - hat_one * jnp.mean(grad_hat * hat_one, axis=-1, keepdims=True))
    return (
        block_out,
        grad_input,
        qkv_grad[0],
        qkv_grad[1],
        qkv_grad[2],
        grad_out_proj,
        small[0],
        small[1],
        grad_attn_gain,
        grad_mlp_gain,
        grad_router,
        grad_gate,
        grad_up,
        grad_down,
    )


def solution(mesh):
    rows = P(("fsdp", "tp"), None)
    in_specs = (
        rows,
        P("fsdp", "tp"),
        P("fsdp", "tp"),
        P("fsdp", "tp"),
        P("tp", "fsdp"),
        P("tp", "fsdp"),
        P("tp", "fsdp"),
        P("fsdp"),
        P("fsdp"),
        P("fsdp", None),
        P(None, "fsdp", "tp"),
        P(None, "fsdp", "tp"),
        P(None, "tp", "fsdp"),
        P("fsdp", None),
        P("fsdp", None),
        P("fsdp"),
        rows,
    )
    out_specs = (
        rows,
        rows,
        P("fsdp", "tp"),
        P("fsdp", "tp"),
        P("fsdp", "tp"),
        P("tp", "fsdp"),
        P("tp", "fsdp"),
        P("tp", "fsdp"),
        P("fsdp"),
        P("fsdp"),
        P("fsdp", None),
        P(None, "fsdp", "tp"),
        P(None, "fsdp", "tp"),
        P(None, "tp", "fsdp"),
    )
    return jax.shard_map(on_device, mesh=mesh, in_specs=in_specs, out_specs=out_specs, check_vma=False)
```

```python
import functools
import math

import jax
import jax.numpy as jnp
from jax import lax
from jax.experimental import pallas as pl
from jax.experimental.pallas import tpu as pltpu
from jax.sharding import PartitionSpec as P

HEAD_DIM = 128
CONTS = 8
CAP = 512
EPS = 1e-05
NEG = -1e30
QT = 256
BF = jnp.bfloat16
F32 = jnp.float32
NT = (((1,), (1,)), ((), ()))
TN = (((0,), (0,)), ((), ()))


def dot(a, b, dims=(((1,), (0,)), ((), ()))):
    return lax.dot_general(a, b, dims, preferred_element_type=F32)


def params(count=1):
    return pltpu.CompilerParams(
        dimension_semantics=("arbitrary",) * count, vmem_limit_bytes=56 << 20
    )


def cost(flops, nbytes, trans=0):
    return pl.CostEstimate(flops=int(flops), bytes_accessed=int(nbytes), transcendentals=int(trans))


def swap_core(value):
    count = lax.axis_size("fsdp")
    return lax.ppermute(value, "fsdp", [(i, i ^ 1) for i in range(count)])


def chip_groups():
    count = lax.axis_size("fsdp")
    return [list(range(c, count, 2)) for c in range(2)]


def after(value, *others):
    return lax.optimization_barrier((value,) + others)[0]


def line_gather(value, halves=2, gates=None):
    count = lax.axis_size("tp")
    gates = gates or {}
    rows = value.shape[0] // halves
    ups = [[value[h * rows : (h + 1) * rows]] for h in range(halves)]
    downs = [[u[0]] for u in ups]
    for s in range(1, count):
        for up, down in zip(ups, downs):
            ahead, behind = up[-1], down[-1]
            if s > 1 or s in gates:
                ahead, behind = lax.optimization_barrier((ahead, behind, *gates.get(s, ())))[:2]
            up.append(lax.ppermute(ahead, "tp", [(i, i + 1) for i in range(s - 1, count - 1)]))
            down.append(lax.ppermute(behind, "tp", [(i + 1, i) for i in range(count - s)]))
    arrivals = [[t[s] for t in ups + downs] for s in range(count)]
    return assemble(ups, downs), arrivals


def assemble_kernel(count, halves, place_ref, *refs):
    out, sems = refs[-2], refs[-1]
    place = place_ref[0]
    rows = out.shape[0] // (count * halves)
    stride = 2 * count - 1

    def each(action):
        for h in range(halves):
            mine = refs[h * stride : (h + 1) * stride]
            for j in range(count):
                target = out.at[pl.ds((j * halves + h) * rows, rows), :]
                for s in range(-(count - 1), count):
                    source = mine[s + count - 1]

                    @pl.when(place - j == s)
                    def _(source=source, target=target, h=h, j=j):
                        action(pltpu.make_async_copy(source, target, sems.at[h * count + j]))

    each(lambda copy: copy.start())
    each(lambda copy: copy.wait())


def assemble(ups, downs):
    count, halves = len(ups[0]), len(ups)
    rows, dim = ups[0][0].shape
    flat = []
    for up, down in zip(ups, downs):
        flat += down[:0:-1] + up
    anywhere = pl.BlockSpec(memory_space=pl.ANY)
    return pl.pallas_call(
        functools.partial(assemble_kernel, count, halves),
        in_specs=[pl.BlockSpec(memory_space=pltpu.SMEM)] + [anywhere] * len(flat),
        out_specs=pl.BlockSpec(memory_space=pltpu.VMEM),
        out_shape=jax.ShapeDtypeStruct((count * halves * rows, dim), ups[0][0].dtype),
        scratch_shapes=[pltpu.SemaphoreType.DMA((count * halves,))],
        cost_estimate=cost(1, 4 * count * halves * rows * dim),
        name="assemble",
    )(lax.axis_index("tp").astype(jnp.int32).reshape(1), *flat)


def line_scatter(parts, gates=None):
    count = lax.axis_size("tp")
    gates = gates or {}
    up = down = None
    arrivals, sends = [()], [()]
    for s in range(count - 1, 0, -1):
        send_up, send_down = parts[s].astype(F32), parts[count - s].astype(F32)
        if up is not None:
            send_up, send_down = send_up + up.astype(F32), send_down + down.astype(F32)
        step = count - s
        send_up, send_down = send_up.astype(BF), send_down.astype(BF)
        send_up, send_down = lax.optimization_barrier((send_up, send_down, *gates.get(step, ())))[:2]
        sends.append((send_up, send_down))
        up = lax.ppermute(send_up, "tp", [(i, i + 1) for i in range(count - s)])
        down = lax.ppermute(send_down, "tp", [(i + 1, i) for i in range(s - 1, count - 1)])
        arrivals.append((up, down))
    return parts[0].astype(F32) + up.astype(F32) + down.astype(F32), arrivals, sends


def total_fsdp(value):
    count = lax.axis_size("fsdp")
    bit = 1
    while bit < count:
        value = value + lax.ppermute(value, "fsdp", [(i, i ^ bit) for i in range(count)])
        bit *= 2
    return value


def total_tp(value):
    count = lax.axis_size("tp")
    out = flat = lax.optimization_barrier(value.reshape(-1, 128))
    for s in range(1, count):
        out = out + lax.ppermute(flat, "tp", [(i, (i + s) % count) for i in range(count)])
    return lax.optimization_barrier(out).reshape(value.shape)


def shares(value):
    count = lax.axis_size("tp")
    place = lax.axis_index("tp")
    rows = value.shape[0] // count
    return [lax.dynamic_slice_in_dim(value, ((place + d) % count) * rows, rows, 0) for d in range(count)]


def keep_kernel(pos_ref, keep_ref):
    pos = pos_ref[...]
    bound = jnp.zeros((1, pos.shape[1]), jnp.int32)
    for b in range(13, -1, -1):
        trial = bound + (1 << b)
        count = jnp.sum((pos <= trial).astype(F32), axis=0, keepdims=True)
        bound = jnp.where(count <= CAP, trial, bound)
    keep_ref[...] = (pos <= bound).astype(F32)


def kept_pairs(routes, order_row, experts):
    pairs = order_row.shape[0]
    tokens = routes.shape[0]
    step = jnp.arange(pairs, dtype=jnp.int32)
    high = (order_row[:, None] // 128 == jnp.arange(pairs // 128, dtype=jnp.int32)[None, :]).astype(BF)
    low = (order_row[:, None] % 128 == jnp.arange(128, dtype=jnp.int32)[None, :]).astype(BF)
    step_high = (step // 64).astype(BF)[:, None]
    step_low = (step % 64).astype(BF)[:, None]
    table = 64.0 * dot(high * step_high, low, TN) + dot(high * step_low, low, TN)
    place = table.astype(jnp.int32).reshape(tokens, -1) + 1
    hot = routes[:, :, None] == jnp.arange(experts, dtype=jnp.int32)[None, None, :]
    pos = jnp.sum(jnp.where(hot, place[:, :, None], 0), axis=1)
    pos = jnp.where(pos == 0, 1 << 20, pos)
    return pl.pallas_call(
        keep_kernel, out_shape=jax.ShapeDtypeStruct((tokens, experts), F32), name="keep"
    )(pos)


def turn_kernel(q_ref, k_ref, norm_ref, cos_ref, sin_ref, gain_ref, q_out, k_out):
    cos, sin = cos_ref[...], sin_ref[...]
    for slot, (raw, out) in enumerate(((q_ref, q_out), (k_ref, k_out))):
        x = raw[...] * norm_ref[:, slot : slot + 1] * gain_ref[slot]
        out[...] = (x * cos + pltpu.roll(x, HEAD_DIM // 2, 1) * sin).astype(BF)


def turn(raw, norms, cos, sin, gains):
    rows = raw.shape[0]
    heads = raw.shape[1] // (3 * HEAD_DIM)
    part = lambda j: pl.BlockSpec((rows, HEAD_DIM), lambda h: (0, j * heads + h))
    whole = lambda shape: pl.BlockSpec(shape, lambda h: (0,) * len(shape))
    return pl.pallas_call(
        turn_kernel,
        grid=(heads,),
        in_specs=[
            part(0),
            part(1),
            whole(norms.shape),
            whole(cos.shape),
            whole(sin.shape),
            pl.BlockSpec((2, 1, HEAD_DIM), lambda h: (0, 0, h)),
        ],
        out_specs=[part(0)] * 2,
        out_shape=[jax.ShapeDtypeStruct((rows, heads * HEAD_DIM), BF)] * 2,
        compiler_params=params(),
        cost_estimate=cost(10 * raw.size, 6 * raw.size),
        name="turn",
    )(raw, raw, norms, cos, sin, gains)


def turn_back_kernel(
    dq_ref, dk_ref, dkr_ref, q_ref, k_ref, norm_ref, cos_ref, sin_ref, gain_ref, uq_out, uk_out, dots_out, part_out
):
    cos, sin = cos_ref[...], sin_ref[...]
    grads = (dq_ref[...], dk_ref[...] + dkr_ref[...].astype(F32))
    lane = lax.broadcasted_iota(jnp.int32, dots_out.shape, 1)

    @pl.when(pl.program_id(0) == 0)
    def _():
        dots_out[...] = jnp.zeros_like(dots_out)

    for slot, (grad, raw, out) in enumerate(zip(grads, (q_ref, k_ref), (uq_out, uk_out))):
        back = grad * cos - pltpu.roll(grad, HEAD_DIM // 2, 1) * sin
        x = raw[...]
        part_out[slot] = jnp.sum(back * x * norm_ref[:, slot : slot + 1], axis=0, keepdims=True)
        u = back * gain_ref[slot]
        out[...] = u
        dots_out[...] += jnp.where(lane == slot, jnp.sum(u * x, axis=1, keepdims=True), 0.0)


def turn_back(dq, dk, dk_more, raw, norms, cos, sin, gains):
    rows = raw.shape[0]
    heads = raw.shape[1] // (3 * HEAD_DIM)
    part = lambda j: pl.BlockSpec((rows, HEAD_DIM), lambda h: (0, j * heads + h))
    whole = lambda shape: pl.BlockSpec(shape, lambda h: (0,) * len(shape))
    gain_spec = pl.BlockSpec((2, 1, HEAD_DIM), lambda h: (0, 0, h))
    wide = jax.ShapeDtypeStruct((rows, heads * HEAD_DIM), F32)
    return pl.pallas_call(
        turn_back_kernel,
        grid=(heads,),
        in_specs=[
            part(0),
            part(0),
            part(0),
            part(0),
            part(1),
            whole(norms.shape),
            whole(cos.shape),
            whole(sin.shape),
            gain_spec,
        ],
        out_specs=[part(0), part(0), whole((rows, 2)), gain_spec],
        out_shape=[
            wide,
            wide,
            jax.ShapeDtypeStruct((rows, 2), F32),
            jax.ShapeDtypeStruct((2, 1, heads * HEAD_DIM), F32),
        ],
        compiler_params=params(),
        cost_estimate=cost(10 * raw.size, 8 * raw.size),
        name="turn_back",
    )(dq, dk, dk_more, raw, raw, norms, cos, sin, gains)


def own_mask(seg_col, seg_row, first_row, row_count, first_key, key_count):
    rows = lax.broadcasted_iota(jnp.int32, (row_count, key_count), 0) + first_row
    keys = lax.broadcasted_iota(jnp.int32, (row_count, key_count), 1) + first_key
    same = seg_col[first_row : first_row + row_count, :] == seg_row[:, first_key : first_key + key_count]
    return same & (keys <= rows)


SCALE = HEAD_DIM ** (-0.5)


def tile_probs(q_tile, k_ref, seg_col, seg_row, first_row, first_key, keys, kr):
    own = dot(q_tile, k_ref[first_key : first_key + keys, :], NT)
    own = jnp.where(own_mask(seg_col, seg_row, first_row, QT, first_key, keys), own, NEG)
    peak = jnp.max(own, axis=1, keepdims=True)
    far = None
    if kr is not None:
        far = dot(q_tile, kr[...], NT)
        peak = jnp.maximum(peak, jnp.max(far, axis=1, keepdims=True))
        far = jnp.exp((far - peak) * SCALE)
    own = jnp.exp((own - peak) * SCALE)
    total = jnp.sum(own, axis=1, keepdims=True)
    if far is not None:
        total = total + jnp.sum(far, axis=1, keepdims=True)
    inverse = 1.0 / total
    return own * inverse, (None if far is None else far * inverse)


def attend_kernel(cont_ref, q_ref, k_ref, v_ref, kr_ref, vr_ref, col_ref, row_ref, out_ref):
    rows = q_ref.shape[0]

    def run(far):
        for first in range(0, rows, QT):
            start = max(0, first - QT) if far else 0
            keys = first + QT - start
            own, other = tile_probs(
                q_ref[first : first + QT, :], k_ref, col_ref, row_ref, first, start, keys, kr_ref if far else None
            )
            out = dot(own.astype(BF), v_ref[start : start + keys, :])
            if far:
                out = out + dot(other.astype(BF), vr_ref[...])
            out_ref[first : first + QT, :] = out.astype(BF)

    pl.when(cont_ref[0] == 0)(lambda: run(False))
    pl.when(cont_ref[0] != 0)(lambda: run(True))


def attend_specs(rows, count):
    head = pl.BlockSpec((rows, HEAD_DIM), lambda h, c: (0, h))
    return [head] * count + [
        pl.BlockSpec((rows, 1), lambda h, c: (0, 0)),
        pl.BlockSpec((1, rows), lambda h, c: (0, 0)),
    ], head


def attend(cont, q, k, v, kr, vr, seg_col, seg_row):
    rows, width = q.shape
    specs, head = attend_specs(rows, 5)
    return pl.pallas_call(
        attend_kernel,
        grid_spec=pltpu.PrefetchScalarGridSpec(
            num_scalar_prefetch=1, grid=(width // HEAD_DIM,), in_specs=specs, out_specs=head
        ),
        out_shape=jax.ShapeDtypeStruct((rows, width), BF),
        compiler_params=params(),
        cost_estimate=cost(6 * rows * rows * width, 12 * rows * width, rows * rows * 6),
        name="attend",
    )(cont, q, k, v, kr, vr, seg_col, seg_row)


def attend_back_kernel(
    cont_ref, q_ref, k_ref, v_ref, kr_ref, vr_ref, do_ref, col_ref, row_ref, dq_ref, dk_ref, dv_ref, dkr_ref, dvr_ref, far_dk, far_dv
):
    rows = q_ref.shape[0]
    dk_ref[...] = jnp.zeros_like(dk_ref)
    dv_ref[...] = jnp.zeros_like(dv_ref)

    def run(far):
        if far:
            far_dk[...] = jnp.zeros_like(far_dk)
            far_dv[...] = jnp.zeros_like(far_dv)
        for first in range(0, rows, QT):
            start = max(0, first - QT) if far else 0
            keys = first + QT - start
            here = slice(start, start + keys)
            q_tile = q_ref[first : first + QT, :]
            do_tile = do_ref[first : first + QT, :]
            own, other = tile_probs(q_tile, k_ref, col_ref, row_ref, first, start, keys, kr_ref if far else None)
            grad = dot(do_tile, v_ref[here, :], NT)
            mean = jnp.sum(own * grad, axis=1, keepdims=True)
            if far:
                grad_far = dot(do_tile, vr_ref[...], NT)
                mean = mean + jnp.sum(other * grad_far, axis=1, keepdims=True)
            slope = (own * (grad - mean)).astype(BF)
            dq = dot(slope, k_ref[here, :])
            dk_ref[here, :] += dot(slope, q_tile, TN) * SCALE
            dv_ref[here, :] += dot(own.astype(BF), do_tile, TN)
            if far:
                slope = (other * (grad_far - mean)).astype(BF)
                dq = dq + dot(slope, kr_ref[...])
                far_dk[...] += dot(slope, q_tile, TN) * SCALE
                far_dv[...] += dot(other.astype(BF), do_tile, TN)
            dq_ref[first : first + QT, :] = dq * SCALE
        if far:
            dkr_ref[...] = far_dk[...].astype(BF)
            dvr_ref[...] = far_dv[...].astype(BF)
        else:
            dkr_ref[...] = jnp.zeros_like(dkr_ref)
            dvr_ref[...] = jnp.zeros_like(dvr_ref)

    pl.when(cont_ref[0] == 0)(lambda: run(False))
    pl.when(cont_ref[0] != 0)(lambda: run(True))


def attend_back(cont, q, k, v, kr, vr, do, seg_col, seg_row):
    rows, width = q.shape
    specs, head = attend_specs(rows, 6)
    wide = jax.ShapeDtypeStruct((rows, width), F32)
    low = jax.ShapeDtypeStruct((rows, width), BF)
    return pl.pallas_call(
        attend_back_kernel,
        grid_spec=pltpu.PrefetchScalarGridSpec(
            num_scalar_prefetch=1,
            grid=(width // HEAD_DIM,),
            in_specs=specs,
            out_specs=[head] * 5,
            scratch_shapes=[pltpu.VMEM((rows, HEAD_DIM), F32)] * 2,
        ),
        out_shape=[wide, wide, wide, low, low],
        compiler_params=params(),
        cost_estimate=cost(15 * rows * rows * width, 30 * rows * width, rows * rows * 6),
        name="attend_back",
    )(cont, q, k, v, kr, vr, do, seg_col, seg_row)


def hidden_kernel(x_ref, c_ref, g_ref, u_ref, d_ref, w_ref, act_out, dg_out, du_out, s_out):
    expert = pl.program_id(0)
    gate = dot(x_ref[...], g_ref[...])
    up = dot(x_ref[...], u_ref[...])
    back = dot(c_ref[...], d_ref[...])
    lane = lax.broadcasted_iota(jnp.int32, s_out.shape, 1)
    weight = jnp.sum(jnp.where(lane == expert, w_ref[...], 0.0), axis=1, keepdims=True)
    sig = 1.0 / (1.0 + jnp.exp(-gate))
    swish = gate * sig
    act = swish * up
    act_out[...] = (act * weight).astype(BF)
    s = jnp.sum(act * back, axis=1, keepdims=True)
    back = back * weight
    dg_out[...] = (back * up * (sig + swish * (1.0 - sig))).astype(BF)
    du_out[...] = (back * swish).astype(BF)

    @pl.when(expert == 0)
    def _():
        s_out[...] = jnp.zeros_like(s_out)

    s_out[...] = jnp.where(lane == expert, s, s_out[...])


def hidden(x, c, mats, low_mat, weight, block, held=None):
    rows, dim = x.shape
    experts = weight.shape[1]
    span = low_mat.shape[1] // experts
    full = pl.BlockSpec((rows, dim), lambda e: (0, 0))
    mat = lambda j: pl.BlockSpec((dim, span), lambda e: (0, j * experts + e))
    out = pl.BlockSpec((rows, span), lambda e: (block, e))
    wide = jax.ShapeDtypeStruct((2 * rows, experts * span), BF)
    wider = jax.ShapeDtypeStruct((2 * rows, experts * span + 128), BF)
    held = [] if held is None else list(held)
    kernel = hidden_kernel if not held else lambda *refs: hidden_kernel(*refs[:6], *refs[9:])
    return pl.pallas_call(
        kernel,
        grid=(experts,),
        in_specs=[full, full, mat(0), mat(1), mat(0), pl.BlockSpec((rows, experts), lambda e: (0, 0))]
        + [pl.BlockSpec(memory_space=pl.ANY)] * len(held),
        out_specs=[out, out, out, pl.BlockSpec((rows, experts), lambda e: (0, 0))],
        out_shape=[wide, wider, wide, jax.ShapeDtypeStruct((rows, experts), F32)],
        input_output_aliases={6: 0, 7: 1, 8: 2} if held else {},
        compiler_params=params(),
        cost_estimate=cost(6 * rows * dim * experts * span, 2 * (2 * rows * dim + 6 * dim * experts * span)),
        name="hidden",
    )(x, c, mats, mats, low_mat, weight, *held)


def mix_kernel(*refs):
    count = (len(refs) - 1) // 2
    total = None
    for j in range(count):
        term = dot(refs[2 * j][...], refs[2 * j + 1][...], NT)
        total = term if total is None else total + term
    refs[-1][...] = total.astype(refs[-1].dtype)


def mix(pairs, dtype, rows, tile=512):
    cols = pairs[0][1].shape[0]
    specs, flat, flops, nbytes = [], [], 0, 0
    for a, b, j, k in pairs:
        deep = min(a.shape[1], b.shape[1], b.shape[0])
        specs += [
            pl.BlockSpec((rows, deep), lambda i, k=k: (k, 0)),
            pl.BlockSpec((tile, deep), lambda i, j=j: (i, j)),
        ]
        flat += [a, b]
        flops += 2 * rows * cols * deep
        nbytes += 2 * deep * (rows + cols)
    return pl.pallas_call(
        mix_kernel,
        grid=(cols // tile,),
        in_specs=specs,
        out_specs=pl.BlockSpec((rows, tile), lambda i: (0, i)),
        out_shape=jax.ShapeDtypeStruct((rows, cols), dtype),
        compiler_params=params(),
        cost_estimate=cost(flops, nbytes + 4 * rows * cols),
        name="mix",
    )(*flat)


def attn_pack_kernel(experts, q_ref, k_ref, v_ref, o_ref, r_ref, gain_ref, out_ref):
    cols = q_ref.shape[1]
    for j, ref in enumerate((q_ref, k_ref, v_ref)):
        out_ref[:, j * cols : (j + 1) * cols] = (ref[...].astype(F32) * gain_ref[:, 0:1]).astype(BF)
    out_ref[:, 3 * cols : 4 * cols] = o_ref[...].astype(F32).T.astype(BF)
    rest = r_ref[...].astype(F32)
    lane = lax.broadcasted_iota(jnp.int32, rest.shape, 1)
    out_ref[:, 4 * cols :] = jnp.where(lane < experts, rest * gain_ref[:, 1:2], rest).astype(BF)


def attn_pack(q, k, v, o, r, gains, experts):
    return pl.pallas_call(
        functools.partial(attn_pack_kernel, experts),
        out_shape=jax.ShapeDtypeStruct((q.shape[0], 4 * q.shape[1] + r.shape[1]), BF),
        cost_estimate=cost(1, 4 << 20),
        name="attn_pack",
    )(q, k, v, o, r, gains)


PACK = 4


def moe_pack_kernel(core_ref, g_ref, u_ref, d_ref, gain_ref, g_out, u_out, d_out):
    gain = gain_ref[:, 1:2]
    span = g_ref.shape[2]
    for i in range(PACK):
        here = slice(i * span, (i + 1) * span)
        g_out[0, :, here] = (g_ref[i].astype(F32) * gain).astype(BF)
        u_out[0, :, here] = (u_ref[i].astype(F32) * gain).astype(BF)
        d_out[0, :, here] = d_ref[i].astype(F32).T.astype(BF)


def moe_pack(core, gate, up, down, gains):
    experts, piece, span = gate.shape
    local = experts // 2
    steps = local // PACK
    block = pl.BlockSpec((PACK, piece, span), lambda e, c: (e, 0, 0))
    out = pl.BlockSpec((1, piece, PACK * span), lambda e, c: ((e // steps) ^ c[0], 0, e % steps))
    return pl.pallas_call(
        moe_pack_kernel,
        grid_spec=pltpu.PrefetchScalarGridSpec(
            num_scalar_prefetch=1,
            grid=(experts // PACK,),
            in_specs=[
                block,
                block,
                pl.BlockSpec((PACK, span, piece), lambda e, c: (e, 0, 0)),
                pl.BlockSpec(gains.shape, lambda e, c: (0, 0)),
            ],
            out_specs=[out] * 3,
        ),
        out_shape=[jax.ShapeDtypeStruct((2, piece, local * span), BF)] * 3,
        compiler_params=params(),
        cost_estimate=cost(1, 12 * gate.size),
        name="moe_pack",
    )(core, gate, up, down, gains)


def moe_unpack_kernel(core_ref, *refs):
    mine, theirs, gain_ref, outs = refs[:3], refs[3:6], refs[6], refs[7:]
    steps = pl.num_programs(0) // 2
    here = pl.program_id(0) // steps == core_ref[0]
    gain = gain_ref[:, 1:2]
    span = outs[0].shape[2]
    for i in range(PACK):
        part = slice(i * span, (i + 1) * span)
        g, u, d = (jnp.where(here, a[:, part], b[:, part]).astype(F32) for a, b in zip(mine, theirs))
        outs[0][i] = g * gain
        outs[1][i] = u * gain
        outs[2][i] = d.T


def moe_unpack(core, mine, theirs, gains, experts, local):
    piece = mine[0].shape[0]
    span = mine[1].shape[1] // local
    steps = local // PACK
    block = pl.BlockSpec((piece, PACK * span), lambda e, c: (0, e % steps))
    wide = pl.BlockSpec((PACK, piece, span), lambda e, c: (e, 0, 0))
    return pl.pallas_call(
        moe_unpack_kernel,
        grid_spec=pltpu.PrefetchScalarGridSpec(
            num_scalar_prefetch=1,
            grid=(experts // PACK,),
            in_specs=[block] * 6 + [pl.BlockSpec(gains.shape, lambda e, c: (0, 0))],
            out_specs=[wide, wide, pl.BlockSpec((PACK, span, piece), lambda e, c: (e, 0, 0))],
        ),
        out_shape=[
            jax.ShapeDtypeStruct((experts, piece, span), F32),
            jax.ShapeDtypeStruct((experts, piece, span), F32),
            jax.ShapeDtypeStruct((experts, span, piece), F32),
        ],
        compiler_params=params(),
        cost_estimate=cost(1, 24 * experts * piece * span),
        name="moe_unpack",
    )(core, *mine, *theirs, gains)


def angles(seg_block):
    row_count = seg_block.shape[0]
    labels = jnp.arange(CONTS + 1, dtype=jnp.int32)
    member = (seg_block[:, None] == labels[None, :]).astype(jnp.int32)
    counts = jnp.sum(member, axis=0)
    starts = jnp.sum(jnp.where(labels[:, None] > labels[None, :], counts[None, :], 0), axis=1)
    seg_start = jnp.sum(member * starts[None, :], axis=1)
    offset = row_count * (seg_block != 0).astype(jnp.int32)
    places = jnp.arange(row_count, dtype=jnp.int32) - seg_start + offset
    half = HEAD_DIM // 2
    column = jnp.arange(HEAD_DIM, dtype=jnp.int32)
    frequency = jnp.exp((column % half).astype(F32) * (-2.0 * math.log(10000.0) / HEAD_DIM))
    angle = places.astype(F32)[:, None] * frequency[None, :]
    sign = jnp.where(column < half, -1.0, 1.0).astype(F32)
    return jnp.cos(angle), jnp.sin(angle) * sign[None, :]


def inverse_norm(values):
    return lax.rsqrt(jnp.mean(values * values, axis=-1, keepdims=True) + EPS)


def on_device(
    residual,
    query_weight,
    key_weight,
    value_weight,
    out_weight,
    query_gain,
    key_gain,
    attn_gain,
    mlp_gain,
    router_weight,
    gate_weight,
    up_weight,
    down_weight,
    routes,
    route_order,
    seg_ids,
    cotangent,
):
    fsdp, tp = lax.axis_size("fsdp"), lax.axis_size("tp")
    place = lax.axis_index("fsdp")
    core = place % 2
    core_arg = core.astype(jnp.int32).reshape(1)
    dim = residual.shape[1]
    piece = dim // fsdp
    tokens = seg_ids.shape[0]
    share = tokens // tp
    experts, _, span = gate_weight.shape
    local = experts // 2
    cols = query_weight.shape[1]
    heads = cols // HEAD_DIM
    groups = chip_groups()

    norm_gains = jnp.stack([attn_gain, mlp_gain], axis=1).astype(F32)

    stream = residual.astype(F32)
    norm_first = inverse_norm(stream)
    hat_one = stream * norm_first
    hat_low = hat_one.astype(BF)
    normed, steps_one = line_gather(hat_low)

    narrow = HEAD_DIM // fsdp
    gain_col = jnp.stack([query_gain, key_gain]).reshape(-1, 1)
    gain_col = jnp.pad(gain_col, ((0, piece - gain_col.shape[0]), (0, 127 - experts)))
    attn_mat = lax.all_gather(
        attn_pack(
            after(query_weight, hat_low),
            key_weight,
            value_weight,
            out_weight,
            jnp.concatenate([router_weight, gain_col], axis=1),
            norm_gains,
            experts,
        ),
        "fsdp",
        axis=0,
        tiled=True,
    )
    qkv_mat = attn_mat[:, : 3 * cols]
    out_mat = attn_mat[:, 3 * cols : 4 * cols]
    router_mat = attn_mat[:, 4 * cols :]
    gains = router_mat[:, experts].astype(F32).reshape(fsdp, piece)[:, : 2 * heads * narrow]
    gains = gains.reshape(fsdp, 2, heads, narrow).transpose(1, 2, 0, 3).reshape(2, 1, cols)
    lane = jnp.arange(128, dtype=jnp.int32)[None, :]
    router_mat = jnp.where(lane < experts, router_mat, 0)

    packs = moe_pack(core_arg, after(gate_weight, hat_low), up_weight, down_weight, norm_gains)

    def both_rows(kept, given):
        got = swap_core(given)
        return jnp.concatenate([jnp.where(core == 0, kept, got), jnp.where(core == 0, got, kept)], axis=0)

    def over_chips(value):
        return lax.all_gather(value, "fsdp", axis=0, tiled=True, axis_index_groups=groups)

    low_rows = both_rows(packs[2][0], packs[2][1])
    low_mat = over_chips(after(low_rows, attn_mat, *steps_one[2]))
    rows = both_rows(*[jnp.concatenate([packs[0][h], packs[1][h]], axis=1) for h in range(2)])

    raw = dot(normed, qkv_mat)
    half = fsdp // 2
    forth = [(i, i + half) for i in range(half)]
    value_low = raw[:, 2 * cols :].astype(BF)
    value_far = lax.ppermute(value_low, "fsdp", forth)
    query_key = after(raw, value_low)
    totals = jnp.stack(
        [jnp.sum(query_key[:, :cols] ** 2, axis=1), jnp.sum(query_key[:, cols : 2 * cols] ** 2, axis=1)]
    )
    totals = total_tp(totals)
    norms = lax.rsqrt(totals / dim + EPS).T
    upstream, steps_up = line_gather(cotangent, gates={1: [norms]})
    cos, sin = angles(seg_ids)
    query_rot, key_rot = turn(raw, norms, cos, sin, gains)
    key_far = lax.ppermute(key_rot, "fsdp", forth)
    cont = (place >= half).astype(jnp.int32).reshape(1)
    seg_col, seg_row = seg_ids[:, None], seg_ids[None, :]
    mats = over_chips(after(rows, key_far, value_far, *steps_up[3]))

    upstream_far = swap_core(upstream)

    attended = attend(
        cont, after(query_rot, *steps_up[1]), key_rot, value_low, key_far, value_far, seg_col, seg_row
    )
    attn_part = dot(attended, out_mat, NT).astype(BF)
    attn_out, _, _ = line_scatter(shares(attn_part), {1: steps_up[3]})
    after_attn = stream + attn_out
    norm_second = inverse_norm(after_attn)
    hat_two = after_attn * norm_second

    keep = kept_pairs(routes, route_order[0], experts)
    keep_far = swap_core(keep)
    wide_c = jnp.concatenate([upstream, upstream_far], axis=0)
    mlp_own, _ = line_gather(hat_two.astype(BF), gates={2: [keep_far], 3: [wide_c]})
    mlp_far = swap_core(mlp_own)

    def routed(x, kept):
        logits = dot(x, router_mat)[:, :experts]
        grown = jnp.exp(logits - jnp.max(logits, axis=-1, keepdims=True))
        probs = grown / jnp.sum(grown, axis=-1, keepdims=True)
        return probs, lax.dynamic_slice_in_dim(probs * kept, core * local, local, 1)

    def logits_back(s, kept, probs):
        zero = jnp.zeros_like(s)
        pair = kept * jnp.where(core == 0, jnp.concatenate([s, zero], 1), jnp.concatenate([zero, s], 1))
        grad = probs * (pair - jnp.sum(probs * pair, axis=-1, keepdims=True))
        return jnp.pad(grad, ((0, 0), (0, 128 - experts))).astype(BF)

    probs_own, weight_own = routed(mlp_own, keep)
    *held, s_own = hidden(mlp_own, upstream, mats, low_mat, weight_own, 0)
    probs_far, weight_far = routed(mlp_far, keep_far)
    act, dg, du, s_far = hidden(mlp_far, upstream_far, mats, low_mat, weight_far, 1, held)
    gl_own = logits_back(s_own, keep, probs_own)
    gl_far = logits_back(s_far, keep_far, probs_far)

    def both_cores(own, got):
        return [a.astype(F32) + b.astype(F32) for a, b in zip(shares(own), shares(got))]

    def scattered(value):
        return lax.psum_scatter(value, "fsdp", scatter_dimension=0, tiled=True, axis_index_groups=groups)

    dg = lax.dynamic_update_slice(dg, jnp.concatenate([gl_own, gl_far], axis=0), (0, local * span))
    wide_x = jnp.concatenate([mlp_own, mlp_far], axis=0)
    down_term = dot(wide_c, act, TN).astype(BF)
    down_sum = scattered(down_term)

    gl_far = after(gl_far, down_term)
    back_far = mix([(dg, mats, 0, 1), (du, mats, 1, 1), (gl_far, router_mat, 0, 0)], BF, tokens)
    back_got = swap_core(back_far)
    gl_own = after(gl_own, back_far)
    back_own = mix([(dg, mats, 0, 0), (du, mats, 1, 0), (gl_own, router_mat, 0, 0)], BF, tokens)
    grad_scaled, _, back_sends = line_scatter(both_cores(back_own, back_got), {2: [down_sum]})
    gate_term = dot(wide_x, after(dg, back_own, back_got), TN).astype(BF)
    gate_sum = scattered(gate_term)
    up_term = dot(wide_x, after(du, gate_term, *back_sends[2]), TN).astype(BF)
    up_sum = scattered(up_term)
    sums = [gate_sum, up_sum, down_sum]

    grad_after = cotangent.astype(F32) + norm_second * (
        grad_scaled - hat_two * jnp.mean(grad_scaled * hat_two, axis=-1, keepdims=True)
    )
    grad_after_low = after(grad_after.astype(BF), up_term)
    grad_attn, _ = line_gather(grad_after_low)

    act = after(act, back_own, *back_sends[1])
    out_far = mix([(act, low_mat, 0, 1)], BF, tokens)
    out_got = swap_core(out_far)
    out_own = mix([(act, low_mat, 0, 0)], BF, tokens)
    out_low = (out_own.astype(F32) + out_got.astype(F32)).astype(BF)
    out_total = lax.psum_scatter(after(out_low, up_sum, grad_attn), "tp", scatter_dimension=0, tiled=True)
    block_out = after_attn + out_total.astype(F32)

    grad_attended = after(dot(grad_attn, out_mat).astype(BF), out_low)
    dq, dk, dv, dk_far, dv_far = attend_back(
        cont, query_rot, key_rot, value_low, key_far, value_far, grad_attended, seg_col, seg_row
    )
    back_pairs = [(i + half, i) for i in range(half)]
    dk_got, dv_got = lax.ppermute(dk_far, "fsdp", back_pairs), lax.ppermute(dv_far, "fsdp", back_pairs)

    sums = [after(t, dk_far) for t in sums]
    mine = [lax.dynamic_slice_in_dim(t, core * piece, piece, 0) for t in sums]
    theirs = [swap_core(lax.dynamic_slice_in_dim(t, (1 - core) * piece, piece, 0)) for t in sums]
    grad_gate, grad_up, grad_down = moe_unpack(core_arg, mine, theirs, norm_gains, experts, local)
    router_hat = total_tp(sum(t[0][:, local * span : local * span + experts].astype(F32) for t in (mine, theirs)))
    grad_router = router_hat * norm_gains[:, 1:2]
    gain_term = jnp.sum(gate_weight.astype(F32) * grad_gate + up_weight.astype(F32) * grad_up, axis=(0, 2))
    u_query, u_key, dots, gain_parts = turn_back(
        dq, after(dk, sums[1], grad_gate, grad_up, grad_down), dk_got, raw, norms, cos, sin, gains
    )
    dots = total_tp(dots.T).T
    grad_value = (dv + dv_got.astype(F32)).astype(BF)

    def raw_back(u, x, j):
        n = norms[:, j : j + 1]
        return (n * u - x * (n * n * n * dots[:, j : j + 1] / dim)).astype(BF)

    grad_raw = jnp.concatenate(
        [raw_back(u_query, raw[:, :cols], 0), raw_back(u_key, raw[:, cols : 2 * cols], 1), grad_value], axis=1
    )
    normed_part = dot(grad_raw, qkv_mat, NT).astype(BF)
    small = gain_parts.reshape(2, heads, fsdp, narrow).transpose(2, 0, 1, 3).reshape(fsdp, -1)
    small = total_fsdp(small)
    grad_raw_later = after(grad_raw, normed_part)
    qkv_term = dot(normed, grad_raw_later, TN).astype(BF)
    grad_hat, _, last_sends = line_scatter(shares(normed_part), {1: [out_total], 3: [router_hat, gain_term, small]})


    def summed(value):
        return lax.psum_scatter(value, "fsdp", scatter_dimension=0, tiled=True).astype(F32)

    grad_out_proj = summed(dot(grad_attn, after(attended, dk_far), TN).astype(BF)).T
    attn_sum = summed(qkv_term)
    qkv_hat = [attn_sum[:, j * cols : (j + 1) * cols] for j in range(3)]
    qkv_grad = [norm_gains[:, 0:1] * t for t in qkv_hat]
    small = lax.dynamic_index_in_dim(small, place, 0, keepdims=False)
    small = small.reshape(2, heads, narrow)

    attn_dots = sum(jnp.sum(w.astype(F32) * t, axis=1) for w, t in zip((query_weight, key_weight, value_weight), qkv_hat))
    both_dots = total_tp(jnp.stack([attn_dots, gain_term / norm_gains[:, 1]]))
    grad_attn_gain = both_dots[0]
    grad_mlp_gain = both_dots[1] + jnp.sum(router_weight.astype(F32) * router_hat, axis=1)
    grad_hat = after(grad_hat, both_dots, grad_out_proj, *qkv_grad)
    grad_input = grad_after + norm_first * (grad_hat - hat_one * jnp.mean(grad_hat * hat_one, axis=-1, keepdims=True))
    return (
        block_out,
        grad_input,
        qkv_grad[0],
        qkv_grad[1],
        qkv_grad[2],
        grad_out_proj,
        small[0],
        small[1],
        grad_attn_gain,
        grad_mlp_gain,
        grad_router,
        grad_gate,
        grad_up,
        grad_down,
    )


def solution(mesh):
    rows = P(("fsdp", "tp"), None)
    in_specs = (
        rows,
        P("fsdp", "tp"),
        P("fsdp", "tp"),
        P("fsdp", "tp"),
        P("tp", "fsdp"),
        P("tp", "fsdp"),
        P("tp", "fsdp"),
        P("fsdp"),
        P("fsdp"),
        P("fsdp", None),
        P(None, "fsdp", "tp"),
        P(None, "fsdp", "tp"),
        P(None, "tp", "fsdp"),
        P("fsdp", None),
        P("fsdp", None),
        P("fsdp"),
        rows,
    )
    out_specs = (
        rows,
        rows,
        P("fsdp", "tp"),
        P("fsdp", "tp"),
        P("fsdp", "tp"),
        P("tp", "fsdp"),
        P("tp", "fsdp"),
        P("tp", "fsdp"),
        P("fsdp"),
        P("fsdp"),
        P("fsdp", None),
        P(None, "fsdp", "tp"),
        P(None, "fsdp", "tp"),
        P(None, "tp", "fsdp"),
    )
    return jax.shard_map(on_device, mesh=mesh, in_specs=in_specs, out_specs=out_specs, check_vma=False)
```

```python
import functools
import math

import jax
import jax.numpy as jnp
from jax import lax
from jax.experimental import pallas as pl
from jax.experimental.pallas import tpu as pltpu
from jax.sharding import PartitionSpec as P

HEAD_DIM = 128
CONTS = 8
CAP = 512
EPS = 1e-05
NEG = -1e30
QT = 256
BF = jnp.bfloat16
F32 = jnp.float32
NT = (((1,), (1,)), ((), ()))
TN = (((0,), (0,)), ((), ()))


def dot(a, b, dims=(((1,), (0,)), ((), ()))):
    return lax.dot_general(a, b, dims, preferred_element_type=F32)


def params(count=1):
    return pltpu.CompilerParams(
        dimension_semantics=("arbitrary",) * count, vmem_limit_bytes=56 << 20
    )


def cost(flops, nbytes, trans=0):
    return pl.CostEstimate(flops=int(flops), bytes_accessed=int(nbytes), transcendentals=int(trans))


def swap_core(value):
    count = lax.axis_size("fsdp")
    return lax.ppermute(value, "fsdp", [(i, i ^ 1) for i in range(count)])


def chip_groups():
    count = lax.axis_size("fsdp")
    return [list(range(c, count, 2)) for c in range(2)]


def after(value, *others):
    return lax.optimization_barrier((value,) + others)[0]


def line_gather(value, halves=2, gates=None):
    count = lax.axis_size("tp")
    gates = gates or {}
    rows = value.shape[0] // halves
    ups = [[value[h * rows : (h + 1) * rows]] for h in range(halves)]
    downs = [[u[0]] for u in ups]
    for s in range(1, count):
        for up, down in zip(ups, downs):
            ahead, behind = up[-1], down[-1]
            if s > 1 or s in gates:
                ahead, behind = lax.optimization_barrier((ahead, behind, *gates.get(s, ())))[:2]
            up.append(lax.ppermute(ahead, "tp", [(i, i + 1) for i in range(s - 1, count - 1)]))
            down.append(lax.ppermute(behind, "tp", [(i + 1, i) for i in range(count - s)]))
    arrivals = [[t[s] for t in ups + downs] for s in range(count)]
    return assemble(ups, downs), arrivals


def assemble_kernel(count, halves, place_ref, *refs):
    out, sems = refs[-2], refs[-1]
    place = place_ref[0]
    rows = out.shape[0] // (count * halves)
    stride = 2 * count - 1

    def each(action):
        for h in range(halves):
            mine = refs[h * stride : (h + 1) * stride]
            for j in range(count):
                target = out.at[pl.ds((j * halves + h) * rows, rows), :]
                for s in range(-(count - 1), count):
                    source = mine[s + count - 1]

                    @pl.when(place - j == s)
                    def _(source=source, target=target, h=h, j=j):
                        action(pltpu.make_async_copy(source, target, sems.at[h * count + j]))

    each(lambda copy: copy.start())
    each(lambda copy: copy.wait())


def assemble(ups, downs):
    count, halves = len(ups[0]), len(ups)
    rows, dim = ups[0][0].shape
    flat = []
    for up, down in zip(ups, downs):
        flat += down[:0:-1] + up
    anywhere = pl.BlockSpec(memory_space=pl.ANY)
    return pl.pallas_call(
        functools.partial(assemble_kernel, count, halves),
        in_specs=[pl.BlockSpec(memory_space=pltpu.SMEM)] + [anywhere] * len(flat),
        out_specs=pl.BlockSpec(memory_space=pltpu.VMEM),
        out_shape=jax.ShapeDtypeStruct((count * halves * rows, dim), ups[0][0].dtype),
        scratch_shapes=[pltpu.SemaphoreType.DMA((count * halves,))],
        cost_estimate=cost(1, 4 * count * halves * rows * dim),
        name="assemble",
    )(lax.axis_index("tp").astype(jnp.int32).reshape(1), *flat)


def line_scatter(parts, gates=None):
    count = lax.axis_size("tp")
    gates = gates or {}
    up = down = None
    arrivals, sends = [()], [()]
    for s in range(count - 1, 0, -1):
        send_up, send_down = parts[s].astype(F32), parts[count - s].astype(F32)
        if up is not None:
            send_up, send_down = send_up + up.astype(F32), send_down + down.astype(F32)
        step = count - s
        send_up, send_down = send_up.astype(BF), send_down.astype(BF)
        send_up, send_down = lax.optimization_barrier((send_up, send_down, *gates.get(step, ())))[:2]
        sends.append((send_up, send_down))
        up = lax.ppermute(send_up, "tp", [(i, i + 1) for i in range(count - s)])
        down = lax.ppermute(send_down, "tp", [(i + 1, i) for i in range(s - 1, count - 1)])
        arrivals.append((up, down))
    return parts[0].astype(F32) + up.astype(F32) + down.astype(F32), arrivals, sends


def total_fsdp(value):
    count = lax.axis_size("fsdp")
    bit = 1
    while bit < count:
        value = value + lax.ppermute(value, "fsdp", [(i, i ^ bit) for i in range(count)])
        bit *= 2
    return value


def total_tp(value):
    count = lax.axis_size("tp")
    out = flat = lax.optimization_barrier(value.reshape(-1, 128))
    for s in range(1, count):
        out = out + lax.ppermute(flat, "tp", [(i, (i + s) % count) for i in range(count)])
    return lax.optimization_barrier(out).reshape(value.shape)


def shares(value):
    count = lax.axis_size("tp")
    place = lax.axis_index("tp")
    rows = value.shape[0] // count
    return [lax.dynamic_slice_in_dim(value, ((place + d) % count) * rows, rows, 0) for d in range(count)]


def keep_kernel(pos_ref, keep_ref):
    pos = pos_ref[...]
    bound = jnp.zeros((1, pos.shape[1]), jnp.int32)
    for b in range(13, -1, -1):
        trial = bound + (1 << b)
        count = jnp.sum((pos <= trial).astype(F32), axis=0, keepdims=True)
        bound = jnp.where(count <= CAP, trial, bound)
    keep_ref[...] = (pos <= bound).astype(F32)


def kept_pairs(routes, order_row, experts):
    pairs = order_row.shape[0]
    tokens = routes.shape[0]
    step = jnp.arange(pairs, dtype=jnp.int32)
    high = (order_row[:, None] // 128 == jnp.arange(pairs // 128, dtype=jnp.int32)[None, :]).astype(BF)
    low = (order_row[:, None] % 128 == jnp.arange(128, dtype=jnp.int32)[None, :]).astype(BF)
    step_high = (step // 64).astype(BF)[:, None]
    step_low = (step % 64).astype(BF)[:, None]
    table = 64.0 * dot(high * step_high, low, TN) + dot(high * step_low, low, TN)
    place = table.astype(jnp.int32).reshape(tokens, -1) + 1
    hot = routes[:, :, None] == jnp.arange(experts, dtype=jnp.int32)[None, None, :]
    pos = jnp.sum(jnp.where(hot, place[:, :, None], 0), axis=1)
    pos = jnp.where(pos == 0, 1 << 20, pos)
    return pl.pallas_call(
        keep_kernel, out_shape=jax.ShapeDtypeStruct((tokens, experts), F32), name="keep"
    )(pos)


def turn_kernel(q_ref, k_ref, norm_ref, cos_ref, sin_ref, gain_ref, q_out, k_out):
    cos, sin = cos_ref[...], sin_ref[...]
    for slot, (raw, out) in enumerate(((q_ref, q_out), (k_ref, k_out))):
        x = raw[...] * norm_ref[:, slot : slot + 1] * gain_ref[slot]
        out[...] = (x * cos + pltpu.roll(x, HEAD_DIM // 2, 1) * sin).astype(BF)


def turn(raw, norms, cos, sin, gains):
    rows = raw.shape[0]
    heads = raw.shape[1] // (3 * HEAD_DIM)
    part = lambda j: pl.BlockSpec((rows, HEAD_DIM), lambda h: (0, j * heads + h))
    whole = lambda shape: pl.BlockSpec(shape, lambda h: (0,) * len(shape))
    return pl.pallas_call(
        turn_kernel,
        grid=(heads,),
        in_specs=[
            part(0),
            part(1),
            whole(norms.shape),
            whole(cos.shape),
            whole(sin.shape),
            pl.BlockSpec((2, 1, HEAD_DIM), lambda h: (0, 0, h)),
        ],
        out_specs=[part(0)] * 2,
        out_shape=[jax.ShapeDtypeStruct((rows, heads * HEAD_DIM), BF)] * 2,
        compiler_params=params(),
        cost_estimate=cost(10 * raw.size, 6 * raw.size),
        name="turn",
    )(raw, raw, norms, cos, sin, gains)


def turn_back_kernel(
    dq_ref, dk_ref, dkr_ref, q_ref, k_ref, norm_ref, cos_ref, sin_ref, gain_ref, uq_out, uk_out, dots_out, part_out
):
    cos, sin = cos_ref[...], sin_ref[...]
    grads = (dq_ref[...], dk_ref[...] + dkr_ref[...].astype(F32))
    lane = lax.broadcasted_iota(jnp.int32, dots_out.shape, 1)

    @pl.when(pl.program_id(0) == 0)
    def _():
        dots_out[...] = jnp.zeros_like(dots_out)

    for slot, (grad, raw, out) in enumerate(zip(grads, (q_ref, k_ref), (uq_out, uk_out))):
        back = grad * cos - pltpu.roll(grad, HEAD_DIM // 2, 1) * sin
        x = raw[...]
        part_out[slot] = jnp.sum(back * x * norm_ref[:, slot : slot + 1], axis=0, keepdims=True)
        u = back * gain_ref[slot]
        out[...] = u
        dots_out[...] += jnp.where(lane == slot, jnp.sum(u * x, axis=1, keepdims=True), 0.0)


def turn_back(dq, dk, dk_more, raw, norms, cos, sin, gains):
    rows = raw.shape[0]
    heads = raw.shape[1] // (3 * HEAD_DIM)
    part = lambda j: pl.BlockSpec((rows, HEAD_DIM), lambda h: (0, j * heads + h))
    whole = lambda shape: pl.BlockSpec(shape, lambda h: (0,) * len(shape))
    gain_spec = pl.BlockSpec((2, 1, HEAD_DIM), lambda h: (0, 0, h))
    wide = jax.ShapeDtypeStruct((rows, heads * HEAD_DIM), F32)
    return pl.pallas_call(
        turn_back_kernel,
        grid=(heads,),
        in_specs=[
            part(0),
            part(0),
            part(0),
            part(0),
            part(1),
            whole(norms.shape),
            whole(cos.shape),
            whole(sin.shape),
            gain_spec,
        ],
        out_specs=[part(0), part(0), whole((rows, 2)), gain_spec],
        out_shape=[
            wide,
            wide,
            jax.ShapeDtypeStruct((rows, 2), F32),
            jax.ShapeDtypeStruct((2, 1, heads * HEAD_DIM), F32),
        ],
        compiler_params=params(),
        cost_estimate=cost(10 * raw.size, 8 * raw.size),
        name="turn_back",
    )(dq, dk, dk_more, raw, raw, norms, cos, sin, gains)


def own_mask(seg_col, seg_row, first_row, row_count, first_key, key_count):
    rows = lax.broadcasted_iota(jnp.int32, (row_count, key_count), 0) + first_row
    keys = lax.broadcasted_iota(jnp.int32, (row_count, key_count), 1) + first_key
    same = seg_col[first_row : first_row + row_count, :] == seg_row[:, first_key : first_key + key_count]
    return same & (keys <= rows)


SCALE = HEAD_DIM ** (-0.5)


def tile_probs(q_tile, k_ref, seg_col, seg_row, first_row, first_key, keys, kr):
    own = dot(q_tile, k_ref[first_key : first_key + keys, :], NT)
    own = jnp.where(own_mask(seg_col, seg_row, first_row, QT, first_key, keys), own, NEG)
    peak = jnp.max(own, axis=1, keepdims=True)
    far = None
    if kr is not None:
        far = dot(q_tile, kr[...], NT)
        peak = jnp.maximum(peak, jnp.max(far, axis=1, keepdims=True))
        far = jnp.exp((far - peak) * SCALE)
    own = jnp.exp((own - peak) * SCALE)
    total = jnp.sum(own, axis=1, keepdims=True)
    if far is not None:
        total = total + jnp.sum(far, axis=1, keepdims=True)
    inverse = 1.0 / total
    return own * inverse, (None if far is None else far * inverse)


def attend_kernel(cont_ref, q_ref, k_ref, v_ref, kr_ref, vr_ref, col_ref, row_ref, out_ref):
    rows = q_ref.shape[0]

    def run(far):
        for first in range(0, rows, QT):
            start = max(0, first - QT) if far else 0
            keys = first + QT - start
            own, other = tile_probs(
                q_ref[first : first + QT, :], k_ref, col_ref, row_ref, first, start, keys, kr_ref if far else None
            )
            out = dot(own.astype(BF), v_ref[start : start + keys, :])
            if far:
                out = out + dot(other.astype(BF), vr_ref[...])
            out_ref[first : first + QT, :] = out.astype(BF)

    pl.when(cont_ref[0] == 0)(lambda: run(False))
    pl.when(cont_ref[0] != 0)(lambda: run(True))


def attend_specs(rows, count):
    head = pl.BlockSpec((rows, HEAD_DIM), lambda h, c: (0, h))
    return [head] * count + [
        pl.BlockSpec((rows, 1), lambda h, c: (0, 0)),
        pl.BlockSpec((1, rows), lambda h, c: (0, 0)),
    ], head


def attend(cont, q, k, v, kr, vr, seg_col, seg_row):
    rows, width = q.shape
    specs, head = attend_specs(rows, 5)
    return pl.pallas_call(
        attend_kernel,
        grid_spec=pltpu.PrefetchScalarGridSpec(
            num_scalar_prefetch=1, grid=(width // HEAD_DIM,), in_specs=specs, out_specs=head
        ),
        out_shape=jax.ShapeDtypeStruct((rows, width), BF),
        compiler_params=params(),
        cost_estimate=cost(6 * rows * rows * width, 12 * rows * width, rows * rows * 6),
        name="attend",
    )(cont, q, k, v, kr, vr, seg_col, seg_row)


def attend_back_kernel(
    cont_ref, q_ref, k_ref, v_ref, kr_ref, vr_ref, do_ref, col_ref, row_ref, dq_ref, dk_ref, dv_ref, dkr_ref, dvr_ref, far_dk, far_dv
):
    rows = q_ref.shape[0]
    dk_ref[...] = jnp.zeros_like(dk_ref)
    dv_ref[...] = jnp.zeros_like(dv_ref)

    def run(far):
        if far:
            far_dk[...] = jnp.zeros_like(far_dk)
            far_dv[...] = jnp.zeros_like(far_dv)
        for first in range(0, rows, QT):
            start = max(0, first - QT) if far else 0
            keys = first + QT - start
            here = slice(start, start + keys)
            q_tile = q_ref[first : first + QT, :]
            do_tile = do_ref[first : first + QT, :]
            own, other = tile_probs(q_tile, k_ref, col_ref, row_ref, first, start, keys, kr_ref if far else None)
            grad = dot(do_tile, v_ref[here, :], NT)
            mean = jnp.sum(own * grad, axis=1, keepdims=True)
            if far:
                grad_far = dot(do_tile, vr_ref[...], NT)
                mean = mean + jnp.sum(other * grad_far, axis=1, keepdims=True)
            slope = (own * (grad - mean)).astype(BF)
            dq = dot(slope, k_ref[here, :])
            dk_ref[here, :] += dot(slope, q_tile, TN) * SCALE
            dv_ref[here, :] += dot(own.astype(BF), do_tile, TN)
            if far:
                slope = (other * (grad_far - mean)).astype(BF)
                dq = dq + dot(slope, kr_ref[...])
                far_dk[...] += dot(slope, q_tile, TN) * SCALE
                far_dv[...] += dot(other.astype(BF), do_tile, TN)
            dq_ref[first : first + QT, :] = dq * SCALE
        if far:
            dkr_ref[...] = far_dk[...].astype(BF)
            dvr_ref[...] = far_dv[...].astype(BF)
        else:
            dkr_ref[...] = jnp.zeros_like(dkr_ref)
            dvr_ref[...] = jnp.zeros_like(dvr_ref)

    pl.when(cont_ref[0] == 0)(lambda: run(False))
    pl.when(cont_ref[0] != 0)(lambda: run(True))


def attend_back(cont, q, k, v, kr, vr, do, seg_col, seg_row):
    rows, width = q.shape
    specs, head = attend_specs(rows, 6)
    wide = jax.ShapeDtypeStruct((rows, width), F32)
    low = jax.ShapeDtypeStruct((rows, width), BF)
    return pl.pallas_call(
        attend_back_kernel,
        grid_spec=pltpu.PrefetchScalarGridSpec(
            num_scalar_prefetch=1,
            grid=(width // HEAD_DIM,),
            in_specs=specs,
            out_specs=[head] * 5,
            scratch_shapes=[pltpu.VMEM((rows, HEAD_DIM), F32)] * 2,
        ),
        out_shape=[wide, wide, wide, low, low],
        compiler_params=params(),
        cost_estimate=cost(15 * rows * rows * width, 30 * rows * width, rows * rows * 6),
        name="attend_back",
    )(cont, q, k, v, kr, vr, do, seg_col, seg_row)


def hidden_kernel(x_ref, c_ref, g_ref, u_ref, d_ref, w_ref, act_out, dg_out, du_out, s_out):
    expert = pl.program_id(0)
    gate = dot(x_ref[...], g_ref[...])
    up = dot(x_ref[...], u_ref[...])
    back = dot(c_ref[...], d_ref[...])
    lane = lax.broadcasted_iota(jnp.int32, s_out.shape, 1)
    weight = jnp.sum(jnp.where(lane == expert, w_ref[...], 0.0), axis=1, keepdims=True)
    sig = 1.0 / (1.0 + jnp.exp(-gate))
    swish = gate * sig
    act = swish * up
    act_out[...] = (act * weight).astype(BF)
    s = jnp.sum(act * back, axis=1, keepdims=True)
    back = back * weight
    dg_out[...] = (back * up * (sig + swish * (1.0 - sig))).astype(BF)
    du_out[...] = (back * swish).astype(BF)

    @pl.when(expert == 0)
    def _():
        s_out[...] = jnp.zeros_like(s_out)

    s_out[...] = jnp.where(lane == expert, s, s_out[...])


def hidden(x, c, mats, low_mat, weight, block, held=None):
    rows, dim = x.shape
    experts = weight.shape[1]
    span = low_mat.shape[1] // experts
    full = pl.BlockSpec((rows, dim), lambda e: (0, 0))
    mat = lambda j: pl.BlockSpec((dim, span), lambda e: (0, j * experts + e))
    out = pl.BlockSpec((rows, span), lambda e: (block, e))
    wide = jax.ShapeDtypeStruct((2 * rows, experts * span), BF)
    wider = jax.ShapeDtypeStruct((2 * rows, experts * span + 128), BF)
    held = [] if held is None else list(held)
    kernel = hidden_kernel if not held else lambda *refs: hidden_kernel(*refs[:6], *refs[9:])
    return pl.pallas_call(
        kernel,
        grid=(experts,),
        in_specs=[full, full, mat(0), mat(1), mat(0), pl.BlockSpec((rows, experts), lambda e: (0, 0))]
        + [pl.BlockSpec(memory_space=pl.ANY)] * len(held),
        out_specs=[out, out, out, pl.BlockSpec((rows, experts), lambda e: (0, 0))],
        out_shape=[wide, wider, wide, jax.ShapeDtypeStruct((rows, experts), F32)],
        input_output_aliases={6: 0, 7: 1, 8: 2} if held else {},
        compiler_params=params(),
        cost_estimate=cost(6 * rows * dim * experts * span, 2 * (2 * rows * dim + 6 * dim * experts * span)),
        name="hidden",
    )(x, c, mats, mats, low_mat, weight, *held)


def mix_kernel(*refs):
    count = (len(refs) - 1) // 2
    total = None
    for j in range(count):
        term = dot(refs[2 * j][...], refs[2 * j + 1][...], NT)
        total = term if total is None else total + term
    refs[-1][...] = total.astype(refs[-1].dtype)


def mix(pairs, dtype, rows, tile=512):
    cols = pairs[0][1].shape[0]
    specs, flat, flops, nbytes = [], [], 0, 0
    for a, b, j, k in pairs:
        deep = min(a.shape[1], b.shape[1], b.shape[0])
        specs += [
            pl.BlockSpec((rows, deep), lambda i, k=k: (k, 0)),
            pl.BlockSpec((tile, deep), lambda i, j=j: (i, j)),
        ]
        flat += [a, b]
        flops += 2 * rows * cols * deep
        nbytes += 2 * deep * (rows + cols)
    return pl.pallas_call(
        mix_kernel,
        grid=(cols // tile,),
        in_specs=specs,
        out_specs=pl.BlockSpec((rows, tile), lambda i: (0, i)),
        out_shape=jax.ShapeDtypeStruct((rows, cols), dtype),
        compiler_params=params(),
        cost_estimate=cost(flops, nbytes + 4 * rows * cols),
        name="mix",
    )(*flat)


def attn_pack_kernel(experts, q_ref, k_ref, v_ref, o_ref, r_ref, gain_ref, out_ref):
    cols = q_ref.shape[1]
    for j, ref in enumerate((q_ref, k_ref, v_ref)):
        out_ref[:, j * cols : (j + 1) * cols] = (ref[...].astype(F32) * gain_ref[:, 0:1]).astype(BF)
    out_ref[:, 3 * cols : 4 * cols] = o_ref[...].astype(F32).T.astype(BF)
    rest = r_ref[...].astype(F32)
    lane = lax.broadcasted_iota(jnp.int32, rest.shape, 1)
    out_ref[:, 4 * cols :] = jnp.where(lane < experts, rest * gain_ref[:, 1:2], rest).astype(BF)


def attn_pack(q, k, v, o, r, gains, experts):
    return pl.pallas_call(
        functools.partial(attn_pack_kernel, experts),
        out_shape=jax.ShapeDtypeStruct((q.shape[0], 4 * q.shape[1] + r.shape[1]), BF),
        cost_estimate=cost(1, 4 << 20),
        name="attn_pack",
    )(q, k, v, o, r, gains)


PACK = 4


def moe_pack_kernel(turned, core_ref, gain_ref, *refs):
    gain = gain_ref[:, 1:2]
    count = len(refs) // 2
    for ref, out in zip(refs[:count], refs[count:]):
        span = out.shape[2] // PACK
        for i in range(PACK):
            x = ref[i].astype(F32)
            out[0, :, i * span : (i + 1) * span] = (x.T if turned else x * gain).astype(BF)


def moe_pack(core, weights, gains, turned):
    experts, rows, cols = weights[0].shape
    piece, span = (cols, rows) if turned else (rows, cols)
    local = experts // 2
    steps = local // PACK
    out = pl.BlockSpec((1, piece, PACK * span), lambda e, c: ((e // steps) ^ c[0], 0, e % steps))
    return pl.pallas_call(
        functools.partial(moe_pack_kernel, turned),
        grid_spec=pltpu.PrefetchScalarGridSpec(
            num_scalar_prefetch=1,
            grid=(experts // PACK,),
            in_specs=[pl.BlockSpec(gains.shape, lambda e, c: (0, 0))]
            + [pl.BlockSpec((PACK, rows, cols), lambda e, c: (e, 0, 0))] * len(weights),
            out_specs=[out] * len(weights),
        ),
        out_shape=[jax.ShapeDtypeStruct((2, piece, local * span), BF)] * len(weights),
        compiler_params=params(),
        cost_estimate=cost(1, 4 * len(weights) * weights[0].size),
        name="moe_pack",
    )(core, gains, *weights)


def moe_unpack_kernel(core_ref, *refs):
    mine, theirs, gain_ref, outs = refs[:3], refs[3:6], refs[6], refs[7:]
    steps = pl.num_programs(0) // 2
    here = pl.program_id(0) // steps == core_ref[0]
    gain = gain_ref[:, 1:2]
    span = outs[0].shape[2]
    for i in range(PACK):
        part = slice(i * span, (i + 1) * span)
        g, u, d = (jnp.where(here, a[:, part], b[:, part]).astype(F32) for a, b in zip(mine, theirs))
        outs[0][i] = g * gain
        outs[1][i] = u * gain
        outs[2][i] = d.T


def moe_unpack(core, mine, theirs, gains, experts, local):
    piece = mine[0].shape[0]
    span = mine[1].shape[1] // local
    steps = local // PACK
    block = pl.BlockSpec((piece, PACK * span), lambda e, c: (0, e % steps))
    wide = pl.BlockSpec((PACK, piece, span), lambda e, c: (e, 0, 0))
    return pl.pallas_call(
        moe_unpack_kernel,
        grid_spec=pltpu.PrefetchScalarGridSpec(
            num_scalar_prefetch=1,
            grid=(experts // PACK,),
            in_specs=[block] * 6 + [pl.BlockSpec(gains.shape, lambda e, c: (0, 0))],
            out_specs=[wide, wide, pl.BlockSpec((PACK, span, piece), lambda e, c: (e, 0, 0))],
        ),
        out_shape=[
            jax.ShapeDtypeStruct((experts, piece, span), F32),
            jax.ShapeDtypeStruct((experts, piece, span), F32),
            jax.ShapeDtypeStruct((experts, span, piece), F32),
        ],
        compiler_params=params(),
        cost_estimate=cost(1, 24 * experts * piece * span),
        name="moe_unpack",
    )(core, *mine, *theirs, gains)


def angles(seg_block):
    row_count = seg_block.shape[0]
    labels = jnp.arange(CONTS + 1, dtype=jnp.int32)
    member = (seg_block[:, None] == labels[None, :]).astype(jnp.int32)
    counts = jnp.sum(member, axis=0)
    starts = jnp.sum(jnp.where(labels[:, None] > labels[None, :], counts[None, :], 0), axis=1)
    seg_start = jnp.sum(member * starts[None, :], axis=1)
    offset = row_count * (seg_block != 0).astype(jnp.int32)
    places = jnp.arange(row_count, dtype=jnp.int32) - seg_start + offset
    half = HEAD_DIM // 2
    column = jnp.arange(HEAD_DIM, dtype=jnp.int32)
    frequency = jnp.exp((column % half).astype(F32) * (-2.0 * math.log(10000.0) / HEAD_DIM))
    angle = places.astype(F32)[:, None] * frequency[None, :]
    sign = jnp.where(column < half, -1.0, 1.0).astype(F32)
    return jnp.cos(angle), jnp.sin(angle) * sign[None, :]


def inverse_norm(values):
    return lax.rsqrt(jnp.mean(values * values, axis=-1, keepdims=True) + EPS)


def on_device(
    residual,
    query_weight,
    key_weight,
    value_weight,
    out_weight,
    query_gain,
    key_gain,
    attn_gain,
    mlp_gain,
    router_weight,
    gate_weight,
    up_weight,
    down_weight,
    routes,
    route_order,
    seg_ids,
    cotangent,
):
    fsdp, tp = lax.axis_size("fsdp"), lax.axis_size("tp")
    place = lax.axis_index("fsdp")
    core = place % 2
    core_arg = core.astype(jnp.int32).reshape(1)
    dim = residual.shape[1]
    piece = dim // fsdp
    tokens = seg_ids.shape[0]
    share = tokens // tp
    experts, _, span = gate_weight.shape
    local = experts // 2
    cols = query_weight.shape[1]
    heads = cols // HEAD_DIM
    groups = chip_groups()

    norm_gains = jnp.stack([attn_gain, mlp_gain], axis=1).astype(F32)

    stream = residual.astype(F32)
    norm_first = inverse_norm(stream)
    hat_one = stream * norm_first
    hat_low = hat_one.astype(BF)
    normed, steps_one = line_gather(hat_low)

    narrow = HEAD_DIM // fsdp
    gain_col = jnp.stack([query_gain, key_gain]).reshape(-1, 1)
    gain_col = jnp.pad(gain_col, ((0, piece - gain_col.shape[0]), (0, 127 - experts)))
    attn_mat = lax.all_gather(
        attn_pack(
            after(query_weight, hat_low),
            key_weight,
            value_weight,
            out_weight,
            jnp.concatenate([router_weight, gain_col], axis=1),
            norm_gains,
            experts,
        ),
        "fsdp",
        axis=0,
        tiled=True,
    )
    qkv_mat = attn_mat[:, : 3 * cols]
    out_mat = attn_mat[:, 3 * cols : 4 * cols]
    router_mat = attn_mat[:, 4 * cols :]
    gains = router_mat[:, experts].astype(F32).reshape(fsdp, piece)[:, : 2 * heads * narrow]
    gains = gains.reshape(fsdp, 2, heads, narrow).transpose(1, 2, 0, 3).reshape(2, 1, cols)
    lane = jnp.arange(128, dtype=jnp.int32)[None, :]
    router_mat = jnp.where(lane < experts, router_mat, 0)

    (low_pack,) = moe_pack(core_arg, [after(down_weight, hat_low)], norm_gains, True)
    packs = moe_pack(core_arg, [after(gate_weight, *steps_one[2]), up_weight], norm_gains, False)

    def both_rows(kept, given):
        got = swap_core(given)
        return jnp.concatenate([jnp.where(core == 0, kept, got), jnp.where(core == 0, got, kept)], axis=0)

    def over_chips(value):
        return lax.all_gather(value, "fsdp", axis=0, tiled=True, axis_index_groups=groups)

    low_rows = both_rows(low_pack[0], low_pack[1])
    low_mat = over_chips(after(low_rows, attn_mat, *steps_one[2]))
    rows = both_rows(*[jnp.concatenate([packs[0][h], packs[1][h]], axis=1) for h in range(2)])

    raw = dot(normed, qkv_mat)
    half = fsdp // 2
    forth = [(i, i + half) for i in range(half)]
    value_low = raw[:, 2 * cols :].astype(BF)
    value_far = lax.ppermute(value_low, "fsdp", forth)
    query_key = after(raw, value_low)
    totals = jnp.stack(
        [jnp.sum(query_key[:, :cols] ** 2, axis=1), jnp.sum(query_key[:, cols : 2 * cols] ** 2, axis=1)]
    )
    totals = total_tp(totals)
    norms = lax.rsqrt(totals / dim + EPS).T
    upstream, steps_up = line_gather(cotangent, gates={1: [norms]})
    cos, sin = angles(seg_ids)
    query_rot, key_rot = turn(raw, norms, cos, sin, gains)
    key_far = lax.ppermute(key_rot, "fsdp", forth)
    cont = (place >= half).astype(jnp.int32).reshape(1)
    seg_col, seg_row = seg_ids[:, None], seg_ids[None, :]
    mats = over_chips(after(rows, key_far, value_far, *steps_up[3]))

    upstream_far = swap_core(upstream)

    attended = attend(
        cont, after(query_rot, *steps_up[1]), key_rot, value_low, key_far, value_far, seg_col, seg_row
    )
    attn_part = dot(attended, out_mat, NT).astype(BF)
    attn_out, _, _ = line_scatter(shares(attn_part), {1: steps_up[3]})
    after_attn = stream + attn_out
    norm_second = inverse_norm(after_attn)
    hat_two = after_attn * norm_second

    keep = kept_pairs(routes, route_order[0], experts)
    keep_far = swap_core(keep)
    wide_c = jnp.concatenate([upstream, upstream_far], axis=0)
    mlp_own, _ = line_gather(hat_two.astype(BF), gates={2: [keep_far], 3: [wide_c]})
    mlp_far = swap_core(mlp_own)

    def routed(x, kept):
        logits = dot(x, router_mat)[:, :experts]
        grown = jnp.exp(logits - jnp.max(logits, axis=-1, keepdims=True))
        probs = grown / jnp.sum(grown, axis=-1, keepdims=True)
        return probs, lax.dynamic_slice_in_dim(probs * kept, core * local, local, 1)

    def logits_back(s, kept, probs):
        zero = jnp.zeros_like(s)
        pair = kept * jnp.where(core == 0, jnp.concatenate([s, zero], 1), jnp.concatenate([zero, s], 1))
        grad = probs * (pair - jnp.sum(probs * pair, axis=-1, keepdims=True))
        return jnp.pad(grad, ((0, 0), (0, 128 - experts))).astype(BF)

    probs_own, weight_own = routed(mlp_own, keep)
    *held, s_own = hidden(mlp_own, upstream, mats, low_mat, weight_own, 0)
    probs_far, weight_far = routed(mlp_far, keep_far)
    act, dg, du, s_far = hidden(mlp_far, upstream_far, mats, low_mat, weight_far, 1, held)
    gl_own = logits_back(s_own, keep, probs_own)
    gl_far = logits_back(s_far, keep_far, probs_far)

    def both_cores(own, got):
        return [a.astype(F32) + b.astype(F32) for a, b in zip(shares(own), shares(got))]

    def scattered(value):
        return lax.psum_scatter(value, "fsdp", scatter_dimension=0, tiled=True, axis_index_groups=groups)

    dg = lax.dynamic_update_slice(dg, jnp.concatenate([gl_own, gl_far], axis=0), (0, local * span))
    wide_x = jnp.concatenate([mlp_own, mlp_far], axis=0)
    down_term = dot(wide_c, act, TN).astype(BF)
    down_sum = scattered(down_term)

    gl_far = after(gl_far, down_term)
    back_far = mix([(dg, mats, 0, 1), (du, mats, 1, 1), (gl_far, router_mat, 0, 0)], BF, tokens)
    back_got = swap_core(back_far)
    gl_own = after(gl_own, back_far)
    back_own = mix([(dg, mats, 0, 0), (du, mats, 1, 0), (gl_own, router_mat, 0, 0)], BF, tokens)
    grad_scaled, _, back_sends = line_scatter(both_cores(back_own, back_got), {2: [down_sum]})
    gate_term = dot(wide_x, after(dg, back_own, back_got), TN).astype(BF)
    gate_sum = scattered(gate_term)
    up_term = dot(wide_x, after(du, gate_term, *back_sends[2]), TN).astype(BF)
    up_sum = scattered(up_term)
    sums = [gate_sum, up_sum, down_sum]

    grad_after = cotangent.astype(F32) + norm_second * (
        grad_scaled - hat_two * jnp.mean(grad_scaled * hat_two, axis=-1, keepdims=True)
    )
    grad_after_low = after(grad_after.astype(BF), up_term)
    grad_attn, _ = line_gather(grad_after_low)

    act = after(act, back_own, *back_sends[1])
    out_far = mix([(act, low_mat, 0, 1)], BF, tokens)
    out_got = swap_core(out_far)
    out_own = mix([(act, low_mat, 0, 0)], BF, tokens)
    out_low = (out_own.astype(F32) + out_got.astype(F32)).astype(BF)
    out_total = lax.psum_scatter(after(out_low, up_sum, grad_attn), "tp", scatter_dimension=0, tiled=True)
    block_out = after_attn + out_total.astype(F32)

    grad_attended = after(dot(grad_attn, out_mat).astype(BF), out_low)
    dq, dk, dv, dk_far, dv_far = attend_back(
        cont, query_rot, key_rot, value_low, key_far, value_far, grad_attended, seg_col, seg_row
    )
    back_pairs = [(i + half, i) for i in range(half)]
    dk_got, dv_got = lax.ppermute(dk_far, "fsdp", back_pairs), lax.ppermute(dv_far, "fsdp", back_pairs)

    sums = [after(t, dk_far) for t in sums]
    mine = [lax.dynamic_slice_in_dim(t, core * piece, piece, 0) for t in sums]
    theirs = [swap_core(lax.dynamic_slice_in_dim(t, (1 - core) * piece, piece, 0)) for t in sums]
    grad_gate, grad_up, grad_down = moe_unpack(core_arg, mine, theirs, norm_gains, experts, local)
    router_hat = total_tp(sum(t[0][:, local * span : local * span + experts].astype(F32) for t in (mine, theirs)))
    grad_router = router_hat * norm_gains[:, 1:2]
    gain_term = jnp.sum(gate_weight.astype(F32) * grad_gate + up_weight.astype(F32) * grad_up, axis=(0, 2))
    u_query, u_key, dots, gain_parts = turn_back(
        dq, after(dk, sums[1], grad_gate, grad_up, grad_down), dk_got, raw, norms, cos, sin, gains
    )
    dots = total_tp(dots.T).T
    grad_value = (dv + dv_got.astype(F32)).astype(BF)

    def raw_back(u, x, j):
        n = norms[:, j : j + 1]
        return (n * u - x * (n * n * n * dots[:, j : j + 1] / dim)).astype(BF)

    grad_raw = jnp.concatenate(
        [raw_back(u_query, raw[:, :cols], 0), raw_back(u_key, raw[:, cols : 2 * cols], 1), grad_value], axis=1
    )
    normed_part = dot(grad_raw, qkv_mat, NT).astype(BF)
    small = gain_parts.reshape(2, heads, fsdp, narrow).transpose(2, 0, 1, 3).reshape(fsdp, -1)
    small = total_fsdp(small)
    grad_raw_later = after(grad_raw, normed_part)
    qkv_term = dot(normed, grad_raw_later, TN).astype(BF)
    grad_hat, _, last_sends = line_scatter(shares(normed_part), {1: [out_total], 3: [router_hat, gain_term, small]})


    def summed(value):
        return lax.psum_scatter(value, "fsdp", scatter_dimension=0, tiled=True).astype(F32)

    grad_out_proj = summed(dot(grad_attn, after(attended, dk_far), TN).astype(BF)).T
    attn_sum = summed(qkv_term)
    qkv_hat = [attn_sum[:, j * cols : (j + 1) * cols] for j in range(3)]
    qkv_grad = [norm_gains[:, 0:1] * t for t in qkv_hat]
    small = lax.dynamic_index_in_dim(small, place, 0, keepdims=False)
    small = small.reshape(2, heads, narrow)

    attn_dots = sum(jnp.sum(w.astype(F32) * t, axis=1) for w, t in zip((query_weight, key_weight, value_weight), qkv_hat))
    both_dots = total_tp(jnp.stack([attn_dots, gain_term / norm_gains[:, 1]]))
    grad_attn_gain = both_dots[0]
    grad_mlp_gain = both_dots[1] + jnp.sum(router_weight.astype(F32) * router_hat, axis=1)
    grad_hat = after(grad_hat, both_dots, grad_out_proj, *qkv_grad)
    grad_input = grad_after + norm_first * (grad_hat - hat_one * jnp.mean(grad_hat * hat_one, axis=-1, keepdims=True))
    return (
        block_out,
        grad_input,
        qkv_grad[0],
        qkv_grad[1],
        qkv_grad[2],
        grad_out_proj,
        small[0],
        small[1],
        grad_attn_gain,
        grad_mlp_gain,
        grad_router,
        grad_gate,
        grad_up,
        grad_down,
    )


def solution(mesh):
    rows = P(("fsdp", "tp"), None)
    in_specs = (
        rows,
        P("fsdp", "tp"),
        P("fsdp", "tp"),
        P("fsdp", "tp"),
        P("tp", "fsdp"),
        P("tp", "fsdp"),
        P("tp", "fsdp"),
        P("fsdp"),
        P("fsdp"),
        P("fsdp", None),
        P(None, "fsdp", "tp"),
        P(None, "fsdp", "tp"),
        P(None, "tp", "fsdp"),
        P("fsdp", None),
        P("fsdp", None),
        P("fsdp"),
        rows,
    )
    out_specs = (
        rows,
        rows,
        P("fsdp", "tp"),
        P("fsdp", "tp"),
        P("fsdp", "tp"),
        P("tp", "fsdp"),
        P("tp", "fsdp"),
        P("tp", "fsdp"),
        P("fsdp"),
        P("fsdp"),
        P("fsdp", None),
        P(None, "fsdp", "tp"),
        P(None, "fsdp", "tp"),
        P(None, "tp", "fsdp"),
    )
    return jax.shard_map(on_device, mesh=mesh, in_specs=in_specs, out_specs=out_specs, check_vma=False)
```
